32 devices in a mesh: gx: 8 (over y, x, core), gy: 4 (over z).
Axes of the slice: x: 2, y: 2, z: 4, core: 2. Of those that a mesh axis runs over, the one named last changes fastest.
Arguments:
- density: bfloat16 [2048, 128, 128], P(('gx', 'gy')), may hold values from -0.00390625 to 0.00390625
- dest: int32 [2048, 2], P(('gx', 'gy')), may hold values from 0 to 31, all different within a row; in each aligned block of 64 rows (0 to 63, 64 to 127, ...) at most 8 rows name the same one
- code: int32 [2048, 2], P(('gx', 'gy')), may hold values from 0 to 143
- basis: bfloat16 [65536, 1536], P(('gx', 'gy')), may hold values from -6 to 6
- descriptors: float32 [10, 65536], P(None, ('gx', 'gy')), may hold values from -6 to 6
- weights: float32 [65536], P(('gx', 'gy')), may hold values from 0.0055242717 to 0.198873782
- w_in: float32 [11, 128], replicated, may hold values from -1.75 to 1.75
- w_hid1: float32 [128, 128], replicated, may hold values from -0.5 to 0.5
- w_hid2: float32 [128, 128], replicated, may hold values from -0.5 to 0.5
- w_out: float32 [128], replicated, may hold values from -0.5 to 0.5
Outputs:
- fock: float32 [2048, 128, 128], P(('gx', 'gy'))
- energy: float32 [], replicated
The draws below stay inside these ranges and needn't reach their ends.
Inputs may be any that keep to these rules, and one draw needn't show every extreme that they name: `dest`: the two copies of a pair block go to different domains; among the pair blocks of one device at most 8 copies go to one domain.
All inputs are finite; a program needn't handle non-finite values.
Results may differ from the reference program's by a relative error of at most 0.0044.
Values may be sent and summed in bfloat16 or wider, within the bound.
No kernel may reach another device: no remote copies, remote signals or barrier semaphores. Data moves between devices by JAX's collectives and lax.ppermute only.
A program may use at most 128 MiB of HBM per device.

```python
import math
import jax
import jax.numpy as jnp
import numpy as np
from jax import lax

NBF = 128
FIN = 11
HID = 128
TOP = 2
LBLK = 12
PTS_DEV = 2048
PAIR_DEV = 64
FDESC = 10
NDOM = 32
NPAIR = 2048
NPTS = 65536
CAP = 8


def draw_weights(key, part):
    domain_ids = (jnp.arange(NPTS) // PTS_DEV).astype(jnp.float32)
    domain_count = NPTS // PTS_DEV
    rising = 1.0 + 2.0 * domain_ids / max(domain_count - 1, 1)
    base = jnp.exp(jax.random.uniform(key, (NPTS,), jnp.float32, math.log(0.5), math.log(2.0)))
    return (base * rising / math.sqrt(PTS_DEV)).astype(jnp.float32)


def set_ends(result, key, least, top_value):
    extent = result.shape
    index_at = [jax.random.randint(jax.random.fold_in(key, axis), (), 0, extent[axis]) for axis in range(len(extent))]
    result = result.at[tuple(index_at)].set(least)
    longest = extent.index(max(extent))
    index_at[longest] = (index_at[longest] + 1) % extent[longest]
    return result.at[tuple(index_at)].set(top_value)


def steps_of(stream_key, dims, shards, smallest, largest):
    gain, own = 1.0, jax.random.fold_in(stream_key, 6)
    for position, shards_of in shards:
        heights = jnp.exp(jax.random.uniform(jax.random.fold_in(own, position), (shards_of,), jnp.float32, smallest / len(shards), largest / len(shards)))
        gain = gain * jnp.repeat(heights, dims[position] // shards_of).reshape([-1 if axis == position else 1 for axis in range(len(dims))])
    return gain


def deal_out(rng, own, number, rows, count, top, most, slope):
    order = jax.random.permutation(rng, count)
    heavy_load, usual = portions_of(count, rows * top, most, slope, True), portions_of(count, rows * top, most, slope, False)
    places = jnp.arange(count)

    def named(tallies, turn):
        used = int((tallies > 0).sum())
        fixed = max(1, used // 4)
        passed = fixed + (places - fixed + turn * (used - fixed)) % max(1, count - fixed)
        return jnp.zeros((count,), jnp.int32).at[order[jnp.where(places < fixed, places, passed)]].set(jnp.asarray(tallies, jnp.int32))

    tallies = jnp.where(number % 4 == 0, named(heavy_load, number // 4), named(usual, number - number // 4 - 1))
    mixed = jax.random.permutation(jax.random.fold_in(own, 3), count)
    donor, sink = mixed[0:count // 2 * 2:2], mixed[1:count // 2 * 2:2]
    room = jnp.minimum(tallies[donor] - 1, most - tallies[sink]) // 2
    room = jnp.where((donor == order[0]) | (sink == order[0]) | (tallies[sink] == 0), 0, jnp.maximum(room, 0))
    passed = jax.random.randint(jax.random.fold_in(own, 4), (count // 2,), 0, 1 << 20) % (room + 1)
    tallies = tallies.at[donor].add(-passed).at[sink].add(passed)
    labels = jnp.searchsorted(jnp.cumsum(tallies), jnp.arange(rows * top), side="right").astype(jnp.int32)
    table = labels.reshape(top, rows).T
    table = table[jax.random.permutation(jax.random.fold_in(own, 1), rows)]
    turn = jax.random.randint(jax.random.fold_in(own, 2), (rows, 1), 0, top)
    return jnp.take_along_axis(table, (jnp.arange(top)[None, :] + turn) % top, axis=1)


def portions_of(count, total, limit, lean, full):
    portions = [(1 << 20) // math.isqrt(grade ** lean) + 1 for grade in range(1, count + 1)]
    largest = limit if full else min(limit, max(-(-total // count), total * portions[0] // sum(portions)))
    least = 1 if total - largest >= count - 1 else 0
    holding, surplus = [largest] + [least] * (count - 1), total - largest - least * (count - 1)
    while surplus > 0:
        candidates = [i for i in range(1, count) if holding[i] < largest] or [i for i in range(1, count) if holding[i] < limit]
        whole, budget = sum([portions[i] for i in candidates]), surplus
        for i in candidates:
            extra = min(limit - holding[i], max(1, budget * portions[i] // whole), surplus)
            holding[i] = holding[i] + extra
            surplus = surplus - extra
    return np.array(holding)


def gaussian(rng, extent, spread, most, cuts=(), dtype=jnp.bfloat16):
    entries = jax.random.normal(rng, extent, jnp.float32) * spread
    if len(cuts) > 0:
        entries = steps_of(rng, extent, cuts, -0.22, 0.18) * entries
    return jnp.clip(entries, min=-most, max=most).astype(dtype)


def setup_inputs(seed: int = 0) -> dict:
    key_list = jax.random.split(jax.random.key(seed), 11)
    density = gaussian(key_list[0], (NPAIR, NBF, NBF), (1.0 / (NBF * LBLK)), 0.00390625, ((0, 32),))
    dest_keys = jax.random.split(jax.random.fold_in(key_list[1], 1), NPAIR // PAIR_DEV)
    dest_turns = jax.random.permutation(jax.random.fold_in(key_list[1], 3), NPAIR // PAIR_DEV)
    dest = jax.vmap(lambda own, number: deal_out(jax.random.fold_in(key_list[1], 2), own, number, PAIR_DEV, NDOM, TOP, CAP, 1))(dest_keys, dest_turns).reshape((NPAIR, TOP))
    code = set_ends(jax.random.randint(key_list[2], (NPAIR, TOP), 0, LBLK * LBLK), jax.random.fold_in(key_list[2], 1), 0, (LBLK * LBLK) - 1).astype(jnp.int32)
    basis = gaussian(key_list[3], (NPTS, LBLK * NBF), 1.0, 6.0, ((0, 32),))
    descriptors = gaussian(key_list[4], (FDESC, NPTS), 1.0, 6.0, ((1, 32),), jnp.float32)
    weights = draw_weights(jax.random.fold_in(key_list[10], 71), 0)
    w_in = gaussian(key_list[6], (FIN, HID), FIN ** -0.5, 1.75, (), jnp.float32)
    w_hid1 = gaussian(key_list[7], (HID, HID), HID ** -0.5, 0.5, (), jnp.float32)
    w_hid2 = gaussian(key_list[8], (HID, HID), HID ** -0.5, 0.5, (), jnp.float32)
    w_out = gaussian(key_list[9], (HID,), HID ** -0.5, 0.5, (), jnp.float32)
    return {"density": density, "dest": dest, "code": code, "basis": basis, "descriptors": descriptors, "weights": weights, "w_in": w_in, "w_hid1": w_hid1, "w_hid2": w_hid2, "w_out": w_out}


def network(density_at, descriptors, w_in, w_hid1, w_hid2, w_out):
    features = jnp.concatenate([density_at[None, :], descriptors], axis=0)
    hidden = jnp.tanh(jnp.dot(w_in.T, features, precision=lax.Precision.HIGHEST))
    hidden = jnp.tanh(jnp.dot(w_hid1.T, hidden, precision=lax.Precision.HIGHEST))
    hidden = jnp.tanh(jnp.dot(w_hid2.T, hidden, precision=lax.Precision.HIGHEST))
    logits = jnp.dot(w_out, hidden, precision=lax.Precision.HIGHEST)
    return -jax.nn.softplus(logits)

def local_build(summed, basis, descriptors, weights, w_in, w_hid1, w_hid2, w_out):
    order_size = LBLK * NBF
    dense = summed.reshape(LBLK, LBLK, NBF, NBF).transpose(0, 2, 1, 3).reshape(order_size, order_size)
    projected = jnp.dot(basis, dense, preferred_element_type=jnp.float32)
    density_at = lax.optimization_barrier(jnp.sum(projected * basis.astype(jnp.float32), axis=1))

    def energy_fn(values):
        return network(values, descriptors, w_in, w_hid1, w_hid2, w_out)
    energy_at, pullback = jax.vjp(energy_fn, density_at)
    deriv = pullback(jnp.ones_like(energy_at))[0]
    potential = weights * deriv
    scaled = (potential[:, None] * basis.astype(jnp.float32)).astype(jnp.bfloat16)
    fock_mat = lax.dot_general(basis, scaled, (((0,), (0,)), ((), ())), preferred_element_type=jnp.float32).astype(jnp.bfloat16)
    blocks = fock_mat.reshape(LBLK, NBF, LBLK, NBF).transpose(0, 2, 1, 3).reshape(LBLK * LBLK, NBF * NBF)
    return (blocks, jnp.sum(weights * energy_at))

def reference(density, dest, code, basis, descriptors, weights, w_in, w_hid1, w_hid2, w_out):
    local_pairs = LBLK * LBLK
    block_width = NBF * NBF
    rows = density.reshape(NPAIR, block_width).astype(jnp.float32)
    sums = jnp.zeros((NDOM * local_pairs, block_width), jnp.float32)
    for copy_index in range(TOP):
        target = (dest[:, copy_index] * local_pairs + code[:, copy_index]).astype(jnp.int32)
        sums = sums.at[target].add(rows)
    sums = sums.astype(jnp.bfloat16).reshape(NDOM, local_pairs, block_width)
    basis_dom = basis.reshape(NDOM, PTS_DEV, LBLK * NBF)
    desc_dom = descriptors.reshape(FDESC, NDOM, PTS_DEV).transpose(1, 0, 2)
    weights_dom = weights.reshape(NDOM, PTS_DEV)

    def one_domain(items):
        return local_build(items[0], items[1], items[2], items[3], w_in, w_hid1, w_hid2, w_out)
    blocks, partial_sums = lax.map(one_domain, (sums, basis_dom, desc_dom, weights_dom))
    flat_blocks = blocks.reshape(NDOM * local_pairs, block_width)
    fock = jnp.zeros((NPAIR, block_width), jnp.float32)
    for copy_index in range(TOP):
        target = (dest[:, copy_index] * local_pairs + code[:, copy_index]).astype(jnp.int32)
        fock = fock + flat_blocks[target].astype(jnp.float32)
    factor = 1.0 / (math.sqrt(PTS_DEV) * NDOM)
    energy = jnp.sum(partial_sums) * jnp.float32(factor)
    return (fock.reshape(NPAIR, NBF, NBF), energy)
```

```python
import functools
import math

import jax
import jax.numpy as jnp
from jax import lax
from jax.experimental import pallas as pl
from jax.experimental.pallas import tpu as pltpu
from jax.sharding import PartitionSpec as P

NBF = 128
META = 8
AXES = ("gx", "gy")
HI = lax.Precision.HIGHEST


def any_spec():
    return pl.BlockSpec(memory_space=pl.ANY)


def smem_spec():
    return pl.BlockSpec(memory_space=pltpu.SMEM)


def vmem_spec():
    return pl.BlockSpec(memory_space=pltpu.VMEM)


def block_rows(rank):
    return pl.ds(pl.multiple_of(rank * NBF, NBF), NBF)


def send_kernel(domains, capacity, dest, code, density, out, slots, count, blocks, codes, codes16, load_sem, out_sem, meta_sem):
    copies, owned = dest.shape
    load = pltpu.make_async_copy(density, blocks, load_sem)
    load.start()

    @pl.loop(0, domains)
    def _(d):
        count[d] = 0

    codes[...] = jnp.full(codes.shape, -1.0, jnp.float32)
    lane = lax.broadcasted_iota(jnp.int32, (META, NBF), 1)

    @pl.loop(0, owned)
    def _(p):
        for t in range(copies):
            d = dest[t, p]
            rank = count[d]
            count[d] = rank + 1
            slots[t, p] = d * capacity + rank
            value = code[t, p].astype(jnp.float32)
            codes[d] = jnp.where(lane == rank, value, codes[d])

    codes16[...] = codes[...].astype(jnp.bfloat16)
    meta = pltpu.make_async_copy(codes16, out.at[:, pl.ds(capacity * NBF, META), :], meta_sem)
    meta.start()
    load.wait()

    @pl.loop(0, owned)
    def _(p):
        for t in range(copies):
            slot = slots[t, p]
            d = slot // capacity
            rank = slot - d * capacity
            pltpu.make_async_copy(blocks.at[p], out.at[d, block_rows(rank)], out_sem).start()

    meta.wait()
    part = out.at[pl.ds(0, copies * owned // capacity), pl.ds(0, capacity * NBF), :]
    pltpu.make_async_copy(part, part, out_sem).wait()


def send_blocks(density, dest, code, domains, capacity):
    owned = density.shape[0]
    copies = dest.shape[1]
    return pl.pallas_call(
        functools.partial(send_kernel, domains, capacity),
        out_shape=(
            jax.ShapeDtypeStruct((domains, capacity * NBF + META, NBF), jnp.bfloat16),
            jax.ShapeDtypeStruct((copies, owned), jnp.int32),
        ),
        in_specs=[smem_spec(), smem_spec(), any_spec()],
        out_specs=(any_spec(), smem_spec()),
        scratch_shapes=[
            pltpu.SMEM((domains,), jnp.int32),
            pltpu.VMEM((owned, NBF, NBF), jnp.bfloat16),
            pltpu.VMEM((domains, META, NBF), jnp.float32),
            pltpu.VMEM((domains, META, NBF), jnp.bfloat16),
            pltpu.SemaphoreType.DMA,
            pltpu.SemaphoreType.DMA,
            pltpu.SemaphoreType.DMA,
        ],
        name="send_blocks",
    )(dest.T, code.T, density)


def domain_kernel(
    capacity,
    codes,
    inbound,
    basis,
    basis_t,
    base_in,
    w_row,
    w_hid1,
    w_hid1_t,
    w_hid2,
    w_hid2_t,
    w_out,
    weights,
    reply,
    seen,
    stage,
    acc,
    dense,
    basis_v,
    basis_tv,
    rho,
    hid1,
    hid2,
    blocks,
    meta,
    in_sem,
    basis_sem,
    out_sem,
    meta_sem,
):
    sources = inbound.shape[0]
    slots = sources * capacity
    points, order = basis.shape
    width = order // NBF
    pairs = width * width
    load_t = pltpu.make_async_copy(basis_t, basis_tv, basis_sem.at[0])
    load_n = pltpu.make_async_copy(basis, basis_v, basis_sem.at[1])

    def fetch(source, rank, slot):
        return pltpu.make_async_copy(inbound.at[source, block_rows(rank)], stage.at[slot], in_sem.at[slot])

    @pl.loop(0, sources)
    def _(source):
        for rank in range(capacity):
            slot = source * capacity + rank

            @pl.when(codes[slot] >= 0)
            def _():
                fetch(source, rank, slot).start()

    load_t.start()
    load_n.start()

    @pl.loop(0, pairs)
    def _(c):
        seen[c] = 0

    @pl.loop(0, slots)
    def _(slot):
        c = codes[slot]

        @pl.when(c >= 0)
        def _():
            fetch(0, 0, slot).wait()
            value = stage[slot].astype(jnp.float32)
            before = seen[c]
            seen[c] = 1

            @pl.when(before == 0)
            def _():
                acc[c] = value

            @pl.when(before != 0)
            def _():
                acc[c] = acc[c] + value

    @pl.loop(0, width)
    def _(a):
        rows = block_rows(a)
        for b in range(width):
            there = seen[a * width + b] != 0
            value = jnp.where(there, acc[a * width + b], 0.0)
            dense[rows, b * NBF : (b + 1) * NBF] = value.astype(jnp.bfloat16)

    load_t.wait()
    tile = 256

    @pl.loop(0, points // tile)
    def _(n):
        cols = pl.ds(pl.multiple_of(n * tile, tile), tile)
        part = basis_tv[:, cols]
        projected = jnp.dot(dense[...], part, preferred_element_type=jnp.float32)
        rho[:, cols] = jnp.sum(projected * part.astype(jnp.float32), axis=0, keepdims=True)

    h1 = jnp.tanh(base_in[...] + w_row[...] * rho[...])
    hid1[...] = h1
    h2 = jnp.tanh(jnp.dot(w_hid1_t[...], h1, precision=HI, preferred_element_type=jnp.float32))
    hid2[...] = h2
    h3 = jnp.tanh(jnp.dot(w_hid2_t[...], h2, precision=HI, preferred_element_type=jnp.float32))
    logits = jnp.sum(w_out[...] * h3, axis=0, keepdims=True)
    decay = jnp.exp(-jnp.abs(logits))
    energy_at = -(jnp.maximum(logits, 0.0) + jnp.log1p(decay))
    slope = -jnp.where(logits >= 0, 1.0, decay) / (1.0 + decay)
    g3 = (w_out[...] * slope) * (1.0 - h3 * h3)
    h2 = hid2[...]
    g2 = jnp.dot(w_hid2[...], g3, precision=HI, preferred_element_type=jnp.float32) * (1.0 - h2 * h2)
    h1 = hid1[...]
    g1 = jnp.dot(w_hid1[...], g2, precision=HI, preferred_element_type=jnp.float32) * (1.0 - h1 * h1)
    deriv = jnp.sum(w_row[...] * g1, axis=0, keepdims=True)
    rho[...] = weights[...] * deriv
    total = jnp.sum(weights[...] * energy_at, axis=1, keepdims=True)
    top = total.astype(jnp.bfloat16).astype(jnp.float32)
    rest = total - top
    middle = rest.astype(jnp.bfloat16).astype(jnp.float32)
    low = rest - middle
    lane = lax.broadcasted_iota(jnp.int32, (META, NBF), 1)
    line = jnp.where(lane == 0, top, jnp.where(lane == 1, middle, jnp.where(lane == 2, low, 0.0)))
    meta[...] = line.astype(jnp.bfloat16)

    @pl.loop(0, sources)
    def _(source):
        pltpu.make_async_copy(meta, reply.at[source, pl.ds(capacity * NBF, META)], meta_sem).start()

    load_n.wait()

    @pl.loop(0, points // NBF)
    def _(n):
        rows = block_rows(n)
        line = jnp.broadcast_to(rho[:, rows], (NBF, NBF))
        column = line.T
        for b in range(width):
            cols = slice(b * NBF, (b + 1) * NBF)
            basis_v[rows, cols] = (column * basis_v[rows, cols].astype(jnp.float32)).astype(jnp.bfloat16)

    @pl.loop(0, width // 2)
    def _(n):
        cols = pl.ds(pl.multiple_of(n * 2 * NBF, 2 * NBF), 2 * NBF)
        result = jnp.dot(basis_tv[...], basis_v[:, cols], preferred_element_type=jnp.float32).astype(jnp.bfloat16)
        for a in range(width):
            for half in range(2):
                blocks[a * width + 2 * n + half] = result[a * NBF : (a + 1) * NBF, half * NBF : (half + 1) * NBF]

    def give(source, rank, c):
        return pltpu.make_async_copy(blocks.at[c], reply.at[source, block_rows(rank)], out_sem)

    @pl.loop(0, sources)
    def _(source):
        for rank in range(capacity):
            c = codes[source * capacity + rank]

            @pl.when(c >= 0)
            def _():
                give(source, rank, c).start()

    @pl.loop(0, slots)
    def _(slot):
        @pl.when(codes[slot] >= 0)
        def _():
            give(0, 0, 0).wait()

    whole = reply.at[:, pl.ds(capacity * NBF, META), :]
    pltpu.make_async_copy(whole, whole, meta_sem).wait()


def domain_build(codes, inbound, basis, basis_t, base_in, w_row, w_hid1, w_hid2, w_out, weights, capacity):
    sources = inbound.shape[0]
    points, order = basis.shape
    hid = w_hid1.shape[0]
    pairs = (order // NBF) ** 2
    return pl.pallas_call(
        functools.partial(domain_kernel, capacity),
        out_shape=jax.ShapeDtypeStruct(inbound.shape, jnp.bfloat16),
        in_specs=[smem_spec(), any_spec(), any_spec(), any_spec()] + [vmem_spec()] * 8,
        out_specs=any_spec(),
        scratch_shapes=[
            pltpu.SMEM((pairs,), jnp.int32),
            pltpu.VMEM((sources * capacity, NBF, NBF), jnp.bfloat16),
            pltpu.VMEM((pairs, NBF, NBF), jnp.float32),
            pltpu.VMEM((order, order), jnp.bfloat16),
            pltpu.VMEM((points, order), jnp.bfloat16),
            pltpu.VMEM((order, points), jnp.bfloat16),
            pltpu.VMEM((1, points), jnp.float32),
            pltpu.VMEM((hid, points), jnp.float32),
            pltpu.VMEM((hid, points), jnp.float32),
            pltpu.VMEM((pairs, NBF, NBF), jnp.bfloat16),
            pltpu.VMEM((META, NBF), jnp.bfloat16),
            pltpu.SemaphoreType.DMA((sources * capacity,)),
            pltpu.SemaphoreType.DMA((2,)),
            pltpu.SemaphoreType.DMA,
            pltpu.SemaphoreType.DMA,
        ],
        compiler_params=pltpu.CompilerParams(vmem_limit_bytes=60 << 20),
        name="domain_build",
    )(
        codes, inbound, basis, basis_t, base_in, w_row[:, None], w_hid1, w_hid1.T, w_hid2, w_hid2.T,
        w_out[:, None], weights[None, :],
    )


def collect_kernel(capacity, scale, slots, returned, fock, energy, parts, result, meta, in_sem, out_sem, meta_sem):
    copies, owned = slots.shape
    meta_in = pltpu.make_async_copy(returned.at[:, pl.ds(capacity * NBF, META), :], meta, meta_sem)
    meta_in.start()

    def fetch(source, rank, p, t):
        return pltpu.make_async_copy(returned.at[source, block_rows(rank)], parts.at[p, t], in_sem.at[p])

    @pl.loop(0, owned)
    def _(p):
        for t in range(copies):
            slot = slots[t, p]
            source = slot // capacity
            fetch(source, slot - source * capacity, p, t).start()

    meta_in.wait()
    lane = lax.broadcasted_iota(jnp.int32, meta.shape, 2)
    row = lax.broadcasted_iota(jnp.int32, meta.shape, 1)
    sent = jnp.where((lane < 3) & (row == 0), meta[...].astype(jnp.float32), 0.0)
    per_source = jnp.sum(jnp.sum(sent, axis=0), axis=0, keepdims=True)
    energy[...] = jnp.sum(per_source, axis=1, keepdims=True) * scale

    def give(p):
        return pltpu.make_async_copy(result.at[p], fock.at[p], out_sem)

    @pl.loop(0, owned)
    def _(p):
        pltpu.make_async_copy(parts.at[p], parts.at[p], in_sem.at[p]).wait()
        total = parts[p, 0].astype(jnp.float32)
        for t in range(1, copies):
            total = total + parts[p, t].astype(jnp.float32)
        result[p] = total
        give(p).start()

    pltpu.make_async_copy(result, fock, out_sem).wait()


def collect_blocks(slots, returned, capacity, scale):
    copies, owned = slots.shape
    sources = returned.shape[0]
    return pl.pallas_call(
        functools.partial(collect_kernel, capacity, scale),
        out_shape=(
            jax.ShapeDtypeStruct((owned, NBF, NBF), jnp.float32),
            jax.ShapeDtypeStruct((1, 1), jnp.float32),
        ),
        in_specs=[smem_spec(), any_spec()],
        out_specs=(any_spec(), vmem_spec()),
        scratch_shapes=[
            pltpu.VMEM((owned, copies, NBF, NBF), jnp.bfloat16),
            pltpu.VMEM((owned, NBF, NBF), jnp.float32),
            pltpu.VMEM((sources, META, NBF), jnp.bfloat16),
            pltpu.SemaphoreType.DMA((owned,)),
            pltpu.SemaphoreType.DMA,
            pltpu.SemaphoreType.DMA,
        ],
        name="collect_blocks",
    )(slots, returned)


def body(density, dest, code, basis, descriptors, weights, w_in, w_hid1, w_hid2, w_out):
    domains = lax.axis_size(AXES)
    owned = density.shape[0]
    copies = dest.shape[1]
    capacity = max(2, 2 * copies * owned // domains)
    points = basis.shape[0]
    outgoing, slots = send_blocks(density, dest, code, domains, capacity)
    inbound = lax.all_to_all(outgoing, AXES, split_axis=0, concat_axis=0, tiled=True)
    basis_t = basis.T
    base_in = jnp.dot(w_in[1:].T, descriptors, precision=HI)
    codes = inbound[:, capacity * NBF, :capacity].astype(jnp.int32).reshape(-1)
    replies = domain_build(
        codes, inbound, basis, basis_t, base_in, w_in[0], w_hid1, w_hid2, w_out, weights, capacity
    )
    returned = lax.all_to_all(replies, AXES, split_axis=0, concat_axis=0, tiled=True)
    scale = 1.0 / (math.sqrt(points) * domains)
    fock, energy = collect_blocks(slots, returned, capacity, scale)
    return (fock, energy[0, 0])


def solution(mesh):
    placed = (
        P(AXES, None, None),
        P(AXES, None),
        P(AXES, None),
        P(AXES, None),
        P(None, AXES),
        P(AXES),
        P(),
        P(),
        P(),
        P(),
    )
    return jax.shard_map(
        body,
        mesh=mesh,
        in_specs=placed,
        out_specs=(P(AXES, None, None), P()),
        check_vma=False,
    )
```

```python
import functools
import math

import jax
import jax.numpy as jnp
from jax import lax
from jax.experimental import pallas as pl
from jax.experimental.pallas import tpu as pltpu
from jax.sharding import PartitionSpec as P

NBF = 128
META = 8
LINE = 32
FLAG = 64
POOL = 16
AXES = ("gx", "gy")
HI = lax.Precision.HIGHEST


def any_spec():
    return pl.BlockSpec(memory_space=pl.ANY)


def smem_spec():
    return pl.BlockSpec(memory_space=pltpu.SMEM)


def vmem_spec():
    return pl.BlockSpec(memory_space=pltpu.VMEM)


def block_rows(rank):
    return pl.ds(pl.multiple_of(rank * NBF, NBF), NBF)


def panel(ranks):
    return jax.ShapeDtypeStruct((ranks * NBF + META, NBF), jnp.bfloat16)


def ranks_of(array):
    return array.shape[-2] // NBF


def meta_rows(array):
    return pl.ds(ranks_of(array) * NBF, META)


def lane_row(shape):
    lane = lax.broadcasted_iota(jnp.int32, shape, len(shape) - 1)
    row = lax.broadcasted_iota(jnp.int32, shape, len(shape) - 2)
    return lane, row


def send_kernel(groups, dest, code, density, *refs):
    copies, owned = dest.shape
    out, *extras, places = refs[:-7]
    count, pool, flag, blocks, codes, codes16, sems = refs[-7:]
    domains = out.shape[0]
    direct = ranks_of(out)
    load = pltpu.make_async_copy(density, blocks, sems.at[0])
    load.start()

    @pl.loop(0, domains)
    def _(d):
        count[d] = 0

    codes[...] = jnp.full(codes.shape, -1.0, jnp.float32)
    lane, row = lane_row((META, NBF))
    flag[0] = 0
    if groups is not None:
        rows_x, rows_z = groups
        me_x, me_z = lax.axis_index("gx"), lax.axis_index("gy")
        for k in range(rows_z):
            pool[k] = 0

    @pl.loop(0, owned)
    def _(p):
        for t in range(copies):
            d = dest[t, p]
            rank = count[d]
            count[d] = rank + 1
            value = code[t, p].astype(jnp.float32)
            if groups is None:
                entry, place = d, rank
                codes[entry] = jnp.where((lane == place) & (row == 0), value, codes[entry])
            else:
                target = d // rows_z
                near = target ^ me_x
                far = (d - target * rows_z) ^ me_z
                slot = pool[far]
                spill = (rank >= direct) & (far != 0)
                pool[far] = slot + spill.astype(jnp.int32)
                flag[0] = flag[0] | (spill & (slot >= POOL)).astype(jnp.int32)
                other = jnp.where(far == 0, domains + near, domains + rows_x + far - 1)
                entry = jnp.where(rank < direct, d, other)
                other = jnp.where(far == 0, rank - direct, jnp.minimum(slot, POOL - 1))
                place = jnp.where(rank < direct, rank, other)
                side = jnp.where(row == 0, value, target.astype(jnp.float32))
                codes[entry] = jnp.where((lane == place) & (row < 2), side, codes[entry])
            places[t, p] = entry * LINE + place

    if groups is not None:
        raised = flag[0].astype(jnp.float32)
        mark = (lane == FLAG) & (row == 0)
        codes[0:domains] = jnp.where(mark, raised, codes[0:domains])
    codes16[...] = codes[...].astype(jnp.bfloat16)
    metas = [pltpu.make_async_copy(codes16.at[pl.ds(0, domains)], out.at[:, meta_rows(out), :], sems.at[1])]
    for k, ref in enumerate(extras):
        metas.append(pltpu.make_async_copy(codes16.at[domains + k], ref.at[meta_rows(ref), :], sems.at[3 + k]))
    for copy in metas:
        copy.start()
    load.wait()

    @pl.loop(0, owned)
    def _(p):
        for t in range(copies):
            entry = places[t, p] // LINE
            rows = block_rows(places[t, p] - entry * LINE)

            @pl.when(entry < domains)
            def _():
                pltpu.make_async_copy(blocks.at[p], out.at[entry, rows], sems.at[2]).start()

            if extras:

                @pl.when(entry >= domains)
                def _():
                    for k, ref in enumerate(extras):

                        @pl.when(entry == domains + k)
                        def _():
                            pltpu.make_async_copy(blocks.at[p], ref.at[rows], sems.at[2]).start()

    for copy in metas:
        copy.wait()
    part = out.at[pl.ds(0, copies * owned // direct), pl.ds(0, direct * NBF), :]
    pltpu.make_async_copy(part, part, sems.at[2]).wait()


def send_blocks(density, dest, code, domains, direct, groups):
    owned = density.shape[0]
    copies = dest.shape[1]
    extras = []
    if groups is not None:
        extras = [panel(direct)] * groups[0] + [panel(POOL)] * (groups[1] - 1)
    entries = domains + len(extras)
    return pl.pallas_call(
        functools.partial(send_kernel, groups),
        out_shape=(
            jax.ShapeDtypeStruct((domains, direct * NBF + META, NBF), jnp.bfloat16),
            *extras,
            jax.ShapeDtypeStruct((copies, owned), jnp.int32),
        ),
        in_specs=[smem_spec(), smem_spec(), any_spec()],
        out_specs=(any_spec(),) * (1 + len(extras)) + (smem_spec(),),
        scratch_shapes=[
            pltpu.SMEM((domains,), jnp.int32),
            pltpu.SMEM((LINE,), jnp.int32),
            pltpu.SMEM((1,), jnp.int32),
            pltpu.VMEM((owned, NBF, NBF), jnp.bfloat16),
            pltpu.VMEM((entries, META, NBF), jnp.float32),
            pltpu.VMEM((entries, META, NBF), jnp.bfloat16),
            pltpu.SemaphoreType.DMA((3 + len(extras),)),
        ],
        name="send_blocks",
    )(dest.T, code.T, density)


def relay_kernel(*refs):
    info, count, stage, lines, ints, codes, codes16, in_sem, sems = refs[-9:]
    hops = lines.shape[0]
    arrived = refs[:hops]
    outs = refs[hops : -10]
    places = refs[-10]
    ranks = ranks_of(outs[0])
    me = lax.axis_index("gx")
    loads = [
        pltpu.make_async_copy(ref.at[meta_rows(ref), :], lines.at[h], sems.at[h]) for h, ref in enumerate(arrived)
    ]
    for load in loads:
        load.start()
    codes[...] = jnp.full(codes.shape, -1.0, jnp.float32)
    lane, row = lane_row((META, NBF))
    for k in range(len(outs)):
        count[k] = 0
    for load in loads:
        load.wait()
    ints[...] = lines[...].astype(jnp.float32).astype(jnp.int32)
    load = pltpu.make_async_copy(ints, info, sems.at[0])
    load.start()
    load.wait()

    def fetch(h, q):
        return pltpu.make_async_copy(arrived[h].at[block_rows(q)], stage.at[h * POOL + q], in_sem.at[h * POOL + q])

    for h in range(hops):

        @pl.loop(0, POOL)
        def _(q):
            places[h, q] = -1
            c = info[h, 0, q]

            @pl.when(c >= 0)
            def _():
                fetch(h, q).start()
                near = info[h, 1, q] ^ me
                slot = jnp.minimum(count[near], ranks - 1)
                count[near] = slot + 1
                places[h, q] = near * LINE + slot
                hit = (lane == slot) & (row == 0)
                codes[near] = jnp.where(hit, c.astype(jnp.float32), codes[near])

    codes16[...] = codes[...].astype(jnp.bfloat16)
    metas = [
        pltpu.make_async_copy(codes16.at[k], ref.at[meta_rows(ref), :], sems.at[hops + k])
        for k, ref in enumerate(outs)
    ]
    for copy in metas:
        copy.start()
    last = sems.at[hops + len(outs)]
    for h in range(hops):

        @pl.loop(0, POOL)
        def _(q):
            place = places[h, q]

            @pl.when(place >= 0)
            def _():
                fetch(h, q).wait()
                near = place // LINE
                rows = block_rows(place - near * LINE)
                for k, ref in enumerate(outs):

                    @pl.when(near == k)
                    def _():
                        pltpu.make_async_copy(stage.at[h * POOL + q], ref.at[rows], last).start()

    for copy in metas:
        copy.wait()
    for h in range(hops):

        @pl.loop(0, POOL)
        def _(q):
            @pl.when(places[h, q] >= 0)
            def _():
                pltpu.make_async_copy(stage.at[0], outs[0].at[block_rows(0)], last).wait()


def relay(arrived, near_count, ranks):
    hops = len(arrived)
    return pl.pallas_call(
        relay_kernel,
        out_shape=tuple([panel(ranks)] * near_count + [jax.ShapeDtypeStruct((hops, POOL), jnp.int32)]),
        in_specs=[any_spec()] * hops,
        out_specs=tuple([any_spec()] * near_count + [smem_spec()]),
        scratch_shapes=[
            pltpu.SMEM((hops, META, NBF), jnp.int32),
            pltpu.SMEM((near_count,), jnp.int32),
            pltpu.VMEM((hops * POOL, NBF, NBF), jnp.bfloat16),
            pltpu.VMEM((hops, META, NBF), jnp.bfloat16),
            pltpu.VMEM((hops, META, NBF), jnp.int32),
            pltpu.VMEM((near_count, META, NBF), jnp.float32),
            pltpu.VMEM((near_count, META, NBF), jnp.bfloat16),
            pltpu.SemaphoreType.DMA((hops * POOL,)),
            pltpu.SemaphoreType.DMA((hops + near_count + 1,)),
        ],
        cost_estimate=pl.CostEstimate(flops=1000, bytes_accessed=4 << 20, transcendentals=0),
        name="relay",
    )(*arrived)


def relay_back_kernel(places, *refs):
    stage, in_sem, out_sem = refs[-3:]
    hops = places.shape[0]
    arrived, outs = refs[: -3 - hops], refs[-3 - hops : -3]

    def fetch(ref, rows, h, q):
        return pltpu.make_async_copy(ref.at[rows], stage.at[h * POOL + q], in_sem.at[h * POOL + q])

    def give(h, q):
        return pltpu.make_async_copy(stage.at[h * POOL + q], outs[h].at[block_rows(q)], out_sem)

    for h in range(hops):

        @pl.loop(0, POOL)
        def _(q):
            place = places[h, q]

            @pl.when(place >= 0)
            def _():
                near = place // LINE
                rows = block_rows(place - near * LINE)
                for k, ref in enumerate(arrived):

                    @pl.when(near == k)
                    def _():
                        fetch(ref, rows, h, q).start()

    for h in range(hops):

        @pl.loop(0, POOL)
        def _(q):
            @pl.when(places[h, q] >= 0)
            def _():
                fetch(arrived[0], block_rows(0), h, q).wait()
                give(h, q).start()

    for h in range(hops):

        @pl.loop(0, POOL)
        def _(q):
            @pl.when(places[h, q] >= 0)
            def _():
                give(h, q).wait()


def relay_back(places, arrived):
    hops = places.shape[0]
    return pl.pallas_call(
        relay_back_kernel,
        out_shape=tuple([panel(POOL)] * hops),
        in_specs=[smem_spec()] + [any_spec()] * len(arrived),
        out_specs=tuple([any_spec()] * hops),
        scratch_shapes=[
            pltpu.VMEM((hops * POOL, NBF, NBF), jnp.bfloat16),
            pltpu.SemaphoreType.DMA((hops * POOL,)),
            pltpu.SemaphoreType.DMA,
        ],
        cost_estimate=pl.CostEstimate(flops=1000, bytes_accessed=4 << 20, transcendentals=0),
        name="relay_back",
    )(places, *arrived)


def domain_kernel(extra_count, *refs):
    inbound, *extras = refs[: 1 + extra_count]
    basis, basis_t, base_in, w_row, w_hid1, w_hid1_t, w_hid2, w_hid2_t, w_out, weights = refs[
        1 + extra_count : 11 + extra_count
    ]
    reply, *extra_replies = refs[11 + extra_count : 12 + 2 * extra_count]
    (
        lines,
        codes_v,
        codes,
        seen,
        live_slot,
        live_code,
        live,
        stage,
        acc,
        dense,
        basis_v,
        basis_tv,
        rho,
        hid1,
        hid2,
        blocks,
        meta,
        line_sem,
        in_sem,
        basis_sem,
        out_sem,
        meta_sem,
    ) = refs[12 + 2 * extra_count :]
    sources = inbound.shape[0]
    direct = ranks_of(inbound)
    points, order = basis.shape
    width = order // NBF
    pairs = width * width
    load_t = pltpu.make_async_copy(basis_t, basis_tv, basis_sem.at[0])
    load_n = pltpu.make_async_copy(basis, basis_v, basis_sem.at[1])
    loads = [pltpu.make_async_copy(inbound.at[:, meta_rows(inbound), :], lines.at[pl.ds(0, sources)], line_sem.at[0])]
    for k, ref in enumerate(extras):
        loads.append(pltpu.make_async_copy(ref.at[meta_rows(ref), :], lines.at[sources + k], line_sem.at[1 + k]))
    for load in loads:
        load.start()

    @pl.loop(0, pairs)
    def _(c):
        seen[c] = 0

    live[0] = 0
    for load in loads:
        load.wait()
    head = lax.broadcasted_iota(jnp.int32, lines.shape, 1) == 0
    codes_v[...] = jnp.sum(jnp.where(head, lines[...].astype(jnp.float32), 0.0), axis=1).astype(jnp.int32)
    load = pltpu.make_async_copy(codes_v, codes, line_sem.at[0])
    load.start()
    load.wait()

    def note(ref, entry, rank, slot):
        c = codes[entry, rank]

        @pl.when(c >= 0)
        def _():
            pltpu.make_async_copy(ref.at[block_rows(rank)], stage.at[slot], in_sem.at[slot]).start()
            k = live[0]
            live_slot[k] = slot
            live_code[k] = c
            live[0] = k + 1

    @pl.loop(0, sources)
    def _(source):
        for rank in range(direct):
            note(inbound.at[source], source, rank, source * direct + rank)

    offset = sources * direct
    for k, ref in enumerate(extras):

        @pl.loop(0, ranks_of(ref))
        def _(rank):
            note(ref, sources + k, rank, offset + rank)

        offset += ranks_of(ref)

    load_t.start()
    load_n.start()

    @pl.loop(0, live[0])
    def _(k):
        slot = live_slot[k]
        c = live_code[k]
        pltpu.make_async_copy(inbound.at[0, block_rows(0)], stage.at[slot], in_sem.at[slot]).wait()
        value = stage[slot].astype(jnp.float32)
        before = seen[c]
        seen[c] = 1

        @pl.when(before == 0)
        def _():
            acc[c] = value

        @pl.when(before != 0)
        def _():
            acc[c] = acc[c] + value

    @pl.loop(0, width)
    def _(a):
        rows = block_rows(a)
        for b in range(width):
            there = seen[a * width + b] != 0
            value = jnp.where(there, acc[a * width + b], 0.0)
            dense[rows, b * NBF : (b + 1) * NBF] = value.astype(jnp.bfloat16)

    load_t.wait()
    tile = 256

    @pl.loop(0, points // tile)
    def _(n):
        cols = pl.ds(pl.multiple_of(n * tile, tile), tile)
        part = basis_tv[:, cols]
        projected = jnp.dot(dense[...], part, preferred_element_type=jnp.float32)
        rho[:, cols] = jnp.sum(projected * part.astype(jnp.float32), axis=0, keepdims=True)

    h1 = jnp.tanh(base_in[...] + w_row[...] * rho[...])
    hid1[...] = h1
    h2 = jnp.tanh(jnp.dot(w_hid1_t[...], h1, precision=HI, preferred_element_type=jnp.float32))
    hid2[...] = h2
    h3 = jnp.tanh(jnp.dot(w_hid2_t[...], h2, precision=HI, preferred_element_type=jnp.float32))
    logits = jnp.sum(w_out[...] * h3, axis=0, keepdims=True)
    decay = jnp.exp(-jnp.abs(logits))
    energy_at = -(jnp.maximum(logits, 0.0) + jnp.log1p(decay))
    slope = -jnp.where(logits >= 0, 1.0, decay) / (1.0 + decay)
    g3 = (w_out[...] * slope) * (1.0 - h3 * h3)
    h2 = hid2[...]
    g2 = jnp.dot(w_hid2[...], g3, precision=HI, preferred_element_type=jnp.float32) * (1.0 - h2 * h2)
    h1 = hid1[...]
    g1 = jnp.dot(w_hid1[...], g2, precision=HI, preferred_element_type=jnp.float32) * (1.0 - h1 * h1)
    deriv = jnp.sum(w_row[...] * g1, axis=0, keepdims=True)
    rho[...] = weights[...] * deriv
    total = jnp.sum(weights[...] * energy_at, axis=1, keepdims=True)
    top = total.astype(jnp.bfloat16).astype(jnp.float32)
    rest = total - top
    middle = rest.astype(jnp.bfloat16).astype(jnp.float32)
    low = rest - middle
    lane = lax.broadcasted_iota(jnp.int32, (META, NBF), 1)
    line = jnp.where(lane == 0, top, jnp.where(lane == 1, middle, jnp.where(lane == 2, low, 0.0)))
    meta[...] = line.astype(jnp.bfloat16)

    @pl.loop(0, sources)
    def _(source):
        pltpu.make_async_copy(meta, reply.at[source, pl.ds(direct * NBF, META)], meta_sem).start()

    load_n.wait()

    @pl.loop(0, points // NBF)
    def _(n):
        rows = block_rows(n)
        line = jnp.broadcast_to(rho[:, rows], (NBF, NBF))
        column = line.T
        for b in range(width):
            cols = slice(b * NBF, (b + 1) * NBF)
            basis_v[rows, cols] = (column * basis_v[rows, cols].astype(jnp.float32)).astype(jnp.bfloat16)

    @pl.loop(0, width // 2)
    def _(n):
        cols = pl.ds(pl.multiple_of(n * 2 * NBF, 2 * NBF), 2 * NBF)
        result = jnp.dot(basis_tv[...], basis_v[:, cols], preferred_element_type=jnp.float32).astype(jnp.bfloat16)
        for a in range(width):
            for half in range(2):
                blocks[a * width + 2 * n + half] = result[a * NBF : (a + 1) * NBF, half * NBF : (half + 1) * NBF]

    def give(ref, entry, rank):
        c = codes[entry, rank]

        @pl.when(c >= 0)
        def _():
            pltpu.make_async_copy(blocks.at[c], ref.at[block_rows(rank)], out_sem).start()

    for k, ref in enumerate(extra_replies):

        @pl.loop(0, ranks_of(ref))
        def _(rank):
            give(ref, sources + k, rank)

    @pl.loop(0, sources)
    def _(source):
        for rank in range(direct):
            give(reply.at[source], source, rank)

    @pl.loop(0, live[0])
    def _(k):
        pltpu.make_async_copy(blocks.at[0], reply.at[0, block_rows(0)], out_sem).wait()

    whole = reply.at[:, meta_rows(reply), :]
    pltpu.make_async_copy(whole, whole, meta_sem).wait()


def domain_build(inbound, extras, basis, basis_t, base_in, w_row, w_hid1, w_hid2, w_out, weights):
    sources = inbound.shape[0]
    points, order = basis.shape
    hid = w_hid1.shape[0]
    pairs = (order // NBF) ** 2
    entries = sources + len(extras)
    slots = sources * ranks_of(inbound) + sum(ranks_of(ref) for ref in extras)
    arrays = [inbound] + list(extras)
    return pl.pallas_call(
        functools.partial(domain_kernel, len(extras)),
        out_shape=tuple(jax.ShapeDtypeStruct(ref.shape, jnp.bfloat16) for ref in arrays),
        in_specs=[any_spec()] * (len(arrays) + 2) + [vmem_spec()] * 8,
        out_specs=(any_spec(),) * len(arrays),
        scratch_shapes=[
            pltpu.VMEM((entries, META, NBF), jnp.bfloat16),
            pltpu.VMEM((entries, NBF), jnp.int32),
            pltpu.SMEM((entries, NBF), jnp.int32),
            pltpu.SMEM((pairs,), jnp.int32),
            pltpu.SMEM((slots,), jnp.int32),
            pltpu.SMEM((slots,), jnp.int32),
            pltpu.SMEM((1,), jnp.int32),
            pltpu.VMEM((slots, NBF, NBF), jnp.bfloat16),
            pltpu.VMEM((pairs, NBF, NBF), jnp.float32),
            pltpu.VMEM((order, order), jnp.bfloat16),
            pltpu.VMEM((points, order), jnp.bfloat16),
            pltpu.VMEM((order, points), jnp.bfloat16),
            pltpu.VMEM((1, points), jnp.float32),
            pltpu.VMEM((hid, points), jnp.float32),
            pltpu.VMEM((hid, points), jnp.float32),
            pltpu.VMEM((pairs, NBF, NBF), jnp.bfloat16),
            pltpu.VMEM((META, NBF), jnp.bfloat16),
            pltpu.SemaphoreType.DMA((1 + len(extras),)),
            pltpu.SemaphoreType.DMA((slots,)),
            pltpu.SemaphoreType.DMA((2,)),
            pltpu.SemaphoreType.DMA,
            pltpu.SemaphoreType.DMA,
        ],
        compiler_params=pltpu.CompilerParams(vmem_limit_bytes=60 << 20),
        name="domain_build",
    )(
        *arrays, basis, basis_t, base_in, w_row[:, None], w_hid1, w_hid1.T, w_hid2, w_hid2.T,
        w_out[:, None], weights[None, :],
    )


def collect_kernel(scale, places, returned, *refs):
    extras = refs[:-8]
    fock, energy, parts, result, meta, in_sem, out_sem, meta_sem = refs[-8:]
    copies, owned = places.shape
    sources = returned.shape[0]
    meta_in = pltpu.make_async_copy(returned.at[:, meta_rows(returned), :], meta, meta_sem)
    meta_in.start()

    @pl.loop(0, owned)
    def _(p):
        for t in range(copies):
            entry = places[t, p] // LINE
            rows = block_rows(places[t, p] - entry * LINE)

            @pl.when(entry < sources)
            def _():
                pltpu.make_async_copy(returned.at[entry, rows], parts.at[p, t], in_sem.at[p]).start()

            if extras:

                @pl.when(entry >= sources)
                def _():
                    for k, ref in enumerate(extras):

                        @pl.when(entry == sources + k)
                        def _():
                            pltpu.make_async_copy(ref.at[rows], parts.at[p, t], in_sem.at[p]).start()

    meta_in.wait()
    lane = lax.broadcasted_iota(jnp.int32, meta.shape, 2)
    row = lax.broadcasted_iota(jnp.int32, meta.shape, 1)
    sent = jnp.where((lane < 3) & (row == 0), meta[...].astype(jnp.float32), 0.0)
    per_source = jnp.sum(jnp.sum(sent, axis=0), axis=0, keepdims=True)
    energy[...] = jnp.sum(per_source, axis=1, keepdims=True) * scale

    @pl.loop(0, owned)
    def _(p):
        pltpu.make_async_copy(parts.at[p], parts.at[p], in_sem.at[p]).wait()
        total = parts[p, 0].astype(jnp.float32)
        for t in range(1, copies):
            total = total + parts[p, t].astype(jnp.float32)
        result[p] = total
        pltpu.make_async_copy(result.at[p], fock.at[p], out_sem).start()

    pltpu.make_async_copy(result, fock, out_sem).wait()


def collect_blocks(places, returned, extras, scale):
    copies, owned = places.shape
    sources = returned.shape[0]
    fock, energy = pl.pallas_call(
        functools.partial(collect_kernel, scale),
        out_shape=(
            jax.ShapeDtypeStruct((owned, NBF, NBF), jnp.float32),
            jax.ShapeDtypeStruct((1, 1), jnp.float32),
        ),
        in_specs=[smem_spec()] + [any_spec()] * (1 + len(extras)),
        out_specs=(any_spec(), vmem_spec()),
        scratch_shapes=[
            pltpu.VMEM((owned, copies, NBF, NBF), jnp.bfloat16),
            pltpu.VMEM((owned, NBF, NBF), jnp.float32),
            pltpu.VMEM((sources, META, NBF), jnp.bfloat16),
            pltpu.SemaphoreType.DMA((owned,)),
            pltpu.SemaphoreType.DMA,
            pltpu.SemaphoreType.DMA,
        ],
        name="collect_blocks",
    )(places, returned, *extras)
    return fock, energy[0, 0]


def exchange(array):
    return lax.all_to_all(array, AXES, split_axis=0, concat_axis=0, tiled=True)


def swap(arrays, axis, first):
    size = lax.axis_size(axis)
    return [
        lax.ppermute(array, axis, [(i, i ^ (first + k)) for i in range(size)]) if first + k else array
        for k, array in enumerate(arrays)
    ]


def body(density, dest, code, basis, descriptors, weights, w_in, w_hid1, w_hid2, w_out):
    rows_x, rows_z = lax.axis_size("gx"), lax.axis_size("gy")
    domains = rows_x * rows_z
    owned = density.shape[0]
    copies = dest.shape[1]
    capacity = max(2, 2 * copies * owned // domains)
    points = basis.shape[0]
    scale = 1.0 / (math.sqrt(points) * domains)
    basis_t = basis.T
    base_in = jnp.dot(w_in[1:].T, descriptors, precision=HI)
    fixed = (basis, basis_t, base_in, w_in[0], w_hid1, w_hid2, w_out, weights)

    def plain():
        outgoing, places = send_blocks(density, dest, code, domains, capacity, None)
        (replies,) = domain_build(exchange(outgoing), [], *fixed)
        return collect_blocks(places, exchange(replies), [], scale)

    if capacity < 8:
        return plain()
    direct = capacity // 2
    ranks = (rows_z - 1) * (capacity - direct)
    outgoing, *extras, places = send_blocks(density, dest, code, domains, direct, (rows_x, rows_z))
    lines_in = swap(extras[rows_x:], "gy", 1)
    near_in = swap(extras[:rows_x], "gx", 0)
    inbound = exchange(outgoing)
    *relayed, relay_places = relay(lines_in, rows_x, ranks)
    relayed_in = swap(relayed, "gx", 0)
    raised = jnp.max(inbound[:, direct * NBF, FLAG].astype(jnp.float32)) > 0

    def split():
        replies, *others = domain_build(inbound, near_in + relayed_in, *fixed)
        relayed_back = swap(others[rows_x:], "gx", 0)
        near_back = swap(others[:rows_x], "gx", 0)
        returned = exchange(replies)
        lines_back = swap(relay_back(relay_places, relayed_back), "gy", 1)
        return collect_blocks(places, returned, near_back + lines_back, scale)

    return lax.cond(raised, plain, split)


def solution(mesh):
    placed = (
        P(AXES, None, None),
        P(AXES, None),
        P(AXES, None),
        P(AXES, None),
        P(None, AXES),
        P(AXES),
        P(),
        P(),
        P(),
        P(),
    )
    return jax.shard_map(
        body,
        mesh=mesh,
        in_specs=placed,
        out_specs=(P(AXES, None, None), P()),
        check_vma=False,
    )
```

```python
import functools
import math

import jax
import jax.numpy as jnp
from jax import lax
from jax.experimental import pallas as pl
from jax.experimental.pallas import tpu as pltpu
from jax.sharding import PartitionSpec as P

NBF = 128
META = 8
LINE = 32
FLAG = 64
POOL = 16
AXES = ("gx", "gy")
HI = lax.Precision.HIGHEST


def any_spec():
    return pl.BlockSpec(memory_space=pl.ANY)


def smem_spec():
    return pl.BlockSpec(memory_space=pltpu.SMEM)


def vmem_spec():
    return pl.BlockSpec(memory_space=pltpu.VMEM)


def block_rows(rank):
    return pl.ds(pl.multiple_of(rank * NBF, NBF), NBF)


def panel(ranks):
    return jax.ShapeDtypeStruct((ranks * NBF + META, NBF), jnp.bfloat16)


def ranks_of(array):
    return array.shape[-2] // NBF


def meta_rows(array):
    return pl.ds(ranks_of(array) * NBF, META)


def lane_row(shape):
    lane = lax.broadcasted_iota(jnp.int32, shape, len(shape) - 1)
    row = lax.broadcasted_iota(jnp.int32, shape, len(shape) - 2)
    return lane, row


def send_kernel(groups, dest, code, density, *refs):
    copies, owned = dest.shape
    out, *extras, places = refs[:-7]
    count, pool, flag, blocks, codes, codes16, sems = refs[-7:]
    domains = out.shape[0]
    direct = ranks_of(out)
    load = pltpu.make_async_copy(density, blocks, sems.at[0])
    load.start()

    @pl.loop(0, domains)
    def _(d):
        count[d] = 0

    codes[...] = jnp.full(codes.shape, -1.0, jnp.float32)
    lane, row = lane_row((META, NBF))
    flag[0] = 0
    if groups is not None:
        rows_x, rows_z = groups
        me_x, me_z = lax.axis_index("gx"), lax.axis_index("gy")
        for k in range(rows_z):
            pool[k] = 0

    @pl.loop(0, owned)
    def _(p):
        for t in range(copies):
            d = dest[t, p]
            rank = count[d]
            count[d] = rank + 1
            value = code[t, p].astype(jnp.float32)
            if groups is None:
                entry, place = d, rank
                codes[entry] = jnp.where((lane == place) & (row == 0), value, codes[entry])
            else:
                target = d // rows_z
                near = target ^ me_x
                far = (d - target * rows_z) ^ me_z
                slot = pool[far]
                spill = (rank >= direct) & (far != 0)
                pool[far] = slot + spill.astype(jnp.int32)
                flag[0] = flag[0] | (spill & (slot >= POOL)).astype(jnp.int32)
                other = jnp.where(far == 0, domains + near, domains + rows_x + far - 1)
                entry = jnp.where(rank < direct, d, other)
                other = jnp.where(far == 0, rank - direct, jnp.minimum(slot, POOL - 1))
                place = jnp.where(rank < direct, rank, other)
                side = jnp.where(row == 0, value, target.astype(jnp.float32))
                codes[entry] = jnp.where((lane == place) & (row < 2), side, codes[entry])
            places[t, p] = entry * LINE + place

    if groups is not None:
        raised = flag[0].astype(jnp.float32)
        mark = (lane == FLAG) & (row == 0)
        codes[0:domains] = jnp.where(mark, raised, codes[0:domains])
    codes16[...] = codes[...].astype(jnp.bfloat16)
    metas = [pltpu.make_async_copy(codes16.at[pl.ds(0, domains)], out.at[:, meta_rows(out), :], sems.at[1])]
    for k, ref in enumerate(extras):
        metas.append(pltpu.make_async_copy(codes16.at[domains + k], ref.at[meta_rows(ref), :], sems.at[3 + k]))
    for copy in metas:
        copy.start()
    load.wait()

    @pl.loop(0, owned)
    def _(p):
        for t in range(copies):
            entry = places[t, p] // LINE
            rows = block_rows(places[t, p] - entry * LINE)

            @pl.when(entry < domains)
            def _():
                pltpu.make_async_copy(blocks.at[p], out.at[entry, rows], sems.at[2]).start()

            if extras:

                @pl.when(entry >= domains)
                def _():
                    for k, ref in enumerate(extras):

                        @pl.when(entry == domains + k)
                        def _():
                            pltpu.make_async_copy(blocks.at[p], ref.at[rows], sems.at[2]).start()

    for copy in metas:
        copy.wait()
    part = out.at[pl.ds(0, copies * owned // direct), pl.ds(0, direct * NBF), :]
    pltpu.make_async_copy(part, part, sems.at[2]).wait()


def send_blocks(density, dest, code, domains, direct, groups):
    owned = density.shape[0]
    copies = dest.shape[1]
    extras = []
    if groups is not None:
        extras = [panel(direct)] * groups[0] + [panel(POOL)] * (groups[1] - 1)
    entries = domains + len(extras)
    return pl.pallas_call(
        functools.partial(send_kernel, groups),
        out_shape=(
            jax.ShapeDtypeStruct((domains, direct * NBF + META, NBF), jnp.bfloat16),
            *extras,
            jax.ShapeDtypeStruct((copies, owned), jnp.int32),
        ),
        in_specs=[smem_spec(), smem_spec(), any_spec()],
        out_specs=(any_spec(),) * (1 + len(extras)) + (smem_spec(),),
        scratch_shapes=[
            pltpu.SMEM((domains,), jnp.int32),
            pltpu.SMEM((LINE,), jnp.int32),
            pltpu.SMEM((1,), jnp.int32),
            pltpu.VMEM((owned, NBF, NBF), jnp.bfloat16),
            pltpu.VMEM((entries, META, NBF), jnp.float32),
            pltpu.VMEM((entries, META, NBF), jnp.bfloat16),
            pltpu.SemaphoreType.DMA((3 + len(extras),)),
        ],
        name="send_blocks",
    )(dest.T, code.T, density)


def relay_kernel(*refs):
    info, count, stage, lines, ints, codes, codes16, in_sem, sems = refs[-9:]
    hops = lines.shape[0]
    arrived = refs[:hops]
    outs = refs[hops : -10]
    places = refs[-10]
    ranks = ranks_of(outs[0])
    me = lax.axis_index("gx")
    loads = [
        pltpu.make_async_copy(ref.at[meta_rows(ref), :], lines.at[h], sems.at[h]) for h, ref in enumerate(arrived)
    ]
    for load in loads:
        load.start()
    codes[...] = jnp.full(codes.shape, -1.0, jnp.float32)
    lane, row = lane_row((META, NBF))
    for k in range(len(outs)):
        count[k] = 0
    for load in loads:
        load.wait()
    ints[...] = lines[...].astype(jnp.float32).astype(jnp.int32)
    load = pltpu.make_async_copy(ints, info, sems.at[0])
    load.start()
    load.wait()

    def fetch(h, q):
        return pltpu.make_async_copy(arrived[h].at[block_rows(q)], stage.at[h * POOL + q], in_sem.at[h * POOL + q])

    for h in range(hops):

        @pl.loop(0, POOL)
        def _(q):
            places[h, q] = -1
            c = info[h, 0, q]

            @pl.when(c >= 0)
            def _():
                fetch(h, q).start()
                near = info[h, 1, q] ^ me
                slot = jnp.minimum(count[near], ranks - 1)
                count[near] = slot + 1
                places[h, q] = near * LINE + slot
                hit = (lane == slot) & (row == 0)
                codes[near] = jnp.where(hit, c.astype(jnp.float32), codes[near])

    codes16[...] = codes[...].astype(jnp.bfloat16)
    metas = [
        pltpu.make_async_copy(codes16.at[k], ref.at[meta_rows(ref), :], sems.at[hops + k])
        for k, ref in enumerate(outs)
    ]
    for copy in metas:
        copy.start()
    last = sems.at[hops + len(outs)]
    for h in range(hops):

        @pl.loop(0, POOL)
        def _(q):
            place = places[h, q]

            @pl.when(place >= 0)
            def _():
                fetch(h, q).wait()
                near = place // LINE
                rows = block_rows(place - near * LINE)
                for k, ref in enumerate(outs):

                    @pl.when(near == k)
                    def _():
                        pltpu.make_async_copy(stage.at[h * POOL + q], ref.at[rows], last).start()

    for copy in metas:
        copy.wait()
    for h in range(hops):

        @pl.loop(0, POOL)
        def _(q):
            @pl.when(places[h, q] >= 0)
            def _():
                pltpu.make_async_copy(stage.at[0], outs[0].at[block_rows(0)], last).wait()


def relay(arrived, near_count, ranks):
    hops = len(arrived)
    return pl.pallas_call(
        relay_kernel,
        out_shape=tuple([panel(ranks)] * near_count + [jax.ShapeDtypeStruct((hops, POOL), jnp.int32)]),
        in_specs=[any_spec()] * hops,
        out_specs=tuple([any_spec()] * near_count + [smem_spec()]),
        scratch_shapes=[
            pltpu.SMEM((hops, META, NBF), jnp.int32),
            pltpu.SMEM((near_count,), jnp.int32),
            pltpu.VMEM((hops * POOL, NBF, NBF), jnp.bfloat16),
            pltpu.VMEM((hops, META, NBF), jnp.bfloat16),
            pltpu.VMEM((hops, META, NBF), jnp.int32),
            pltpu.VMEM((near_count, META, NBF), jnp.float32),
            pltpu.VMEM((near_count, META, NBF), jnp.bfloat16),
            pltpu.SemaphoreType.DMA((hops * POOL,)),
            pltpu.SemaphoreType.DMA((hops + near_count + 1,)),
        ],
        cost_estimate=pl.CostEstimate(flops=1000, bytes_accessed=4 << 20, transcendentals=0),
        name="relay",
    )(*arrived)


def relay_back_kernel(places, *refs):
    stage, in_sem, out_sem = refs[-3:]
    hops = places.shape[0]
    arrived, outs = refs[: -3 - hops], refs[-3 - hops : -3]

    def fetch(ref, rows, h, q):
        return pltpu.make_async_copy(ref.at[rows], stage.at[h * POOL + q], in_sem.at[h * POOL + q])

    def give(h, q):
        return pltpu.make_async_copy(stage.at[h * POOL + q], outs[h].at[block_rows(q)], out_sem)

    for h in range(hops):

        @pl.loop(0, POOL)
        def _(q):
            place = places[h, q]

            @pl.when(place >= 0)
            def _():
                near = place // LINE
                rows = block_rows(place - near * LINE)
                for k, ref in enumerate(arrived):

                    @pl.when(near == k)
                    def _():
                        fetch(ref, rows, h, q).start()

    for h in range(hops):

        @pl.loop(0, POOL)
        def _(q):
            @pl.when(places[h, q] >= 0)
            def _():
                fetch(arrived[0], block_rows(0), h, q).wait()
                give(h, q).start()

    for h in range(hops):

        @pl.loop(0, POOL)
        def _(q):
            @pl.when(places[h, q] >= 0)
            def _():
                give(h, q).wait()


def relay_back(places, arrived):
    hops = places.shape[0]
    return pl.pallas_call(
        relay_back_kernel,
        out_shape=tuple([panel(POOL)] * hops),
        in_specs=[smem_spec()] + [any_spec()] * len(arrived),
        out_specs=tuple([any_spec()] * hops),
        scratch_shapes=[
            pltpu.VMEM((hops * POOL, NBF, NBF), jnp.bfloat16),
            pltpu.SemaphoreType.DMA((hops * POOL,)),
            pltpu.SemaphoreType.DMA,
        ],
        cost_estimate=pl.CostEstimate(flops=1000, bytes_accessed=4 << 20, transcendentals=0),
        name="relay_back",
    )(places, *arrived)


def domain_kernel(extra_count, *refs):
    inbound, *extras = refs[: 1 + extra_count]
    basis, basis_t, base_in, w_row, w_hid1, w_hid1_t, w_hid2, w_hid2_t, w_out, weights = refs[
        1 + extra_count : 11 + extra_count
    ]
    reply, *extra_replies = refs[11 + extra_count : 12 + 2 * extra_count]
    (
        lines,
        codes_v,
        codes,
        seen,
        live_slot,
        live_code,
        live,
        stage,
        acc,
        dense,
        basis_v,
        basis_tv,
        rho,
        hid1,
        hid2,
        blocks,
        meta,
        line_sem,
        in_sem,
        basis_sem,
        out_sem,
        meta_sem,
    ) = refs[12 + 2 * extra_count :]
    sources = inbound.shape[0]
    direct = ranks_of(inbound)
    points, order = basis.shape
    width = order // NBF
    pairs = width * width
    load_t = pltpu.make_async_copy(basis_t, basis_tv, basis_sem.at[0])
    load_n = pltpu.make_async_copy(basis, basis_v, basis_sem.at[1])
    loads = [pltpu.make_async_copy(inbound.at[:, meta_rows(inbound), :], lines.at[pl.ds(0, sources)], line_sem.at[0])]
    for k, ref in enumerate(extras):
        loads.append(pltpu.make_async_copy(ref.at[meta_rows(ref), :], lines.at[sources + k], line_sem.at[1 + k]))
    for load in loads:
        load.start()

    @pl.loop(0, pairs)
    def _(c):
        seen[c] = 0

    live[0] = 0
    for load in loads:
        load.wait()
    head = lax.broadcasted_iota(jnp.int32, lines.shape, 1) == 0
    codes_v[...] = jnp.sum(jnp.where(head, lines[...].astype(jnp.float32), 0.0), axis=1).astype(jnp.int32)
    load = pltpu.make_async_copy(codes_v, codes, line_sem.at[0])
    load.start()
    load.wait()

    def note(ref, entry, rank, slot):
        c = codes[entry, rank]

        @pl.when(c >= 0)
        def _():
            pltpu.make_async_copy(ref.at[block_rows(rank)], stage.at[slot], in_sem.at[slot]).start()
            k = live[0]
            live_slot[k] = slot
            live_code[k] = c
            live[0] = k + 1

    @pl.loop(0, sources)
    def _(source):
        for rank in range(direct):
            note(inbound.at[source], source, rank, source * direct + rank)

    offset = sources * direct
    for k, ref in enumerate(extras):

        @pl.loop(0, ranks_of(ref))
        def _(rank):
            note(ref, sources + k, rank, offset + rank)

        offset += ranks_of(ref)

    load_t.start()
    load_n.start()

    @pl.loop(0, live[0])
    def _(k):
        slot = live_slot[k]
        c = live_code[k]
        pltpu.make_async_copy(inbound.at[0, block_rows(0)], stage.at[slot], in_sem.at[slot]).wait()
        value = stage[slot].astype(jnp.float32)
        before = seen[c]
        seen[c] = 1

        @pl.when(before == 0)
        def _():
            acc[c] = value

        @pl.when(before != 0)
        def _():
            acc[c] = acc[c] + value

    @pl.loop(0, width)
    def _(a):
        rows = block_rows(a)
        for b in range(width):
            there = seen[a * width + b] != 0
            value = jnp.where(there, acc[a * width + b], 0.0)
            dense[rows, b * NBF : (b + 1) * NBF] = value.astype(jnp.bfloat16)

    load_t.wait()
    tile = 256

    @pl.loop(0, points // tile)
    def _(n):
        cols = pl.ds(pl.multiple_of(n * tile, tile), tile)
        part = basis_tv[:, cols]
        projected = jnp.dot(dense[...], part, preferred_element_type=jnp.float32)
        rho[:, cols] = jnp.sum(projected * part.astype(jnp.float32), axis=0, keepdims=True)

    h1 = jnp.tanh(base_in[...] + w_row[...] * rho[...])
    hid1[...] = h1
    h2 = jnp.tanh(jnp.dot(w_hid1_t[...], h1, precision=HI, preferred_element_type=jnp.float32))
    hid2[...] = h2
    h3 = jnp.tanh(jnp.dot(w_hid2_t[...], h2, precision=HI, preferred_element_type=jnp.float32))
    logits = jnp.sum(w_out[...] * h3, axis=0, keepdims=True)
    decay = jnp.exp(-jnp.abs(logits))
    energy_at = -(jnp.maximum(logits, 0.0) + jnp.log1p(decay))
    slope = -jnp.where(logits >= 0, 1.0, decay) / (1.0 + decay)
    g3 = (w_out[...] * slope) * (1.0 - h3 * h3)
    h2 = hid2[...]
    g2 = jnp.dot(w_hid2[...], g3, precision=HI, preferred_element_type=jnp.float32) * (1.0 - h2 * h2)
    h1 = hid1[...]
    g1 = jnp.dot(w_hid1[...], g2, precision=HI, preferred_element_type=jnp.float32) * (1.0 - h1 * h1)
    deriv = jnp.sum(w_row[...] * g1, axis=0, keepdims=True)
    rho[...] = weights[...] * deriv
    total = jnp.sum(weights[...] * energy_at, axis=1, keepdims=True)
    top = total.astype(jnp.bfloat16).astype(jnp.float32)
    rest = total - top
    middle = rest.astype(jnp.bfloat16).astype(jnp.float32)
    low = rest - middle
    lane = lax.broadcasted_iota(jnp.int32, (META, NBF), 1)
    line = jnp.where(lane == 0, top, jnp.where(lane == 1, middle, jnp.where(lane == 2, low, 0.0)))
    meta[...] = line.astype(jnp.bfloat16)

    @pl.loop(0, sources)
    def _(source):
        pltpu.make_async_copy(meta, reply.at[source, pl.ds(direct * NBF, META)], meta_sem).start()

    load_n.wait()

    @pl.loop(0, points // NBF)
    def _(n):
        rows = block_rows(n)
        line = jnp.broadcast_to(rho[:, rows], (NBF, NBF))
        column = line.T
        for b in range(width):
            cols = slice(b * NBF, (b + 1) * NBF)
            basis_v[rows, cols] = (column * basis_v[rows, cols].astype(jnp.float32)).astype(jnp.bfloat16)

    @pl.loop(0, width // 2)
    def _(n):
        cols = pl.ds(pl.multiple_of(n * 2 * NBF, 2 * NBF), 2 * NBF)
        result = jnp.dot(basis_tv[...], basis_v[:, cols], preferred_element_type=jnp.float32).astype(jnp.bfloat16)
        for a in range(width):
            for half in range(2):
                blocks[a * width + 2 * n + half] = result[a * NBF : (a + 1) * NBF, half * NBF : (half + 1) * NBF]

    def give(ref, entry, rank):
        c = codes[entry, rank]

        @pl.when(c >= 0)
        def _():
            pltpu.make_async_copy(blocks.at[c], ref.at[block_rows(rank)], out_sem).start()

    for k, ref in enumerate(extra_replies):

        @pl.loop(0, ranks_of(ref))
        def _(rank):
            give(ref, sources + k, rank)

    @pl.loop(0, sources)
    def _(source):
        for rank in range(direct):
            give(reply.at[source], source, rank)

    @pl.loop(0, live[0])
    def _(k):
        pltpu.make_async_copy(blocks.at[0], reply.at[0, block_rows(0)], out_sem).wait()

    whole = reply.at[:, meta_rows(reply), :]
    pltpu.make_async_copy(whole, whole, meta_sem).wait()


def domain_build(inbound, extras, basis, *fixed):
    sources = inbound.shape[0]
    points, order = basis.shape
    hid = fixed[1].shape[0]
    pairs = (order // NBF) ** 2
    entries = sources + len(extras)
    slots = sources * ranks_of(inbound) + sum(ranks_of(ref) for ref in extras)
    arrays = [inbound] + list(extras)
    return pl.pallas_call(
        functools.partial(domain_kernel, len(extras)),
        out_shape=tuple(jax.ShapeDtypeStruct(ref.shape, jnp.bfloat16) for ref in arrays),
        in_specs=[any_spec()] * (len(arrays) + 2) + [vmem_spec()] * 8,
        out_specs=(any_spec(),) * len(arrays),
        scratch_shapes=[
            pltpu.VMEM((entries, META, NBF), jnp.bfloat16),
            pltpu.VMEM((entries, NBF), jnp.int32),
            pltpu.SMEM((entries, NBF), jnp.int32),
            pltpu.SMEM((pairs,), jnp.int32),
            pltpu.SMEM((slots,), jnp.int32),
            pltpu.SMEM((slots,), jnp.int32),
            pltpu.SMEM((1,), jnp.int32),
            pltpu.VMEM((slots, NBF, NBF), jnp.bfloat16),
            pltpu.VMEM((pairs, NBF, NBF), jnp.float32),
            pltpu.VMEM((order, order), jnp.bfloat16),
            pltpu.VMEM((points, order), jnp.bfloat16),
            pltpu.VMEM((order, points), jnp.bfloat16),
            pltpu.VMEM((1, points), jnp.float32),
            pltpu.VMEM((hid, points), jnp.float32),
            pltpu.VMEM((hid, points), jnp.float32),
            pltpu.VMEM((pairs, NBF, NBF), jnp.bfloat16),
            pltpu.VMEM((META, NBF), jnp.bfloat16),
            pltpu.SemaphoreType.DMA((1 + len(extras),)),
            pltpu.SemaphoreType.DMA((slots,)),
            pltpu.SemaphoreType.DMA((2,)),
            pltpu.SemaphoreType.DMA,
            pltpu.SemaphoreType.DMA,
        ],
        compiler_params=pltpu.CompilerParams(vmem_limit_bytes=60 << 20),
        name="domain_build",
    )(*arrays, basis, *fixed)


def collect_kernel(scale, places, returned, *refs):
    extras = refs[:-8]
    fock, energy, parts, result, meta, in_sem, out_sem, meta_sem = refs[-8:]
    copies, owned = places.shape
    sources = returned.shape[0]
    meta_in = pltpu.make_async_copy(returned.at[:, meta_rows(returned), :], meta, meta_sem)
    meta_in.start()

    @pl.loop(0, owned)
    def _(p):
        for t in range(copies):
            entry = places[t, p] // LINE
            rows = block_rows(places[t, p] - entry * LINE)

            @pl.when(entry < sources)
            def _():
                pltpu.make_async_copy(returned.at[entry, rows], parts.at[p, t], in_sem.at[p]).start()

            if extras:

                @pl.when(entry >= sources)
                def _():
                    for k, ref in enumerate(extras):

                        @pl.when(entry == sources + k)
                        def _():
                            pltpu.make_async_copy(ref.at[rows], parts.at[p, t], in_sem.at[p]).start()

    meta_in.wait()
    lane = lax.broadcasted_iota(jnp.int32, meta.shape, 2)
    row = lax.broadcasted_iota(jnp.int32, meta.shape, 1)
    sent = jnp.where((lane < 3) & (row == 0), meta[...].astype(jnp.float32), 0.0)
    per_source = jnp.sum(jnp.sum(sent, axis=0), axis=0, keepdims=True)
    energy[...] = jnp.sum(per_source, axis=1, keepdims=True) * scale

    @pl.loop(0, owned)
    def _(p):
        pltpu.make_async_copy(parts.at[p], parts.at[p], in_sem.at[p]).wait()
        total = parts[p, 0].astype(jnp.float32)
        for t in range(1, copies):
            total = total + parts[p, t].astype(jnp.float32)
        result[p] = total
        pltpu.make_async_copy(result.at[p], fock.at[p], out_sem).start()

    pltpu.make_async_copy(result, fock, out_sem).wait()


def collect_blocks(places, returned, extras, scale):
    copies, owned = places.shape
    sources = returned.shape[0]
    fock, energy = pl.pallas_call(
        functools.partial(collect_kernel, scale),
        out_shape=(
            jax.ShapeDtypeStruct((owned, NBF, NBF), jnp.float32),
            jax.ShapeDtypeStruct((1, 1), jnp.float32),
        ),
        in_specs=[smem_spec()] + [any_spec()] * (1 + len(extras)),
        out_specs=(any_spec(), vmem_spec()),
        scratch_shapes=[
            pltpu.VMEM((owned, copies, NBF, NBF), jnp.bfloat16),
            pltpu.VMEM((owned, NBF, NBF), jnp.float32),
            pltpu.VMEM((sources, META, NBF), jnp.bfloat16),
            pltpu.SemaphoreType.DMA((owned,)),
            pltpu.SemaphoreType.DMA,
            pltpu.SemaphoreType.DMA,
        ],
        name="collect_blocks",
    )(places, returned, *extras)
    return fock, energy[0, 0]


def exchange(array):
    return lax.all_to_all(array, AXES, split_axis=0, concat_axis=0, tiled=True)


def swap(arrays, axis, first):
    size = lax.axis_size(axis)
    return [
        lax.ppermute(array, axis, [(i, i ^ (first + k)) for i in range(size)]) if first + k else array
        for k, array in enumerate(arrays)
    ]


def body(density, dest, code, basis, descriptors, weights, w_in, w_hid1, w_hid2, w_out):
    rows_x, rows_z = lax.axis_size("gx"), lax.axis_size("gy")
    domains = rows_x * rows_z
    owned = density.shape[0]
    copies = dest.shape[1]
    capacity = max(2, 2 * copies * owned // domains)
    points = basis.shape[0]
    scale = 1.0 / (math.sqrt(points) * domains)
    basis_t = basis.T
    base_in = jnp.dot(w_in[1:].T, descriptors, precision=HI)
    fixed = (
        basis, basis_t, base_in, w_in[0][:, None], w_hid1, w_hid1.T, w_hid2, w_hid2.T, w_out[:, None],
        weights[None, :],
    )

    def plain():
        outgoing, places = send_blocks(density, dest, code, domains, capacity, None)
        (replies,) = domain_build(exchange(outgoing), [], *fixed)
        return collect_blocks(places, exchange(replies), [], scale)

    if capacity < 8:
        return plain()
    direct = capacity // 2
    ranks = (rows_z - 1) * (capacity - direct)
    outgoing, *extras, places = send_blocks(density, dest, code, domains, direct, (rows_x, rows_z))
    lines_in = swap(extras[rows_x:], "gy", 1)
    near_in = swap(extras[:rows_x], "gx", 0)
    outgoing, lines_in, near_in = lax.optimization_barrier((outgoing, lines_in, near_in))
    inbound = exchange(outgoing)
    *relayed, relay_places = relay(lines_in, rows_x, ranks)
    relayed_in = swap(relayed, "gx", 0)
    raised = jnp.max(inbound[:, direct * NBF, FLAG].astype(jnp.float32)) > 0

    def split():
        replies, *others = domain_build(inbound, near_in + relayed_in, *fixed)
        relayed_back = swap(others[rows_x:], "gx", 0)
        near_back = swap(others[:rows_x], "gx", 0)
        returned = exchange(replies)
        lines_back = swap(relay_back(relay_places, relayed_back), "gy", 1)
        return collect_blocks(places, returned, near_back + lines_back, scale)

    return lax.cond(raised, plain, split)


def solution(mesh):
    placed = (
        P(AXES, None, None),
        P(AXES, None),
        P(AXES, None),
        P(AXES, None),
        P(None, AXES),
        P(AXES),
        P(),
        P(),
        P(),
        P(),
    )
    return jax.shard_map(
        body,
        mesh=mesh,
        in_specs=placed,
        out_specs=(P(AXES, None, None), P()),
        check_vma=False,
    )
```

```python
import functools
import math

import jax
import jax.numpy as jnp
from jax import lax
from jax.experimental import pallas as pl
from jax.experimental.pallas import tpu as pltpu
from jax.sharding import PartitionSpec as P

NBF = 128
META = 8
LINE = 32
FLAG = 64
POOL = 16
AXES = ("gx", "gy")
HI = lax.Precision.HIGHEST


def any_spec():
    return pl.BlockSpec(memory_space=pl.ANY)


def smem_spec():
    return pl.BlockSpec(memory_space=pltpu.SMEM)


def vmem_spec():
    return pl.BlockSpec(memory_space=pltpu.VMEM)


def block_rows(rank):
    return pl.ds(pl.multiple_of(rank * NBF, NBF), NBF)


def panel(ranks):
    return jax.ShapeDtypeStruct((ranks * NBF + META, NBF), jnp.bfloat16)


def ranks_of(array):
    return array.shape[-2] // NBF


def meta_rows(array):
    return pl.ds(ranks_of(array) * NBF, META)


def lane_row(shape):
    lane = lax.broadcasted_iota(jnp.int32, shape, len(shape) - 1)
    row = lax.broadcasted_iota(jnp.int32, shape, len(shape) - 2)
    return lane, row


def plan_kernel(groups, direct, dest, code, density, *refs):
    copies, owned = dest.shape
    heads, *extras, places = refs[:-7]
    count, pool, flag, blocks, codes, codes16, sems = refs[-7:]
    domains = heads.shape[0]
    load = pltpu.make_async_copy(density, blocks, sems.at[0])
    if extras:
        load.start()

    @pl.loop(0, domains)
    def _(d):
        count[d] = 0

    codes[...] = jnp.full(codes.shape, -1.0, jnp.float32)
    lane, row = lane_row((META, NBF))
    flag[0] = 0
    if groups is not None:
        rows_x, rows_z = groups
        me_x, me_z = lax.axis_index("gx"), lax.axis_index("gy")
        for k in range(rows_z):
            pool[k] = 0

    @pl.loop(0, owned)
    def _(p):
        for t in range(copies):
            d = dest[t, p]
            rank = count[d]
            count[d] = rank + 1
            value = code[t, p].astype(jnp.float32)
            if groups is None:
                entry, place = d, rank
                codes[entry] = jnp.where((lane == place) & (row == 0), value, codes[entry])
            else:
                target = d // rows_z
                near = target ^ me_x
                far = (d - target * rows_z) ^ me_z
                slot = pool[far]
                spill = (rank >= direct) & (far != 0)
                pool[far] = slot + spill.astype(jnp.int32)
                flag[0] = flag[0] | (spill & (slot >= POOL)).astype(jnp.int32)
                other = jnp.where(far == 0, domains + near, domains + rows_x + far - 1)
                entry = jnp.where(rank < direct, d, other)
                other = jnp.where(far == 0, rank - direct, jnp.minimum(slot, POOL - 1))
                place = jnp.where(rank < direct, rank, other)
                side = jnp.where(row == 0, value, target.astype(jnp.float32))
                codes[entry] = jnp.where((lane == place) & (row < 2), side, codes[entry])
            places[t, p] = entry * LINE + place

    if groups is not None:
        raised = flag[0].astype(jnp.float32)
        mark = (lane == FLAG) & (row == 0)
        codes[0:domains] = jnp.where(mark, raised, codes[0:domains])
    codes16[...] = codes[...].astype(jnp.bfloat16)
    metas = [pltpu.make_async_copy(codes16.at[pl.ds(0, domains)], heads, sems.at[1])]
    for k, ref in enumerate(extras):
        metas.append(pltpu.make_async_copy(codes16.at[domains + k], ref.at[meta_rows(ref), :], sems.at[3 + k]))
    for copy in metas:
        copy.start()
    if extras:
        load.wait()
        count[0] = 0

        @pl.loop(0, owned)
        def _(p):
            for t in range(copies):
                entry = places[t, p] // LINE
                rows = block_rows(places[t, p] - entry * LINE)

                @pl.when(entry >= domains)
                def _():
                    count[0] = count[0] + 1
                    for k, ref in enumerate(extras):

                        @pl.when(entry == domains + k)
                        def _():
                            pltpu.make_async_copy(blocks.at[p], ref.at[rows], sems.at[2]).start()

        @pl.loop(0, count[0])
        def _(k):
            pltpu.make_async_copy(blocks.at[0], extras[0].at[block_rows(0)], sems.at[2]).wait()

    for copy in metas:
        copy.wait()


def plan_blocks(density, dest, code, domains, direct, groups):
    owned = density.shape[0]
    copies = dest.shape[1]
    extras = []
    if groups is not None:
        extras = [panel(direct)] * groups[0] + [panel(POOL)] * (groups[1] - 1)
    entries = domains + len(extras)
    return pl.pallas_call(
        functools.partial(plan_kernel, groups, direct),
        out_shape=(
            jax.ShapeDtypeStruct((domains, META, NBF), jnp.bfloat16),
            *extras,
            jax.ShapeDtypeStruct((copies, owned), jnp.int32),
        ),
        in_specs=[smem_spec(), smem_spec(), any_spec()],
        out_specs=(any_spec(),) * (1 + len(extras)) + (smem_spec(),),
        scratch_shapes=[
            pltpu.SMEM((domains,), jnp.int32),
            pltpu.SMEM((LINE,), jnp.int32),
            pltpu.SMEM((1,), jnp.int32),
            pltpu.VMEM((owned, NBF, NBF), jnp.bfloat16),
            pltpu.VMEM((entries, META, NBF), jnp.float32),
            pltpu.VMEM((entries, META, NBF), jnp.bfloat16),
            pltpu.SemaphoreType.DMA((3 + len(extras),)),
        ],
        name="plan_blocks",
    )(dest.T, code.T, density)


def direct_kernel(places, density, out, blocks, live, load_sem, out_sem):
    copies, owned = places.shape
    domains = out.shape[0]
    load = pltpu.make_async_copy(density, blocks, load_sem)
    load.start()
    load.wait()
    live[0] = 0

    @pl.loop(0, owned)
    def _(p):
        for t in range(copies):
            entry = places[t, p] // LINE
            rows = block_rows(places[t, p] - entry * LINE)

            @pl.when(entry < domains)
            def _():
                live[0] = live[0] + 1
                pltpu.make_async_copy(blocks.at[p], out.at[entry, rows], out_sem).start()

    @pl.loop(0, live[0])
    def _(k):
        pltpu.make_async_copy(blocks.at[0], out.at[0, block_rows(0)], out_sem).wait()


def direct_blocks(places, density, domains, direct):
    return pl.pallas_call(
        direct_kernel,
        out_shape=jax.ShapeDtypeStruct((domains, direct * NBF, NBF), jnp.bfloat16),
        in_specs=[smem_spec(), any_spec()],
        out_specs=any_spec(),
        scratch_shapes=[
            pltpu.VMEM(density.shape, jnp.bfloat16),
            pltpu.SMEM((1,), jnp.int32),
            pltpu.SemaphoreType.DMA,
            pltpu.SemaphoreType.DMA,
        ],
        cost_estimate=pl.CostEstimate(flops=1000, bytes_accessed=8 << 20, transcendentals=0),
        name="direct_blocks",
    )(places, density)


def scan_kernel(direct, heads, *refs):
    extras = refs[:-9]
    starts, places, marks, lines, codes_v, codes, live, line_sem, code_sem = refs[-9:]
    sources = heads.shape[0]
    loads = [pltpu.make_async_copy(heads, lines.at[pl.ds(0, sources)], line_sem.at[0])]
    for k, ref in enumerate(extras):
        loads.append(pltpu.make_async_copy(ref.at[meta_rows(ref), :], lines.at[sources + k], line_sem.at[1 + k]))
    for load in loads:
        load.start()
    for load in loads:
        load.wait()
    head = lax.broadcasted_iota(jnp.int32, lines.shape, 1) == 0
    codes_v[...] = jnp.sum(jnp.where(head, lines[...].astype(jnp.float32), 0.0), axis=1).astype(jnp.int32)
    load = pltpu.make_async_copy(codes_v, codes, code_sem)
    load.start()
    load.wait()
    live[0] = 0

    def note(entry, rank):
        c = codes[entry, rank]

        @pl.when(c >= 0)
        def _():
            k = live[0]
            places[k] = entry * LINE + rank
            marks[k] = c
            live[0] = k + 1

    starts[0] = 0

    @pl.loop(0, sources)
    def _(source):
        for rank in range(direct):
            note(source, rank)

    starts[1] = live[0]
    for k, ref in enumerate(extras):

        @pl.loop(0, ranks_of(ref))
        def _(rank):
            note(sources + k, rank)

        starts[2 + k] = live[0]


def scan(heads, extras, direct):
    sources = heads.shape[0]
    entries = sources + len(extras)
    slots = sources * direct + sum(ranks_of(ref) for ref in extras)
    return pl.pallas_call(
        functools.partial(scan_kernel, direct),
        out_shape=(
            jax.ShapeDtypeStruct((2 + len(extras),), jnp.int32),
            jax.ShapeDtypeStruct((slots,), jnp.int32),
            jax.ShapeDtypeStruct((slots,), jnp.int32),
        ),
        in_specs=[any_spec()] * (1 + len(extras)),
        out_specs=(smem_spec(),) * 3,
        scratch_shapes=[
            pltpu.VMEM((entries, META, NBF), jnp.bfloat16),
            pltpu.VMEM((entries, NBF), jnp.int32),
            pltpu.SMEM((entries, NBF), jnp.int32),
            pltpu.SMEM((1,), jnp.int32),
            pltpu.SemaphoreType.DMA((1 + len(extras),)),
            pltpu.SemaphoreType.DMA,
        ],
        cost_estimate=pl.CostEstimate(flops=1000, bytes_accessed=8 << 20, transcendentals=0),
        name="scan",
    )(heads, *extras)


def relay_kernel(*refs):
    info, count, stage, lines, ints, codes, codes16, in_sem, sems = refs[-9:]
    hops = lines.shape[0]
    arrived = refs[:hops]
    outs = refs[hops : -10]
    places = refs[-10]
    ranks = ranks_of(outs[0])
    me = lax.axis_index("gx")
    loads = [
        pltpu.make_async_copy(ref.at[meta_rows(ref), :], lines.at[h], sems.at[h]) for h, ref in enumerate(arrived)
    ]
    for load in loads:
        load.start()
    codes[...] = jnp.full(codes.shape, -1.0, jnp.float32)
    lane, row = lane_row((META, NBF))
    for k in range(len(outs)):
        count[k] = 0
    for load in loads:
        load.wait()
    ints[...] = lines[...].astype(jnp.float32).astype(jnp.int32)
    load = pltpu.make_async_copy(ints, info, sems.at[0])
    load.start()
    load.wait()

    def fetch(h, q):
        return pltpu.make_async_copy(arrived[h].at[block_rows(q)], stage.at[h * POOL + q], in_sem.at[h * POOL + q])

    for h in range(hops):

        @pl.loop(0, POOL)
        def _(q):
            places[h, q] = -1
            c = info[h, 0, q]

            @pl.when(c >= 0)
            def _():
                fetch(h, q).start()
                near = info[h, 1, q] ^ me
                slot = jnp.minimum(count[near], ranks - 1)
                count[near] = slot + 1
                places[h, q] = near * LINE + slot
                hit = (lane == slot) & (row == 0)
                codes[near] = jnp.where(hit, c.astype(jnp.float32), codes[near])

    codes16[...] = codes[...].astype(jnp.bfloat16)
    metas = [
        pltpu.make_async_copy(codes16.at[k], ref.at[meta_rows(ref), :], sems.at[hops + k])
        for k, ref in enumerate(outs)
    ]
    for copy in metas:
        copy.start()
    last = sems.at[hops + len(outs)]
    for h in range(hops):

        @pl.loop(0, POOL)
        def _(q):
            place = places[h, q]

            @pl.when(place >= 0)
            def _():
                fetch(h, q).wait()
                near = place // LINE
                rows = block_rows(place - near * LINE)
                for k, ref in enumerate(outs):

                    @pl.when(near == k)
                    def _():
                        pltpu.make_async_copy(stage.at[h * POOL + q], ref.at[rows], last).start()

    for copy in metas:
        copy.wait()
    for h in range(hops):

        @pl.loop(0, POOL)
        def _(q):
            @pl.when(places[h, q] >= 0)
            def _():
                pltpu.make_async_copy(stage.at[0], outs[0].at[block_rows(0)], last).wait()


def relay(arrived, near_count, ranks):
    hops = len(arrived)
    return pl.pallas_call(
        relay_kernel,
        out_shape=tuple([panel(ranks)] * near_count + [jax.ShapeDtypeStruct((hops, POOL), jnp.int32)]),
        in_specs=[any_spec()] * hops,
        out_specs=tuple([any_spec()] * near_count + [smem_spec()]),
        scratch_shapes=[
            pltpu.SMEM((hops, META, NBF), jnp.int32),
            pltpu.SMEM((near_count,), jnp.int32),
            pltpu.VMEM((hops * POOL, NBF, NBF), jnp.bfloat16),
            pltpu.VMEM((hops, META, NBF), jnp.bfloat16),
            pltpu.VMEM((hops, META, NBF), jnp.int32),
            pltpu.VMEM((near_count, META, NBF), jnp.float32),
            pltpu.VMEM((near_count, META, NBF), jnp.bfloat16),
            pltpu.SemaphoreType.DMA((hops * POOL,)),
            pltpu.SemaphoreType.DMA((hops + near_count + 1,)),
        ],
        cost_estimate=pl.CostEstimate(flops=1000, bytes_accessed=4 << 20, transcendentals=0),
        name="relay",
    )(*arrived)


def relay_back_kernel(places, *refs):
    stage, in_sem, out_sem = refs[-3:]
    hops = places.shape[0]
    arrived, outs = refs[: -3 - hops], refs[-3 - hops : -3]

    def fetch(ref, rows, h, q):
        return pltpu.make_async_copy(ref.at[rows], stage.at[h * POOL + q], in_sem.at[h * POOL + q])

    def give(h, q):
        return pltpu.make_async_copy(stage.at[h * POOL + q], outs[h].at[block_rows(q)], out_sem)

    for h in range(hops):

        @pl.loop(0, POOL)
        def _(q):
            place = places[h, q]

            @pl.when(place >= 0)
            def _():
                near = place // LINE
                rows = block_rows(place - near * LINE)
                for k, ref in enumerate(arrived):

                    @pl.when(near == k)
                    def _():
                        fetch(ref, rows, h, q).start()

    for h in range(hops):

        @pl.loop(0, POOL)
        def _(q):
            @pl.when(places[h, q] >= 0)
            def _():
                fetch(arrived[0], block_rows(0), h, q).wait()
                give(h, q).start()

    for h in range(hops):

        @pl.loop(0, POOL)
        def _(q):
            @pl.when(places[h, q] >= 0)
            def _():
                give(h, q).wait()


def relay_back(places, arrived):
    hops = places.shape[0]
    return pl.pallas_call(
        relay_back_kernel,
        out_shape=tuple([panel(POOL)] * hops),
        in_specs=[smem_spec()] + [any_spec()] * len(arrived),
        out_specs=tuple([any_spec()] * hops),
        scratch_shapes=[
            pltpu.VMEM((hops * POOL, NBF, NBF), jnp.bfloat16),
            pltpu.SemaphoreType.DMA((hops * POOL,)),
            pltpu.SemaphoreType.DMA,
        ],
        cost_estimate=pl.CostEstimate(flops=1000, bytes_accessed=4 << 20, transcendentals=0),
        name="relay_back",
    )(places, *arrived)


def domain_kernel(extra_count, starts, places, marks, *refs):
    inbound, *extras = refs[: 1 + extra_count]
    basis, basis_t, base_in, w_in, w_hid1, w_hid1_t, w_hid2, w_hid2_t, w_last, weights = refs[
        1 + extra_count : 11 + extra_count
    ]
    reply, *extra_replies = refs[11 + extra_count : 12 + 2 * extra_count]
    (
        seen,
        stage,
        acc,
        dense,
        basis_v,
        basis_tv,
        rho,
        hid1,
        hid2,
        blocks,
        meta,
        w_row,
        w_out,
        in_sem,
        basis_sem,
        out_sem,
        meta_sem,
    ) = refs[12 + 2 * extra_count :]
    sources = inbound.shape[0]
    direct = ranks_of(inbound)
    points, order = basis.shape
    width = order // NBF
    pairs = width * width
    load_t = pltpu.make_async_copy(basis_t, basis_tv, basis_sem.at[0])
    load_n = pltpu.make_async_copy(basis, basis_v, basis_sem.at[1])
    live = starts[1 + extra_count]

    @pl.loop(0, starts[1])
    def _(k):
        entry = places[k] // LINE
        rows = block_rows(places[k] - entry * LINE)
        pltpu.make_async_copy(inbound.at[entry, rows], stage.at[k], in_sem.at[k]).start()

    for e, ref in enumerate(extras):

        @pl.loop(starts[1 + e], starts[2 + e])
        def _(k):
            rows = block_rows(places[k] - (sources + e) * LINE)
            pltpu.make_async_copy(ref.at[rows], stage.at[k], in_sem.at[k]).start()

    load_t.start()
    load_n.start()

    @pl.loop(0, pairs)
    def _(c):
        seen[c] = 0

    w_row[...] = jnp.broadcast_to(w_in[0:1, :], w_row.shape).T
    w_out[...] = jnp.broadcast_to(w_last[...], w_out.shape).T

    @pl.loop(0, live)
    def _(k):
        c = marks[k]
        pltpu.make_async_copy(inbound.at[0, block_rows(0)], stage.at[k], in_sem.at[k]).wait()
        value = stage[k].astype(jnp.float32)
        before = seen[c]
        seen[c] = 1

        @pl.when(before == 0)
        def _():
            acc[c] = value

        @pl.when(before != 0)
        def _():
            acc[c] = acc[c] + value

    @pl.loop(0, width)
    def _(a):
        rows = block_rows(a)
        for b in range(width):
            there = seen[a * width + b] != 0
            value = jnp.where(there, acc[a * width + b], 0.0)
            dense[rows, b * NBF : (b + 1) * NBF] = value.astype(jnp.bfloat16)

    load_t.wait()
    tile = 512

    @pl.loop(0, points // tile)
    def _(n):
        cols = pl.ds(pl.multiple_of(n * tile, tile), tile)
        part = basis_tv[:, cols]
        projected = jnp.dot(dense[...], part, preferred_element_type=jnp.float32)
        rho[:, cols] = jnp.sum(projected * part.astype(jnp.float32), axis=0, keepdims=True)

    h1 = jnp.tanh(base_in[...] + w_row[:, 0:1] * rho[...])
    hid1[...] = h1
    h2 = jnp.tanh(jnp.dot(w_hid1_t[...], h1, precision=HI, preferred_element_type=jnp.float32))
    hid2[...] = h2
    h3 = jnp.tanh(jnp.dot(w_hid2_t[...], h2, precision=HI, preferred_element_type=jnp.float32))
    logits = jnp.sum(w_out[:, 0:1] * h3, axis=0, keepdims=True)
    decay = jnp.exp(-jnp.abs(logits))
    energy_at = -(jnp.maximum(logits, 0.0) + jnp.log1p(decay))
    slope = -jnp.where(logits >= 0, 1.0, decay) / (1.0 + decay)
    g3 = (w_out[:, 0:1] * slope) * (1.0 - h3 * h3)
    h2 = hid2[...]
    g2 = jnp.dot(w_hid2[...], g3, precision=HI, preferred_element_type=jnp.float32) * (1.0 - h2 * h2)
    h1 = hid1[...]
    g1 = jnp.dot(w_hid1[...], g2, precision=HI, preferred_element_type=jnp.float32) * (1.0 - h1 * h1)
    deriv = jnp.sum(w_row[:, 0:1] * g1, axis=0, keepdims=True)
    rho[...] = weights[...] * deriv
    total = jnp.sum(weights[...] * energy_at, axis=1, keepdims=True)
    top = total.astype(jnp.bfloat16).astype(jnp.float32)
    rest = total - top
    middle = rest.astype(jnp.bfloat16).astype(jnp.float32)
    low = rest - middle
    lane = lax.broadcasted_iota(jnp.int32, (META, NBF), 1)
    line = jnp.where(lane == 0, top, jnp.where(lane == 1, middle, jnp.where(lane == 2, low, 0.0)))
    meta[...] = line.astype(jnp.bfloat16)

    @pl.loop(0, sources)
    def _(source):
        pltpu.make_async_copy(meta, reply.at[source, pl.ds(direct * NBF, META)], meta_sem).start()

    load_n.wait()

    @pl.loop(0, points // NBF)
    def _(n):
        rows = block_rows(n)
        line = jnp.broadcast_to(rho[:, rows], (NBF, NBF))
        column = line.T
        for b in range(width):
            cols = slice(b * NBF, (b + 1) * NBF)
            basis_v[rows, cols] = (column * basis_v[rows, cols].astype(jnp.float32)).astype(jnp.bfloat16)

    @pl.loop(0, width // 2)
    def _(n):
        cols = pl.ds(pl.multiple_of(n * 2 * NBF, 2 * NBF), 2 * NBF)
        result = jnp.dot(basis_tv[...], basis_v[:, cols], preferred_element_type=jnp.float32).astype(jnp.bfloat16)
        for a in range(width):
            for half in range(2):
                blocks[a * width + 2 * n + half] = result[a * NBF : (a + 1) * NBF, half * NBF : (half + 1) * NBF]

    def give(ref, rows, k):
        pltpu.make_async_copy(blocks.at[marks[k]], ref.at[rows], out_sem).start()

    for e, ref in enumerate(extra_replies):

        @pl.loop(starts[1 + e], starts[2 + e])
        def _(k):
            give(ref, block_rows(places[k] - (sources + e) * LINE), k)

    @pl.loop(0, starts[1])
    def _(k):
        entry = places[k] // LINE
        give(reply.at[entry], block_rows(places[k] - entry * LINE), k)

    @pl.loop(0, live)
    def _(k):
        pltpu.make_async_copy(blocks.at[0], reply.at[0, block_rows(0)], out_sem).wait()

    whole = reply.at[:, meta_rows(reply), :]
    pltpu.make_async_copy(whole, whole, meta_sem).wait()


def domain_build(lists, inbound, extras, basis, *fixed):
    sources = inbound.shape[0]
    direct = ranks_of(inbound)
    points, order = basis.shape
    hid = fixed[1].shape[0]
    pairs = (order // NBF) ** 2
    slots = lists[1].shape[0]
    arrays = [inbound] + list(extras)
    replies = [jax.ShapeDtypeStruct((sources, direct * NBF + META, NBF), jnp.bfloat16)]
    replies += [jax.ShapeDtypeStruct((ranks_of(ref) * NBF, NBF), jnp.bfloat16) for ref in extras]
    return pl.pallas_call(
        functools.partial(domain_kernel, len(extras)),
        out_shape=tuple(replies),
        in_specs=[smem_spec()] * 3 + [any_spec()] * (len(arrays) + 2) + [vmem_spec()] * 8,
        out_specs=(any_spec(),) * len(arrays),
        scratch_shapes=[
            pltpu.SMEM((pairs,), jnp.int32),
            pltpu.VMEM((slots, NBF, NBF), jnp.bfloat16),
            pltpu.VMEM((pairs, NBF, NBF), jnp.float32),
            pltpu.VMEM((order, order), jnp.bfloat16),
            pltpu.VMEM((points, order), jnp.bfloat16),
            pltpu.VMEM((order, points), jnp.bfloat16),
            pltpu.VMEM((1, points), jnp.float32),
            pltpu.VMEM((hid, points), jnp.float32),
            pltpu.VMEM((hid, points), jnp.float32),
            pltpu.VMEM((pairs, NBF, NBF), jnp.bfloat16),
            pltpu.VMEM((META, NBF), jnp.bfloat16),
            pltpu.VMEM((NBF, hid), jnp.float32),
            pltpu.VMEM((NBF, hid), jnp.float32),
            pltpu.SemaphoreType.DMA((slots,)),
            pltpu.SemaphoreType.DMA((2,)),
            pltpu.SemaphoreType.DMA,
            pltpu.SemaphoreType.DMA,
        ],
        compiler_params=pltpu.CompilerParams(vmem_limit_bytes=60 << 20),
        name="domain_build",
    )(*lists, *arrays, basis, *fixed)


def collect_kernel(scale, places, returned, *refs):
    extras = refs[:-8]
    fock, energy, parts, result, meta, in_sem, out_sem, meta_sem = refs[-8:]
    copies, owned = places.shape
    sources = returned.shape[0]
    meta_in = pltpu.make_async_copy(returned.at[:, meta_rows(returned), :], meta, meta_sem)
    meta_in.start()

    @pl.loop(0, owned)
    def _(p):
        for t in range(copies):
            entry = places[t, p] // LINE
            rows = block_rows(places[t, p] - entry * LINE)

            @pl.when(entry < sources)
            def _():
                pltpu.make_async_copy(returned.at[entry, rows], parts.at[p, t], in_sem.at[p]).start()

            if extras:

                @pl.when(entry >= sources)
                def _():
                    for k, ref in enumerate(extras):

                        @pl.when(entry == sources + k)
                        def _():
                            pltpu.make_async_copy(ref.at[rows], parts.at[p, t], in_sem.at[p]).start()

    meta_in.wait()
    lane = lax.broadcasted_iota(jnp.int32, meta.shape, 2)
    row = lax.broadcasted_iota(jnp.int32, meta.shape, 1)
    sent = jnp.where((lane < 3) & (row == 0), meta[...].astype(jnp.float32), 0.0)
    per_source = jnp.sum(jnp.sum(sent, axis=0), axis=0, keepdims=True)
    energy[...] = jnp.sum(per_source, axis=1, keepdims=True) * scale
    last = (sources + len(extras)) * LINE

    @pl.loop(0, owned)
    def _(p):
        total = jnp.zeros((NBF, NBF), jnp.float32)
        for t in range(copies):
            here = places[t, p] < last

            @pl.when(here)
            def _():
                pltpu.make_async_copy(parts.at[p, t], parts.at[p, t], in_sem.at[p]).wait()

            total = total + jnp.where(here, parts[p, t].astype(jnp.float32), 0.0)
        result[p] = total
        pltpu.make_async_copy(result.at[p], fock.at[p], out_sem).start()

    pltpu.make_async_copy(result, fock, out_sem).wait()


def collect_blocks(places, returned, extras, scale):
    copies, owned = places.shape
    sources = returned.shape[0]
    return pl.pallas_call(
        functools.partial(collect_kernel, scale),
        out_shape=(
            jax.ShapeDtypeStruct((owned, NBF, NBF), jnp.float32),
            jax.ShapeDtypeStruct((1, 1), jnp.float32),
        ),
        in_specs=[smem_spec()] + [any_spec()] * (1 + len(extras)),
        out_specs=(any_spec(), vmem_spec()),
        scratch_shapes=[
            pltpu.VMEM((owned, copies, NBF, NBF), jnp.bfloat16),
            pltpu.VMEM((owned, NBF, NBF), jnp.float32),
            pltpu.VMEM((sources, META, NBF), jnp.bfloat16),
            pltpu.SemaphoreType.DMA((owned,)),
            pltpu.SemaphoreType.DMA,
            pltpu.SemaphoreType.DMA,
        ],
        cost_estimate=pl.CostEstimate(flops=1000, bytes_accessed=8 << 20, transcendentals=0),
        name="collect_blocks",
    )(places, returned, *extras)


def add_kernel(first, places, partial, *refs):
    extras = refs[:-8]
    fock, parts, result, listed, live, in_sem, fock_sem, out_sem = refs[-8:]
    copies, owned = places.shape
    live[0] = 0

    @pl.loop(0, owned)
    def _(p):
        hits = [places[t, p] >= first * LINE for t in range(copies)]

        @pl.when(functools.reduce(jnp.logical_or, hits))
        def _():
            k = live[0]
            listed[k] = p
            live[0] = k + 1
            pltpu.make_async_copy(partial.at[p], result.at[k], fock_sem.at[k]).start()
            for t in range(copies):
                entry = places[t, p] // LINE
                rows = block_rows(places[t, p] - entry * LINE)
                for e, ref in enumerate(extras):

                    @pl.when(entry == first + e)
                    def _():
                        pltpu.make_async_copy(ref.at[rows], parts.at[k, t], in_sem.at[k]).start()

    @pl.loop(0, live[0])
    def _(k):
        p = listed[k]
        pltpu.make_async_copy(partial.at[p], result.at[k], fock_sem.at[k]).wait()
        total = result[k]
        for t in range(copies):
            here = places[t, p] >= first * LINE

            @pl.when(here)
            def _():
                pltpu.make_async_copy(parts.at[k, t], parts.at[k, t], in_sem.at[k]).wait()

            total = total + jnp.where(here, parts[k, t].astype(jnp.float32), 0.0)
        result[k] = total
        pltpu.make_async_copy(result.at[k], fock.at[p], out_sem).start()

    @pl.loop(0, live[0])
    def _(k):
        pltpu.make_async_copy(result.at[0], fock.at[0], out_sem).wait()


def add_blocks(places, partial, extras, first):
    copies, owned = places.shape
    return pl.pallas_call(
        functools.partial(add_kernel, first),
        out_shape=jax.ShapeDtypeStruct(partial.shape, partial.dtype),
        in_specs=[smem_spec()] + [any_spec()] * (1 + len(extras)),
        out_specs=any_spec(),
        input_output_aliases={1: 0},
        scratch_shapes=[
            pltpu.VMEM((owned, copies, NBF, NBF), jnp.bfloat16),
            pltpu.VMEM((owned, NBF, NBF), jnp.float32),
            pltpu.SMEM((owned,), jnp.int32),
            pltpu.SMEM((1,), jnp.int32),
            pltpu.SemaphoreType.DMA((owned,)),
            pltpu.SemaphoreType.DMA((owned,)),
            pltpu.SemaphoreType.DMA,
        ],
        name="add_blocks",
    )(places, partial, *extras)


def exchange(array):
    return lax.all_to_all(array, AXES, split_axis=0, concat_axis=0, tiled=True)


def swap(arrays, axis, first):
    size = lax.axis_size(axis)
    return [
        lax.ppermute(array, axis, [(i, i ^ (first + k)) for i in range(size)]) if first + k else array
        for k, array in enumerate(arrays)
    ]


def body(density, dest, code, basis, descriptors, weights, w_in, w_hid1, w_hid2, w_out):
    rows_x, rows_z = lax.axis_size("gx"), lax.axis_size("gy")
    domains = rows_x * rows_z
    owned = density.shape[0]
    copies = dest.shape[1]
    capacity = max(2, 2 * copies * owned // domains)
    points = basis.shape[0]
    scale = 1.0 / (math.sqrt(points) * domains)
    basis_t = basis.T
    base_in = jnp.dot(w_in[1:].T, descriptors, precision=HI)
    fixed = (
        basis, basis_t, base_in, w_in, w_hid1, w_hid1.T, w_hid2, w_hid2.T, w_out[None, :], weights[None, :]
    )

    def plain():
        heads, places = plan_blocks(density, dest, code, domains, capacity, None)
        lists = scan(exchange(heads), [], capacity)
        inbound = exchange(direct_blocks(places, density, domains, capacity))
        (replies,) = domain_build(lists, inbound, [], *fixed)
        fock, energy = collect_blocks(places, exchange(replies), [], scale)
        return fock, energy[0, 0]

    if capacity < 8:
        return plain()
    direct = capacity // 2
    ranks = (rows_z - 1) * (capacity - direct)
    heads, *extras, places = plan_blocks(density, dest, code, domains, direct, (rows_x, rows_z))
    lines_in = swap(extras[rows_x:], "gy", 1)
    near_in = swap(extras[:rows_x], "gx", 0)
    heads_in = exchange(heads)
    outgoing = direct_blocks(places, density, domains, direct)
    outgoing, lines_in, near_in, heads_in = lax.optimization_barrier((outgoing, lines_in, near_in, heads_in))
    inbound = exchange(outgoing)
    *relayed, relay_places = relay(lines_in, rows_x, ranks)
    relayed_in = swap(relayed, "gx", 0)
    lists = scan(heads_in, near_in + relayed_in, direct)
    raised = jnp.max(heads_in[:, 0, FLAG].astype(jnp.float32)) > 0

    def split():
        replies, *others = domain_build(lists, inbound, near_in + relayed_in, *fixed)
        relayed_back = swap(others[rows_x:], "gx", 0)
        near_back = swap(others[:rows_x], "gx", 0)
        returned = exchange(replies)
        lines_back = swap(relay_back(relay_places, relayed_back), "gy", 1)
        fock, energy = collect_blocks(places, returned, near_back, scale)
        return add_blocks(places, fock, lines_back, domains + rows_x), energy[0, 0]

    return lax.cond(raised, plain, split)


def solution(mesh):
    placed = (
        P(AXES, None, None),
        P(AXES, None),
        P(AXES, None),
        P(AXES, None),
        P(None, AXES),
        P(AXES),
        P(),
        P(),
        P(),
        P(),
    )
    return jax.shard_map(
        body,
        mesh=mesh,
        in_specs=placed,
        out_specs=(P(AXES, None, None), P()),
        check_vma=False,
    )
```

```python
import functools
import math

import jax
import jax.numpy as jnp
from jax import lax
from jax.experimental import pallas as pl
from jax.experimental.pallas import tpu as pltpu
from jax.sharding import PartitionSpec as P


NBF = 128
META = 8
LINE = 32
POOL = 16
AXES = ("gx", "gy")
HI = lax.Precision.HIGHEST


def any_spec():
    return pl.BlockSpec(memory_space=pl.ANY)


def smem_spec():
    return pl.BlockSpec(memory_space=pltpu.SMEM)


def vmem_spec():
    return pl.BlockSpec(memory_space=pltpu.VMEM)


def block_rows(rank):
    return pl.ds(pl.multiple_of(rank * NBF, NBF), NBF)


def panel(ranks):
    return jax.ShapeDtypeStruct((ranks * NBF + META, NBF), jnp.bfloat16)


def ranks_of(array):
    return array.shape[-2] // NBF


def meta_rows(array):
    return pl.ds(ranks_of(array) * NBF, META)


def lane_row(shape):
    lane = lax.broadcasted_iota(jnp.int32, shape, len(shape) - 1)
    row = lax.broadcasted_iota(jnp.int32, shape, len(shape) - 2)
    return lane, row


def plan_kernel(dest, code, heads, places, count, codes, codes16, sem):
    copies, owned = dest.shape
    domains = heads.shape[0]

    @pl.loop(0, domains)
    def _(d):
        count[d] = 0

    codes[...] = jnp.full(codes.shape, -1.0, jnp.float32)
    lane, row = lane_row((META, NBF))

    @pl.loop(0, owned)
    def _(p):
        for t in range(copies):
            d = dest[t, p]
            rank = count[d]
            count[d] = rank + 1
            places[t, p] = d * LINE + rank
            value = code[t, p].astype(jnp.float32)
            codes[d] = jnp.where((lane == rank) & (row == 0), value, codes[d])

    codes16[...] = codes[...].astype(jnp.bfloat16)
    copy = pltpu.make_async_copy(codes16, heads, sem)
    copy.start()
    copy.wait()


def plan_blocks(dest, code, domains):
    owned, copies = dest.shape
    return pl.pallas_call(
        plan_kernel,
        out_shape=(
            jax.ShapeDtypeStruct((domains, META, NBF), jnp.bfloat16),
            jax.ShapeDtypeStruct((copies, owned), jnp.int32),
        ),
        in_specs=[smem_spec(), smem_spec()],
        out_specs=(any_spec(), smem_spec()),
        scratch_shapes=[
            pltpu.SMEM((domains,), jnp.int32),
            pltpu.VMEM((domains, META, NBF), jnp.float32),
            pltpu.VMEM((domains, META, NBF), jnp.bfloat16),
            pltpu.SemaphoreType.DMA,
        ],
        name="plan_blocks",
    )(dest.T, code.T)


def split_kernel(direct, groups, dest, code, density, *refs):
    copies, owned = dest.shape
    rows_x, rows_z = groups
    domains = rows_x * rows_z
    shift = rows_z.bit_length() - 1
    *panels, places = refs[:-7]
    count, pool, table, blocks, ints, codes16, sems = refs[-7:]
    load = pltpu.make_async_copy(density, blocks, sems.at[0])
    load.start()
    ints[...] = jnp.full(ints.shape, -1, jnp.int32)
    fill = pltpu.make_async_copy(ints, table, sems.at[1])
    fill.start()

    @pl.loop(0, domains)
    def _(d):
        count[d] = 0

    for k in range(rows_z + 2):
        pool[k] = 0
    live, over = rows_z, rows_z + 1
    me_x, me_z = lax.axis_index("gx"), lax.axis_index("gy")
    fill.wait()
    load.wait()

    @pl.loop(0, owned)
    def _(p):
        for t in range(copies):
            d = dest[t, p]
            value = code[t, p]
            rank = count[d]
            count[d] = rank + 1
            target = d >> shift
            near = target ^ me_x
            far = (d & (rows_z - 1)) ^ me_z
            places[t, p] = d * LINE + rank

            @pl.when((rank < direct) & (far == 0))
            def _():
                table[near, 1, rank] = value

            @pl.when((rank < direct) & (far != 0))
            def _():
                table[rows_x + far - 1, 2, target * direct + rank] = value

            @pl.when((rank >= direct) & (far == 0))
            def _():
                slot = rank - direct
                table[near, 0, slot] = value
                places[t, p] = (domains + near) * LINE + slot
                pool[live] = pool[live] + 1
                for k in range(rows_x):

                    @pl.when(near == k)
                    def _():
                        pltpu.make_async_copy(blocks.at[p], panels[k].at[block_rows(slot)], sems.at[2]).start()

            @pl.when((rank >= direct) & (far != 0))
            def _():
                taken = pool[far]
                pool[far] = taken + 1
                pool[over] = pool[over] | (taken >= POOL).astype(jnp.int32)
                slot = jnp.minimum(taken, POOL - 1)
                table[rows_x + far - 1, 0, slot] = value
                table[rows_x + far - 1, 1, slot] = target
                places[t, p] = (domains + rows_x + far - 1) * LINE + slot
                pool[live] = pool[live] + 1
                for k in range(1, rows_z):

                    @pl.when(far == k)
                    def _():
                        ref = panels[rows_x + k - 1]
                        pltpu.make_async_copy(blocks.at[p], ref.at[block_rows(slot)], sems.at[2]).start()

    for k in range(len(panels)):
        table[k, 3, 0] = pool[over]
    back = pltpu.make_async_copy(table, ints, sems.at[1])
    back.start()
    back.wait()
    codes16[...] = ints[...].astype(jnp.float32).astype(jnp.bfloat16)
    metas = [
        pltpu.make_async_copy(codes16.at[k], ref.at[meta_rows(ref), :], sems.at[3 + k]) for k, ref in enumerate(panels)
    ]
    for copy in metas:
        copy.start()

    @pl.loop(0, pool[live])
    def _(k):
        pltpu.make_async_copy(blocks.at[0], panels[0].at[block_rows(0)], sems.at[2]).wait()

    for copy in metas:
        copy.wait()


def split_blocks(density, dest, code, direct, groups):
    owned, copies = dest.shape
    panels = [panel(direct)] * groups[0] + [panel(POOL)] * (groups[1] - 1)
    return pl.pallas_call(
        functools.partial(split_kernel, direct, groups),
        out_shape=(*panels, jax.ShapeDtypeStruct((copies, owned), jnp.int32)),
        in_specs=[smem_spec(), smem_spec(), any_spec()],
        out_specs=(any_spec(),) * len(panels) + (smem_spec(),),
        scratch_shapes=[
            pltpu.SMEM((groups[0] * groups[1],), jnp.int32),
            pltpu.SMEM((LINE,), jnp.int32),
            pltpu.SMEM((len(panels), META, NBF), jnp.int32),
            pltpu.VMEM((owned, NBF, NBF), jnp.bfloat16),
            pltpu.VMEM((len(panels), META, NBF), jnp.int32),
            pltpu.VMEM((len(panels), META, NBF), jnp.bfloat16),
            pltpu.SemaphoreType.DMA((3 + len(panels),)),
        ],
        name="split_blocks",
    )(dest.T, code.T, density)


def direct_kernel(places, density, out, blocks, live, load_sem, out_sem):
    copies, owned = places.shape
    domains = out.shape[0]
    load = pltpu.make_async_copy(density, blocks, load_sem)
    load.start()
    load.wait()
    live[0] = 0

    @pl.loop(0, owned)
    def _(p):
        for t in range(copies):
            entry = places[t, p] // LINE
            rows = block_rows(places[t, p] - entry * LINE)

            @pl.when(entry < domains)
            def _():
                live[0] = live[0] + 1
                pltpu.make_async_copy(blocks.at[p], out.at[entry, rows], out_sem).start()

    @pl.loop(0, live[0])
    def _(k):
        pltpu.make_async_copy(blocks.at[0], out.at[0, block_rows(0)], out_sem).wait()


def direct_blocks(places, density, domains, direct):
    return pl.pallas_call(
        direct_kernel,
        out_shape=jax.ShapeDtypeStruct((domains, direct * NBF, NBF), jnp.bfloat16),
        in_specs=[smem_spec(), any_spec()],
        out_specs=any_spec(),
        scratch_shapes=[
            pltpu.VMEM(density.shape, jnp.bfloat16),
            pltpu.SMEM((1,), jnp.int32),
            pltpu.SemaphoreType.DMA,
            pltpu.SemaphoreType.DMA,
        ],
        cost_estimate=pl.CostEstimate(flops=1000, bytes_accessed=8 << 20, transcendentals=0),
        name="direct_blocks",
    )(places, density)


def scan_kernel(direct, heads, *refs):
    extras = refs[:-9]
    starts, places, marks, lines, codes_v, codes, live, line_sem, code_sem = refs[-9:]
    sources = heads.shape[0]
    loads = [pltpu.make_async_copy(heads, lines.at[pl.ds(0, sources)], line_sem.at[0])]
    for k, ref in enumerate(extras):
        loads.append(pltpu.make_async_copy(ref.at[meta_rows(ref), :], lines.at[sources + k], line_sem.at[1 + k]))
    for load in loads:
        load.start()
    for load in loads:
        load.wait()
    head = lax.broadcasted_iota(jnp.int32, lines.shape, 1) == 0
    codes_v[...] = jnp.sum(jnp.where(head, lines[...].astype(jnp.float32), 0.0), axis=1).astype(jnp.int32)
    load = pltpu.make_async_copy(codes_v, codes, code_sem)
    load.start()
    load.wait()
    live[0] = 0

    def note(entry, rank):
        c = codes[entry, rank]

        @pl.when(c >= 0)
        def _():
            k = live[0]
            places[k] = entry * LINE + rank
            marks[k] = c
            live[0] = k + 1

    starts[0] = 0

    @pl.loop(0, sources)
    def _(source):
        for rank in range(direct):
            note(source, rank)

    starts[1] = live[0]
    for k, ref in enumerate(extras):

        @pl.loop(0, ranks_of(ref))
        def _(rank):
            note(sources + k, rank)

        starts[2 + k] = live[0]


def scan(heads, extras, direct):
    sources = heads.shape[0]
    entries = sources + len(extras)
    slots = sources * direct + sum(ranks_of(ref) for ref in extras)
    return pl.pallas_call(
        functools.partial(scan_kernel, direct),
        out_shape=(
            jax.ShapeDtypeStruct((2 + len(extras),), jnp.int32),
            jax.ShapeDtypeStruct((slots,), jnp.int32),
            jax.ShapeDtypeStruct((slots,), jnp.int32),
        ),
        in_specs=[any_spec()] * (1 + len(extras)),
        out_specs=(smem_spec(),) * 3,
        scratch_shapes=[
            pltpu.VMEM((entries, META, NBF), jnp.bfloat16),
            pltpu.VMEM((entries, NBF), jnp.int32),
            pltpu.SMEM((entries, NBF), jnp.int32),
            pltpu.SMEM((1,), jnp.int32),
            pltpu.SemaphoreType.DMA((1 + len(extras),)),
            pltpu.SemaphoreType.DMA,
        ],
        cost_estimate=pl.CostEstimate(flops=1000, bytes_accessed=8 << 20, transcendentals=0),
        name="scan",
    )(heads, *extras)


def merge_kernel(direct, groups, *refs):
    rows_x, rows_z = groups
    panels = refs[:-9]
    starts, places, marks, raised, lines, ints, info, live, sems = refs[-9:]
    loads = [pltpu.make_async_copy(ref.at[meta_rows(ref), :], lines.at[k], sems.at[k]) for k, ref in enumerate(panels)]
    for load in loads:
        load.start()
    for load in loads:
        load.wait()
    ints[...] = lines[...].astype(jnp.float32).astype(jnp.int32)
    load = pltpu.make_async_copy(ints, info, sems.at[0])
    load.start()
    load.wait()
    me_x, me_z = lax.axis_index("gx"), lax.axis_index("gy")
    live[0] = 0
    raised[0] = 0
    starts[0] = 0

    def note(entry, rank, c):
        @pl.when(c >= 0)
        def _():
            k = live[0]
            places[k] = entry * LINE + rank
            marks[k] = c
            live[0] = k + 1

    @pl.loop(0, rows_x)
    def _(k):
        first = (k ^ me_x) * rows_z
        raised[0] = raised[0] | info[k, 3, 0] | info[rows_x + k, 3, 0]
        for rank in range(direct):
            note(first + me_z, rank, info[k, 1, rank])
            for h in range(rows_z - 1):
                note(first + (me_z ^ (h + 1)), rank, info[rows_x + k, 1, h * direct + rank])

    starts[1] = live[0]
    domains = rows_x * rows_z
    for k, ref in enumerate(panels):

        @pl.loop(0, ranks_of(ref))
        def _(rank):
            note(domains + k, rank, info[k, 0, rank])

        starts[2 + k] = live[0]


def merge(panels, direct, groups):
    slots = groups[0] * groups[1] * direct + sum(ranks_of(ref) for ref in panels)
    return pl.pallas_call(
        functools.partial(merge_kernel, direct, groups),
        out_shape=(
            jax.ShapeDtypeStruct((2 + len(panels),), jnp.int32),
            jax.ShapeDtypeStruct((slots,), jnp.int32),
            jax.ShapeDtypeStruct((slots,), jnp.int32),
            jax.ShapeDtypeStruct((1,), jnp.int32),
        ),
        in_specs=[any_spec()] * len(panels),
        out_specs=(smem_spec(),) * 4,
        scratch_shapes=[
            pltpu.VMEM((len(panels), META, NBF), jnp.bfloat16),
            pltpu.VMEM((len(panels), META, NBF), jnp.int32),
            pltpu.SMEM((len(panels), META, NBF), jnp.int32),
            pltpu.SMEM((1,), jnp.int32),
            pltpu.SemaphoreType.DMA((len(panels),)),
        ],
        cost_estimate=pl.CostEstimate(flops=1000, bytes_accessed=8 << 20, transcendentals=0),
        name="merge",
    )(*panels)


def relay_kernel(direct, *refs):
    info, count, table, stage, lines, ints, cells, codes16, in_sem, sems = refs[-10:]
    hops = lines.shape[0]
    arrived = refs[:hops]
    outs = refs[hops:-11]
    places = refs[-11]
    ranks = ranks_of(outs[0])
    me = lax.axis_index("gx")
    loads = [
        pltpu.make_async_copy(ref.at[meta_rows(ref), :], lines.at[h], sems.at[h]) for h, ref in enumerate(arrived)
    ]
    for load in loads:
        load.start()
    last = sems.at[hops + len(outs)]
    cells[...] = jnp.full(cells.shape, -1, jnp.int32)
    fill = pltpu.make_async_copy(cells, table, last)
    fill.start()
    for k in range(len(outs)):
        count[k] = 0
    for load in loads:
        load.wait()
    ints[...] = lines[...].astype(jnp.float32).astype(jnp.int32)
    load = pltpu.make_async_copy(ints, info, sems.at[0])
    load.start()
    load.wait()
    fill.wait()

    def fetch(h, q):
        return pltpu.make_async_copy(arrived[h].at[block_rows(q)], stage.at[h * POOL + q], in_sem.at[h * POOL + q])

    for h in range(hops):

        @pl.loop(0, POOL)
        def _(q):
            places[h, q] = -1
            c = info[h, 0, q]

            @pl.when(c >= 0)
            def _():
                fetch(h, q).start()
                near = info[h, 1, q] ^ me
                slot = jnp.minimum(count[near], ranks - 1)
                count[near] = slot + 1
                places[h, q] = near * LINE + slot
                table[near, 0, slot] = c

    raised = functools.reduce(jnp.bitwise_or, [info[h, 3, 0] for h in range(hops)])

    @pl.loop(0, len(outs))
    def _(k):
        table[k, 3, 0] = raised
        for h in range(hops):
            for rank in range(direct):
                table[k, 1, h * direct + rank] = info[h, 2, (k ^ me) * direct + rank]

    back = pltpu.make_async_copy(table, cells, last)
    back.start()
    back.wait()
    codes16[...] = cells[...].astype(jnp.float32).astype(jnp.bfloat16)
    metas = [
        pltpu.make_async_copy(codes16.at[k], ref.at[meta_rows(ref), :], sems.at[hops + k])
        for k, ref in enumerate(outs)
    ]
    for copy in metas:
        copy.start()
    for h in range(hops):

        @pl.loop(0, POOL)
        def _(q):
            place = places[h, q]

            @pl.when(place >= 0)
            def _():
                fetch(h, q).wait()
                near = place // LINE
                rows = block_rows(place - near * LINE)
                for k, ref in enumerate(outs):

                    @pl.when(near == k)
                    def _():
                        pltpu.make_async_copy(stage.at[h * POOL + q], ref.at[rows], last).start()

    for copy in metas:
        copy.wait()
    for h in range(hops):

        @pl.loop(0, POOL)
        def _(q):
            @pl.when(places[h, q] >= 0)
            def _():
                pltpu.make_async_copy(stage.at[0], outs[0].at[block_rows(0)], last).wait()


def relay(arrived, near_count, ranks, direct):
    hops = len(arrived)
    return pl.pallas_call(
        functools.partial(relay_kernel, direct),
        out_shape=tuple([panel(ranks)] * near_count + [jax.ShapeDtypeStruct((hops, POOL), jnp.int32)]),
        in_specs=[any_spec()] * hops,
        out_specs=tuple([any_spec()] * near_count + [smem_spec()]),
        scratch_shapes=[
            pltpu.SMEM((hops, META, NBF), jnp.int32),
            pltpu.SMEM((near_count,), jnp.int32),
            pltpu.SMEM((near_count, META, NBF), jnp.int32),
            pltpu.VMEM((hops * POOL, NBF, NBF), jnp.bfloat16),
            pltpu.VMEM((hops, META, NBF), jnp.bfloat16),
            pltpu.VMEM((hops, META, NBF), jnp.int32),
            pltpu.VMEM((near_count, META, NBF), jnp.int32),
            pltpu.VMEM((near_count, META, NBF), jnp.bfloat16),
            pltpu.SemaphoreType.DMA((hops * POOL,)),
            pltpu.SemaphoreType.DMA((hops + near_count + 1,)),
        ],
        cost_estimate=pl.CostEstimate(flops=1000, bytes_accessed=4 << 20, transcendentals=0),
        name="relay",
    )(*arrived)


def relay_back_kernel(places, *refs):
    stage, in_sem, out_sem = refs[-3:]
    hops = places.shape[0]
    arrived, outs = refs[: -3 - hops], refs[-3 - hops : -3]

    def fetch(ref, rows, h, q):
        return pltpu.make_async_copy(ref.at[rows], stage.at[h * POOL + q], in_sem.at[h * POOL + q])

    def give(h, q):
        return pltpu.make_async_copy(stage.at[h * POOL + q], outs[h].at[block_rows(q)], out_sem)

    for h in range(hops):

        @pl.loop(0, POOL)
        def _(q):
            place = places[h, q]

            @pl.when(place >= 0)
            def _():
                near = place // LINE
                rows = block_rows(place - near * LINE)
                for k, ref in enumerate(arrived):

                    @pl.when(near == k)
                    def _():
                        fetch(ref, rows, h, q).start()

    for h in range(hops):

        @pl.loop(0, POOL)
        def _(q):
            @pl.when(places[h, q] >= 0)
            def _():
                fetch(arrived[0], block_rows(0), h, q).wait()
                give(h, q).start()

    for h in range(hops):

        @pl.loop(0, POOL)
        def _(q):
            @pl.when(places[h, q] >= 0)
            def _():
                give(h, q).wait()


def relay_back(places, arrived):
    hops = places.shape[0]
    return pl.pallas_call(
        relay_back_kernel,
        out_shape=tuple([panel(POOL)] * hops),
        in_specs=[smem_spec()] + [any_spec()] * len(arrived),
        out_specs=tuple([any_spec()] * hops),
        scratch_shapes=[
            pltpu.VMEM((hops * POOL, NBF, NBF), jnp.bfloat16),
            pltpu.SemaphoreType.DMA((hops * POOL,)),
            pltpu.SemaphoreType.DMA,
        ],
        cost_estimate=pl.CostEstimate(flops=1000, bytes_accessed=4 << 20, transcendentals=0),
        name="relay_back",
    )(places, *arrived)


def domain_kernel(extra_count, starts, places, marks, *refs):
    inbound, *extras = refs[: 1 + extra_count]
    basis, basis_t, base_in, w_in, w_hid1, w_hid1_t, w_hid2, w_hid2_t, w_last, weights = refs[
        1 + extra_count : 11 + extra_count
    ]
    reply, *extra_replies = refs[11 + extra_count : 12 + 2 * extra_count]
    (
        seen,
        stage,
        acc,
        dense,
        basis_v,
        basis_tv,
        rho,
        hid1,
        hid2,
        blocks,
        meta,
        w_row,
        w_out,
        in_sem,
        basis_sem,
        out_sem,
        meta_sem,
    ) = refs[12 + 2 * extra_count :]
    sources = inbound.shape[0]
    direct = ranks_of(inbound)
    points, order = basis.shape
    width = order // NBF
    pairs = width * width
    load_t = pltpu.make_async_copy(basis_t, basis_tv, basis_sem.at[0])
    load_n = pltpu.make_async_copy(basis, basis_v, basis_sem.at[1])
    live = starts[1 + extra_count]

    @pl.loop(0, starts[1])
    def _(k):
        entry = places[k] // LINE
        rows = block_rows(places[k] - entry * LINE)
        pltpu.make_async_copy(inbound.at[entry, rows], stage.at[k], in_sem.at[k]).start()

    for e, ref in enumerate(extras):

        @pl.loop(starts[1 + e], starts[2 + e])
        def _(k):
            rows = block_rows(places[k] - (sources + e) * LINE)
            pltpu.make_async_copy(ref.at[rows], stage.at[k], in_sem.at[k]).start()

    load_t.start()
    load_n.start()

    @pl.loop(0, pairs)
    def _(c):
        seen[c] = 0

    w_row[...] = jnp.broadcast_to(w_in[0:1, :], w_row.shape).T
    w_out[...] = jnp.broadcast_to(w_last[...], w_out.shape).T

    @pl.loop(0, live)
    def _(k):
        c = marks[k]
        pltpu.make_async_copy(inbound.at[0, block_rows(0)], stage.at[k], in_sem.at[k]).wait()
        value = stage[k].astype(jnp.float32)
        before = seen[c]
        seen[c] = 1

        @pl.when(before == 0)
        def _():
            acc[c] = value

        @pl.when(before != 0)
        def _():
            acc[c] = acc[c] + value

    @pl.loop(0, width)
    def _(a):
        rows = block_rows(a)
        for b in range(width):
            there = seen[a * width + b] != 0
            value = jnp.where(there, acc[a * width + b], 0.0)
            dense[rows, b * NBF : (b + 1) * NBF] = value.astype(jnp.bfloat16)

    load_t.wait()
    tile = 512

    @pl.loop(0, points // tile)
    def _(n):
        cols = pl.ds(pl.multiple_of(n * tile, tile), tile)
        part = basis_tv[:, cols]
        projected = jnp.dot(dense[...], part, preferred_element_type=jnp.float32)
        rho[:, cols] = jnp.sum(projected * part.astype(jnp.float32), axis=0, keepdims=True)

    h1 = jnp.tanh(base_in[...] + w_row[:, 0:1] * rho[...])
    hid1[...] = h1
    h2 = jnp.tanh(jnp.dot(w_hid1_t[...], h1, precision=HI, preferred_element_type=jnp.float32))
    hid2[...] = h2
    h3 = jnp.tanh(jnp.dot(w_hid2_t[...], h2, precision=HI, preferred_element_type=jnp.float32))
    logits = jnp.sum(w_out[:, 0:1] * h3, axis=0, keepdims=True)
    decay = jnp.exp(-jnp.abs(logits))
    energy_at = -(jnp.maximum(logits, 0.0) + jnp.log1p(decay))
    slope = -jnp.where(logits >= 0, 1.0, decay) / (1.0 + decay)
    g3 = (w_out[:, 0:1] * slope) * (1.0 - h3 * h3)
    h2 = hid2[...]
    g2 = jnp.dot(w_hid2[...], g3, precision=HI, preferred_element_type=jnp.float32) * (1.0 - h2 * h2)
    h1 = hid1[...]
    g1 = jnp.dot(w_hid1[...], g2, precision=HI, preferred_element_type=jnp.float32) * (1.0 - h1 * h1)
    deriv = jnp.sum(w_row[:, 0:1] * g1, axis=0, keepdims=True)
    rho[...] = weights[...] * deriv
    total = jnp.sum(weights[...] * energy_at, axis=1, keepdims=True)
    top = total.astype(jnp.bfloat16).astype(jnp.float32)
    rest = total - top
    middle = rest.astype(jnp.bfloat16).astype(jnp.float32)
    low = rest - middle
    lane = lax.broadcasted_iota(jnp.int32, (META, NBF), 1)
    line = jnp.where(lane == 0, top, jnp.where(lane == 1, middle, jnp.where(lane == 2, low, 0.0)))
    meta[...] = line.astype(jnp.bfloat16)

    @pl.loop(0, sources)
    def _(source):
        pltpu.make_async_copy(meta, reply.at[source, pl.ds(direct * NBF, META)], meta_sem).start()

    load_n.wait()

    @pl.loop(0, points // NBF)
    def _(n):
        rows = block_rows(n)
        line = jnp.broadcast_to(rho[:, rows], (NBF, NBF))
        column = line.T
        for b in range(width):
            cols = slice(b * NBF, (b + 1) * NBF)
            basis_v[rows, cols] = (column * basis_v[rows, cols].astype(jnp.float32)).astype(jnp.bfloat16)

    @pl.loop(0, width // 2)
    def _(n):
        cols = pl.ds(pl.multiple_of(n * 2 * NBF, 2 * NBF), 2 * NBF)
        result = jnp.dot(basis_tv[...], basis_v[:, cols], preferred_element_type=jnp.float32).astype(jnp.bfloat16)
        for a in range(width):
            for half in range(2):
                blocks[a * width + 2 * n + half] = result[a * NBF : (a + 1) * NBF, half * NBF : (half + 1) * NBF]

    def give(ref, rows, k):
        pltpu.make_async_copy(blocks.at[marks[k]], ref.at[rows], out_sem).start()

    for e, ref in enumerate(extra_replies):

        @pl.loop(starts[1 + e], starts[2 + e])
        def _(k):
            give(ref, block_rows(places[k] - (sources + e) * LINE), k)

    @pl.loop(0, starts[1])
    def _(k):
        entry = places[k] // LINE
        give(reply.at[entry], block_rows(places[k] - entry * LINE), k)

    @pl.loop(0, live)
    def _(k):
        pltpu.make_async_copy(blocks.at[0], reply.at[0, block_rows(0)], out_sem).wait()

    whole = reply.at[:, meta_rows(reply), :]
    pltpu.make_async_copy(whole, whole, meta_sem).wait()


def domain_build(lists, inbound, extras, basis, *fixed):
    sources = inbound.shape[0]
    direct = ranks_of(inbound)
    points, order = basis.shape
    hid = fixed[1].shape[0]
    pairs = (order // NBF) ** 2
    slots = lists[1].shape[0]
    arrays = [inbound] + list(extras)
    replies = [jax.ShapeDtypeStruct((sources, direct * NBF + META, NBF), jnp.bfloat16)]
    replies += [jax.ShapeDtypeStruct((ranks_of(ref) * NBF, NBF), jnp.bfloat16) for ref in extras]
    return pl.pallas_call(
        functools.partial(domain_kernel, len(extras)),
        out_shape=tuple(replies),
        in_specs=[smem_spec()] * 3 + [any_spec()] * (len(arrays) + 2) + [vmem_spec()] * 8,
        out_specs=(any_spec(),) * len(arrays),
        scratch_shapes=[
            pltpu.SMEM((pairs,), jnp.int32),
            pltpu.VMEM((slots, NBF, NBF), jnp.bfloat16),
            pltpu.VMEM((pairs, NBF, NBF), jnp.float32),
            pltpu.VMEM((order, order), jnp.bfloat16),
            pltpu.VMEM((points, order), jnp.bfloat16),
            pltpu.VMEM((order, points), jnp.bfloat16),
            pltpu.VMEM((1, points), jnp.float32),
            pltpu.VMEM((hid, points), jnp.float32),
            pltpu.VMEM((hid, points), jnp.float32),
            pltpu.VMEM((pairs, NBF, NBF), jnp.bfloat16),
            pltpu.VMEM((META, NBF), jnp.bfloat16),
            pltpu.VMEM((NBF, hid), jnp.float32),
            pltpu.VMEM((NBF, hid), jnp.float32),
            pltpu.SemaphoreType.DMA((slots,)),
            pltpu.SemaphoreType.DMA((2,)),
            pltpu.SemaphoreType.DMA,
            pltpu.SemaphoreType.DMA,
        ],
        compiler_params=pltpu.CompilerParams(vmem_limit_bytes=60 << 20),
        name="domain_build",
    )(*lists, *arrays, basis, *fixed)


def collect_kernel(scale, places, returned, *refs):
    extras = refs[:-8]
    fock, energy, parts, result, meta, in_sem, out_sem, meta_sem = refs[-8:]
    copies, owned = places.shape
    sources = returned.shape[0]
    meta_in = pltpu.make_async_copy(returned.at[:, meta_rows(returned), :], meta, meta_sem)
    meta_in.start()

    @pl.loop(0, owned)
    def _(p):
        for t in range(copies):
            entry = places[t, p] // LINE
            rows = block_rows(places[t, p] - entry * LINE)

            @pl.when(entry < sources)
            def _():
                pltpu.make_async_copy(returned.at[entry, rows], parts.at[p, t], in_sem.at[p]).start()

            if extras:

                @pl.when(entry >= sources)
                def _():
                    for k, ref in enumerate(extras):

                        @pl.when(entry == sources + k)
                        def _():
                            pltpu.make_async_copy(ref.at[rows], parts.at[p, t], in_sem.at[p]).start()

    meta_in.wait()
    lane = lax.broadcasted_iota(jnp.int32, meta.shape, 2)
    row = lax.broadcasted_iota(jnp.int32, meta.shape, 1)
    sent = jnp.where((lane < 3) & (row == 0), meta[...].astype(jnp.float32), 0.0)
    per_source = jnp.sum(jnp.sum(sent, axis=0), axis=0, keepdims=True)
    energy[...] = jnp.sum(per_source, axis=1, keepdims=True) * scale
    last = (sources + len(extras)) * LINE

    @pl.loop(0, owned)
    def _(p):
        total = jnp.zeros((NBF, NBF), jnp.float32)
        for t in range(copies):
            here = places[t, p] < last

            @pl.when(here)
            def _():
                pltpu.make_async_copy(parts.at[p, t], parts.at[p, t], in_sem.at[p]).wait()

            total = total + jnp.where(here, parts[p, t].astype(jnp.float32), 0.0)
        result[p] = total
        pltpu.make_async_copy(result.at[p], fock.at[p], out_sem).start()

    pltpu.make_async_copy(result, fock, out_sem).wait()


def collect_blocks(places, returned, extras, scale):
    copies, owned = places.shape
    sources = returned.shape[0]
    return pl.pallas_call(
        functools.partial(collect_kernel, scale),
        out_shape=(
            jax.ShapeDtypeStruct((owned, NBF, NBF), jnp.float32),
            jax.ShapeDtypeStruct((1, 1), jnp.float32),
        ),
        in_specs=[smem_spec()] + [any_spec()] * (1 + len(extras)),
        out_specs=(any_spec(), vmem_spec()),
        scratch_shapes=[
            pltpu.VMEM((owned, copies, NBF, NBF), jnp.bfloat16),
            pltpu.VMEM((owned, NBF, NBF), jnp.float32),
            pltpu.VMEM((sources, META, NBF), jnp.bfloat16),
            pltpu.SemaphoreType.DMA((owned,)),
            pltpu.SemaphoreType.DMA,
            pltpu.SemaphoreType.DMA,
        ],
        cost_estimate=pl.CostEstimate(flops=1000, bytes_accessed=8 << 20, transcendentals=0),
        name="collect_blocks",
    )(places, returned, *extras)


def add_kernel(first, places, partial, *refs):
    extras = refs[:-8]
    fock, parts, result, listed, live, in_sem, fock_sem, out_sem = refs[-8:]
    copies, owned = places.shape
    live[0] = 0

    @pl.loop(0, owned)
    def _(p):
        hits = [places[t, p] >= first * LINE for t in range(copies)]

        @pl.when(functools.reduce(jnp.logical_or, hits))
        def _():
            k = live[0]
            listed[k] = p
            live[0] = k + 1
            pltpu.make_async_copy(partial.at[p], result.at[k], fock_sem.at[k]).start()
            for t in range(copies):
                entry = places[t, p] // LINE
                rows = block_rows(places[t, p] - entry * LINE)
                for e, ref in enumerate(extras):

                    @pl.when(entry == first + e)
                    def _():
                        pltpu.make_async_copy(ref.at[rows], parts.at[k, t], in_sem.at[k]).start()

    @pl.loop(0, live[0])
    def _(k):
        p = listed[k]
        pltpu.make_async_copy(partial.at[p], result.at[k], fock_sem.at[k]).wait()
        total = result[k]
        for t in range(copies):
            here = places[t, p] >= first * LINE

            @pl.when(here)
            def _():
                pltpu.make_async_copy(parts.at[k, t], parts.at[k, t], in_sem.at[k]).wait()

            total = total + jnp.where(here, parts[k, t].astype(jnp.float32), 0.0)
        result[k] = total
        pltpu.make_async_copy(result.at[k], fock.at[p], out_sem).start()

    @pl.loop(0, live[0])
    def _(k):
        pltpu.make_async_copy(result.at[0], fock.at[0], out_sem).wait()


def add_blocks(places, partial, extras, first):
    copies, owned = places.shape
    return pl.pallas_call(
        functools.partial(add_kernel, first),
        out_shape=jax.ShapeDtypeStruct(partial.shape, partial.dtype),
        in_specs=[smem_spec()] + [any_spec()] * (1 + len(extras)),
        out_specs=any_spec(),
        input_output_aliases={1: 0},
        scratch_shapes=[
            pltpu.VMEM((owned, copies, NBF, NBF), jnp.bfloat16),
            pltpu.VMEM((owned, NBF, NBF), jnp.float32),
            pltpu.SMEM((owned,), jnp.int32),
            pltpu.SMEM((1,), jnp.int32),
            pltpu.SemaphoreType.DMA((owned,)),
            pltpu.SemaphoreType.DMA((owned,)),
            pltpu.SemaphoreType.DMA,
        ],
        name="add_blocks",
    )(places, partial, *extras)


def exchange(array):
    return lax.all_to_all(array, AXES, split_axis=0, concat_axis=0, tiled=True)


def swap(arrays, axis, first):
    size = lax.axis_size(axis)
    return [
        lax.ppermute(array, axis, [(i, i ^ (first + k)) for i in range(size)]) if first + k else array
        for k, array in enumerate(arrays)
    ]


def body(density, dest, code, basis, descriptors, weights, w_in, w_hid1, w_hid2, w_out):
    rows_x, rows_z = lax.axis_size("gx"), lax.axis_size("gy")
    domains = rows_x * rows_z
    owned = density.shape[0]
    copies = dest.shape[1]
    capacity = max(2, 2 * copies * owned // domains)
    points = basis.shape[0]
    scale = 1.0 / (math.sqrt(points) * domains)
    basis_t = basis.T
    base_in = jnp.dot(w_in[1:].T, descriptors, precision=HI)
    fixed = (
        basis, basis_t, base_in, w_in, w_hid1, w_hid1.T, w_hid2, w_hid2.T, w_out[None, :], weights[None, :]
    )

    def plain():
        heads, places = plan_blocks(dest, code, domains)
        lists = scan(exchange(heads), [], capacity)
        inbound = exchange(direct_blocks(places, density, domains, capacity))
        (replies,) = domain_build(lists, inbound, [], *fixed)
        fock, energy = collect_blocks(places, exchange(replies), [], scale)
        return fock, energy[0, 0]

    if capacity < 8:
        return plain()
    direct = capacity // 2
    ranks = (rows_z - 1) * (capacity - direct)
    groups = (rows_x, rows_z)
    *panels, places = split_blocks(density, dest, code, direct, groups)
    lines_in = swap(panels[rows_x:], "gy", 1)
    near_in = swap(panels[:rows_x], "gx", 0)
    outgoing = direct_blocks(places, density, domains, direct)
    inbound = exchange(outgoing)
    *relayed, relay_places = relay(lines_in, rows_x, ranks, direct)
    relayed_in = swap(relayed, "gx", 0)
    *lists, raised = merge(near_in + relayed_in, direct, groups)

    def split():
        replies, *others = domain_build(lists, inbound, near_in + relayed_in, *fixed)
        relayed_back = swap(others[rows_x:], "gx", 0)
        near_back = swap(others[:rows_x], "gx", 0)
        returned = exchange(replies)
        lines_back = swap(relay_back(relay_places, relayed_back), "gy", 1)
        fock, energy = collect_blocks(places, returned, near_back, scale)
        return add_blocks(places, fock, lines_back, domains + rows_x), energy[0, 0]

    return lax.cond(raised[0] > 0, plain, split)


def solution(mesh):
    placed = (
        P(AXES, None, None),
        P(AXES, None),
        P(AXES, None),
        P(AXES, None),
        P(None, AXES),
        P(AXES),
        P(),
        P(),
        P(),
        P(),
    )
    return jax.shard_map(
        body,
        mesh=mesh,
        in_specs=placed,
        out_specs=(P(AXES, None, None), P()),
        check_vma=False,
    )
```

```python
import functools
import math

import jax
import jax.numpy as jnp
from jax import lax
from jax.experimental import pallas as pl
from jax.experimental.pallas import tpu as pltpu
from jax.sharding import PartitionSpec as P


NBF = 128
META = 8
LINE = 32
POOL = 16
AXES = ("gx", "gy")
HI = lax.Precision.HIGHEST


def any_spec():
    return pl.BlockSpec(memory_space=pl.ANY)


def smem_spec():
    return pl.BlockSpec(memory_space=pltpu.SMEM)


def vmem_spec():
    return pl.BlockSpec(memory_space=pltpu.VMEM)


def block_rows(rank):
    return pl.ds(pl.multiple_of(rank * NBF, NBF), NBF)


def panel(ranks):
    return jax.ShapeDtypeStruct((ranks * NBF + META, NBF), jnp.bfloat16)


def ranks_of(array):
    return array.shape[-2] // NBF


def meta_rows(array):
    return pl.ds(ranks_of(array) * NBF, META)


def lane_row(shape):
    lane = lax.broadcasted_iota(jnp.int32, shape, len(shape) - 1)
    row = lax.broadcasted_iota(jnp.int32, shape, len(shape) - 2)
    return lane, row


def plan_kernel(dest, code, heads, places, count, codes, codes16, sem):
    copies, owned = dest.shape
    domains = heads.shape[0]

    @pl.loop(0, domains)
    def _(d):
        count[d] = 0

    codes[...] = jnp.full(codes.shape, -1.0, jnp.float32)
    lane, row = lane_row((META, NBF))

    @pl.loop(0, owned)
    def _(p):
        for t in range(copies):
            d = dest[t, p]
            rank = count[d]
            count[d] = rank + 1
            places[0, t * owned + p] = d * LINE + rank
            value = code[t, p].astype(jnp.float32)
            codes[d] = jnp.where((lane == rank) & (row == 0), value, codes[d])

    codes16[...] = codes[...].astype(jnp.bfloat16)
    copy = pltpu.make_async_copy(codes16, heads, sem)
    copy.start()
    copy.wait()


def plan_blocks(dest, code, domains):
    owned, copies = dest.shape
    return pl.pallas_call(
        plan_kernel,
        out_shape=(
            jax.ShapeDtypeStruct((domains, META, NBF), jnp.bfloat16),
            jax.ShapeDtypeStruct((1, copies * owned), jnp.int32),
        ),
        in_specs=[smem_spec(), smem_spec()],
        out_specs=(any_spec(), smem_spec()),
        scratch_shapes=[
            pltpu.SMEM((domains,), jnp.int32),
            pltpu.VMEM((domains, META, NBF), jnp.float32),
            pltpu.VMEM((domains, META, NBF), jnp.bfloat16),
            pltpu.SemaphoreType.DMA,
        ],
        name="plan_blocks",
    )(dest.T, code.T)


def spread(line):
    return jnp.broadcast_to(line, (NBF, NBF)).T


def split_kernel(direct, groups, dest, code, density, *refs):
    copies, owned = dest.shape
    rows_x, rows_z = groups
    domains = rows_x * rows_z
    shift = rows_z.bit_length() - 1
    *panels, lists = refs[:-6]
    wide, stage, blocks, _, codes16, sems = refs[-6:]
    load = pltpu.make_async_copy(density, blocks, sems.at[0])
    load.start()
    me_x, me_z = lax.axis_index("gx"), lax.axis_index("gy")
    lane8, row8 = lane_row((META, NBF))

    def flat(ref):
        wide[...] = jnp.zeros(wide.shape, jnp.int32)
        wide[0:copies, 0:owned] = ref[...]
        rows = wide[...]
        line = rows[0:1, :]
        for t in range(1, copies):
            moved = pltpu.roll(rows, t * owned, 1)
            line = jnp.where(lane8[0:1] < t * owned, line, moved[t : t + 1, :])
        return line

    d = flat(dest)
    value = flat(code).astype(jnp.float32)
    lane = lax.broadcasted_iota(jnp.int32, (NBF, NBF), 1)
    row = lax.broadcasted_iota(jnp.int32, (NBF, NBF), 0)
    lane_f = lane.astype(jnp.float32)
    before = row < lane

    def earlier(key):
        same = (spread(key) == key) & before
        return jnp.sum(jnp.where(same, 1.0, 0.0), axis=0, keepdims=True)

    target = lax.shift_right_logical(d, shift)
    near = (target ^ me_x).astype(jnp.float32)
    far_i = (d & (rows_z - 1)) ^ me_z
    far = far_i.astype(jnp.float32)
    target = target.astype(jnp.float32)
    rank = earlier(d.astype(jnp.float32))
    late = rank >= direct
    home = far_i == 0
    spill = jnp.where(late, jnp.where(home, 0.0, 1.0), 0.0)
    close = jnp.where(late, jnp.where(home, 1.0, 0.0), 0.0)
    taken = earlier(far * spill)
    over = jnp.max(jnp.where(taken >= POOL, spill, 0.0), axis=1, keepdims=True)
    slot = jnp.where(home, rank - direct, jnp.minimum(taken, POOL - 1.0))
    kept = jnp.where(taken >= POOL, 0.0, spill)
    extra = kept + close
    entry = jnp.where(home, near, rows_x - 1.0 + far)
    place = jnp.where(late, (domains + entry) * LINE + slot, d.astype(jnp.float32) * LINE + rank)
    order = jnp.sum(jnp.where(before, spread(extra), 0.0), axis=0, keepdims=True)
    pick = jnp.where(spread(order) == lane_f, spread(extra), 0.0)
    listed = jnp.sum(pick * row.astype(jnp.float32), axis=0, keepdims=True)
    listed_entry = jnp.sum(pick * spread(entry), axis=0, keepdims=True)
    listed_slot = jnp.sum(pick * spread(slot), axis=0, keepdims=True)
    number = jnp.sum(extra, axis=1, keepdims=True)
    out = jnp.zeros((META, NBF), jnp.float32)
    for k, line in enumerate((place, listed, listed_entry, listed_slot, number)):
        out = jnp.where(row8 == k, jnp.broadcast_to(line, (META, NBF)), out)
    stage[...] = out.astype(jnp.int32)
    back = pltpu.make_async_copy(stage, lists, sems.at[1])
    back.start()
    rows16 = lax.broadcasted_iota(jnp.int32, (16, NBF), 0).astype(jnp.float32)

    def table(mark, amount, cell):
        left = jnp.where(rows16 == entry, (amount + 1.0) * mark, 0.0).astype(jnp.bfloat16)
        right = jnp.where(spread(cell) == lane_f, 1.0, 0.0).astype(jnp.bfloat16)
        return jnp.dot(left, right, preferred_element_type=jnp.float32) - 1.0

    early = jnp.where(late, 0.0, 1.0)
    own = jnp.where(home, early, 0.0)
    away = jnp.where(home, 0.0, early)
    tables = (
        table(extra, value, slot),
        table(own + kept, jnp.where(home, value, target), jnp.where(late, slot, rank)),
        table(away, value, target * direct + rank),
    )
    for e in range(len(panels)):
        cells = jnp.where(row8 == 3, jnp.broadcast_to(over, (META, NBF)), -1.0)
        for k, cell in enumerate(tables):
            cells = jnp.where(row8 == k, jnp.broadcast_to(cell[e : e + 1, :], (META, NBF)), cells)
        codes16[e] = cells.astype(jnp.bfloat16)
    metas = [
        pltpu.make_async_copy(codes16.at[k], ref.at[meta_rows(ref), :], sems.at[3 + k]) for k, ref in enumerate(panels)
    ]
    for copy in metas:
        copy.start()
    load.wait()
    back.wait()

    @pl.loop(0, lists[4, 0])
    def _(k):
        p = lax.rem(lists[1, k], owned)
        e = lists[2, k]
        rows = block_rows(lists[3, k])
        for j, ref in enumerate(panels):

            @pl.when(e == j)
            def _():
                pltpu.make_async_copy(blocks.at[p], ref.at[rows], sems.at[2]).start()

    for copy in metas:
        copy.wait()

    @pl.loop(0, lists[4, 0])
    def _(k):
        pltpu.make_async_copy(blocks.at[0], panels[0].at[block_rows(0)], sems.at[2]).wait()


def split_blocks(density, dest, code, direct, groups):
    owned, _ = dest.shape
    panels = [panel(direct)] * groups[0] + [panel(POOL)] * (groups[1] - 1)
    return pl.pallas_call(
        functools.partial(split_kernel, direct, groups),
        out_shape=(*panels, jax.ShapeDtypeStruct((META, NBF), jnp.int32)),
        in_specs=[vmem_spec(), vmem_spec(), any_spec()],
        out_specs=(any_spec(),) * len(panels) + (smem_spec(),),
        scratch_shapes=[
            pltpu.VMEM((META, NBF), jnp.int32),
            pltpu.VMEM((META, NBF), jnp.int32),
            pltpu.VMEM((owned, NBF, NBF), jnp.bfloat16),
            pltpu.VMEM((len(panels), META, NBF), jnp.int32),
            pltpu.VMEM((len(panels), META, NBF), jnp.bfloat16),
            pltpu.SemaphoreType.DMA((3 + len(panels),)),
        ],
        name="split_blocks",
    )(dest.T, code.T, density)


def direct_kernel(copies, places, density, out, blocks, live, load_sem, out_sem):
    owned = blocks.shape[0]
    domains = out.shape[0]
    load = pltpu.make_async_copy(density, blocks, load_sem)
    load.start()
    load.wait()
    live[0] = 0

    @pl.loop(0, owned)
    def _(p):
        for t in range(copies):
            entry = places[0, t * owned + p] // LINE
            rows = block_rows(places[0, t * owned + p] - entry * LINE)

            @pl.when(entry < domains)
            def _():
                live[0] = live[0] + 1
                pltpu.make_async_copy(blocks.at[p], out.at[entry, rows], out_sem).start()

    @pl.loop(0, live[0])
    def _(k):
        pltpu.make_async_copy(blocks.at[0], out.at[0, block_rows(0)], out_sem).wait()


def direct_blocks(places, density, domains, direct, copies):
    return pl.pallas_call(
        functools.partial(direct_kernel, copies),
        out_shape=jax.ShapeDtypeStruct((domains, direct * NBF, NBF), jnp.bfloat16),
        in_specs=[smem_spec(), any_spec()],
        out_specs=any_spec(),
        scratch_shapes=[
            pltpu.VMEM(density.shape, jnp.bfloat16),
            pltpu.SMEM((1,), jnp.int32),
            pltpu.SemaphoreType.DMA,
            pltpu.SemaphoreType.DMA,
        ],
        cost_estimate=pl.CostEstimate(flops=1000, bytes_accessed=8 << 20, transcendentals=0),
        name="direct_blocks",
    )(places, density)


def scan_kernel(direct, heads, *refs):
    extras = refs[:-9]
    starts, places, marks, lines, codes_v, codes, live, line_sem, code_sem = refs[-9:]
    sources = heads.shape[0]
    loads = [pltpu.make_async_copy(heads, lines.at[pl.ds(0, sources)], line_sem.at[0])]
    for k, ref in enumerate(extras):
        loads.append(pltpu.make_async_copy(ref.at[meta_rows(ref), :], lines.at[sources + k], line_sem.at[1 + k]))
    for load in loads:
        load.start()
    for load in loads:
        load.wait()
    head = lax.broadcasted_iota(jnp.int32, lines.shape, 1) == 0
    codes_v[...] = jnp.sum(jnp.where(head, lines[...].astype(jnp.float32), 0.0), axis=1).astype(jnp.int32)
    load = pltpu.make_async_copy(codes_v, codes, code_sem)
    load.start()
    load.wait()
    live[0] = 0

    def note(entry, rank):
        c = codes[entry, rank]

        @pl.when(c >= 0)
        def _():
            k = live[0]
            places[k] = entry * LINE + rank
            marks[k] = c
            live[0] = k + 1

    starts[0] = 0

    @pl.loop(0, sources)
    def _(source):
        for rank in range(direct):
            note(source, rank)

    starts[1] = live[0]
    for k, ref in enumerate(extras):

        @pl.loop(0, ranks_of(ref))
        def _(rank):
            note(sources + k, rank)

        starts[2 + k] = live[0]


def scan(heads, extras, direct):
    sources = heads.shape[0]
    entries = sources + len(extras)
    slots = sources * direct + sum(ranks_of(ref) for ref in extras)
    return pl.pallas_call(
        functools.partial(scan_kernel, direct),
        out_shape=(
            jax.ShapeDtypeStruct((2 + len(extras),), jnp.int32),
            jax.ShapeDtypeStruct((slots,), jnp.int32),
            jax.ShapeDtypeStruct((slots,), jnp.int32),
        ),
        in_specs=[any_spec()] * (1 + len(extras)),
        out_specs=(smem_spec(),) * 3,
        scratch_shapes=[
            pltpu.VMEM((entries, META, NBF), jnp.bfloat16),
            pltpu.VMEM((entries, NBF), jnp.int32),
            pltpu.SMEM((entries, NBF), jnp.int32),
            pltpu.SMEM((1,), jnp.int32),
            pltpu.SemaphoreType.DMA((1 + len(extras),)),
            pltpu.SemaphoreType.DMA,
        ],
        cost_estimate=pl.CostEstimate(flops=1000, bytes_accessed=8 << 20, transcendentals=0),
        name="scan",
    )(heads, *extras)


def merge_kernel(direct, groups, *refs):
    rows_x, rows_z = groups
    panels = refs[:-9]
    starts, places, marks, raised, lines, ints, info, live, sems = refs[-9:]
    loads = [pltpu.make_async_copy(ref.at[meta_rows(ref), :], lines.at[k], sems.at[k]) for k, ref in enumerate(panels)]
    for load in loads:
        load.start()
    for load in loads:
        load.wait()
    ints[...] = lines[...].astype(jnp.float32).astype(jnp.int32)
    load = pltpu.make_async_copy(ints, info, sems.at[0])
    load.start()
    load.wait()
    me_x, me_z = lax.axis_index("gx"), lax.axis_index("gy")
    live[0] = 0
    raised[0] = 0
    starts[0] = 0

    def note(entry, rank, c):
        @pl.when(c >= 0)
        def _():
            k = live[0]
            places[k] = entry * LINE + rank
            marks[k] = c
            live[0] = k + 1

    @pl.loop(0, rows_x)
    def _(k):
        first = (k ^ me_x) * rows_z
        raised[0] = raised[0] | info[k, 3, 0] | info[rows_x + k, 3, 0]
        for rank in range(direct):
            note(first + me_z, rank, info[k, 1, rank])
            for h in range(rows_z - 1):
                note(first + (me_z ^ (h + 1)), rank, info[rows_x + k, 1, h * direct + rank])

    starts[1] = live[0]
    domains = rows_x * rows_z
    for k, ref in enumerate(panels):

        @pl.loop(0, ranks_of(ref))
        def _(rank):
            note(domains + k, rank, info[k, 0, rank])

        starts[2 + k] = live[0]


def merge(panels, direct, groups):
    slots = groups[0] * groups[1] * direct + sum(ranks_of(ref) for ref in panels)
    return pl.pallas_call(
        functools.partial(merge_kernel, direct, groups),
        out_shape=(
            jax.ShapeDtypeStruct((2 + len(panels),), jnp.int32),
            jax.ShapeDtypeStruct((slots,), jnp.int32),
            jax.ShapeDtypeStruct((slots,), jnp.int32),
            jax.ShapeDtypeStruct((1,), jnp.int32),
        ),
        in_specs=[any_spec()] * len(panels),
        out_specs=(smem_spec(),) * 4,
        scratch_shapes=[
            pltpu.VMEM((len(panels), META, NBF), jnp.bfloat16),
            pltpu.VMEM((len(panels), META, NBF), jnp.int32),
            pltpu.SMEM((len(panels), META, NBF), jnp.int32),
            pltpu.SMEM((1,), jnp.int32),
            pltpu.SemaphoreType.DMA((len(panels),)),
        ],
        cost_estimate=pl.CostEstimate(flops=1000, bytes_accessed=8 << 20, transcendentals=0),
        name="merge",
    )(*panels)


def relay_kernel(direct, *refs):
    info, count, table, stage, lines, ints, cells, codes16, in_sem, sems = refs[-10:]
    hops = lines.shape[0]
    arrived = refs[:hops]
    outs = refs[hops:-11]
    places = refs[-11]
    ranks = ranks_of(outs[0])
    me = lax.axis_index("gx")
    loads = [
        pltpu.make_async_copy(ref.at[meta_rows(ref), :], lines.at[h], sems.at[h]) for h, ref in enumerate(arrived)
    ]
    for load in loads:
        load.start()
    last = sems.at[hops + len(outs)]
    cells[...] = jnp.full(cells.shape, -1, jnp.int32)
    fill = pltpu.make_async_copy(cells, table, last)
    fill.start()
    for k in range(len(outs)):
        count[k] = 0
    for load in loads:
        load.wait()
    ints[...] = lines[...].astype(jnp.float32).astype(jnp.int32)
    load = pltpu.make_async_copy(ints, info, sems.at[0])
    load.start()
    load.wait()
    fill.wait()

    def fetch(h, q):
        return pltpu.make_async_copy(arrived[h].at[block_rows(q)], stage.at[h * POOL + q], in_sem.at[h * POOL + q])

    for h in range(hops):

        @pl.loop(0, POOL)
        def _(q):
            places[h, q] = -1
            c = info[h, 0, q]

            @pl.when(c >= 0)
            def _():
                fetch(h, q).start()
                near = info[h, 1, q] ^ me
                slot = jnp.minimum(count[near], ranks - 1)
                count[near] = slot + 1
                places[h, q] = near * LINE + slot
                table[near, 0, slot] = c

    raised = functools.reduce(jnp.bitwise_or, [info[h, 3, 0] for h in range(hops)])

    @pl.loop(0, len(outs))
    def _(k):
        table[k, 3, 0] = raised
        for h in range(hops):
            for rank in range(direct):
                table[k, 1, h * direct + rank] = info[h, 2, (k ^ me) * direct + rank]

    back = pltpu.make_async_copy(table, cells, last)
    back.start()
    back.wait()
    codes16[...] = cells[...].astype(jnp.float32).astype(jnp.bfloat16)
    metas = [
        pltpu.make_async_copy(codes16.at[k], ref.at[meta_rows(ref), :], sems.at[hops + k])
        for k, ref in enumerate(outs)
    ]
    for copy in metas:
        copy.start()
    for h in range(hops):

        @pl.loop(0, POOL)
        def _(q):
            place = places[h, q]

            @pl.when(place >= 0)
            def _():
                fetch(h, q).wait()
                near = place // LINE
                rows = block_rows(place - near * LINE)
                for k, ref in enumerate(outs):

                    @pl.when(near == k)
                    def _():
                        pltpu.make_async_copy(stage.at[h * POOL + q], ref.at[rows], last).start()

    for copy in metas:
        copy.wait()
    for h in range(hops):

        @pl.loop(0, POOL)
        def _(q):
            @pl.when(places[h, q] >= 0)
            def _():
                pltpu.make_async_copy(stage.at[0], outs[0].at[block_rows(0)], last).wait()


def relay(arrived, near_count, ranks, direct):
    hops = len(arrived)
    return pl.pallas_call(
        functools.partial(relay_kernel, direct),
        out_shape=tuple([panel(ranks)] * near_count + [jax.ShapeDtypeStruct((hops, POOL), jnp.int32)]),
        in_specs=[any_spec()] * hops,
        out_specs=tuple([any_spec()] * near_count + [smem_spec()]),
        scratch_shapes=[
            pltpu.SMEM((hops, META, NBF), jnp.int32),
            pltpu.SMEM((near_count,), jnp.int32),
            pltpu.SMEM((near_count, META, NBF), jnp.int32),
            pltpu.VMEM((hops * POOL, NBF, NBF), jnp.bfloat16),
            pltpu.VMEM((hops, META, NBF), jnp.bfloat16),
            pltpu.VMEM((hops, META, NBF), jnp.int32),
            pltpu.VMEM((near_count, META, NBF), jnp.int32),
            pltpu.VMEM((near_count, META, NBF), jnp.bfloat16),
            pltpu.SemaphoreType.DMA((hops * POOL,)),
            pltpu.SemaphoreType.DMA((hops + near_count + 1,)),
        ],
        cost_estimate=pl.CostEstimate(flops=1000, bytes_accessed=4 << 20, transcendentals=0),
        name="relay",
    )(*arrived)


def relay_back_kernel(places, *refs):
    stage, in_sem, out_sem = refs[-3:]
    hops = places.shape[0]
    arrived, outs = refs[: -3 - hops], refs[-3 - hops : -3]

    def fetch(ref, rows, h, q):
        return pltpu.make_async_copy(ref.at[rows], stage.at[h * POOL + q], in_sem.at[h * POOL + q])

    def give(h, q):
        return pltpu.make_async_copy(stage.at[h * POOL + q], outs[h].at[block_rows(q)], out_sem)

    for h in range(hops):

        @pl.loop(0, POOL)
        def _(q):
            place = places[h, q]

            @pl.when(place >= 0)
            def _():
                near = place // LINE
                rows = block_rows(place - near * LINE)
                for k, ref in enumerate(arrived):

                    @pl.when(near == k)
                    def _():
                        fetch(ref, rows, h, q).start()

    for h in range(hops):

        @pl.loop(0, POOL)
        def _(q):
            @pl.when(places[h, q] >= 0)
            def _():
                fetch(arrived[0], block_rows(0), h, q).wait()
                give(h, q).start()

    for h in range(hops):

        @pl.loop(0, POOL)
        def _(q):
            @pl.when(places[h, q] >= 0)
            def _():
                give(h, q).wait()


def relay_back(places, arrived):
    hops = places.shape[0]
    return pl.pallas_call(
        relay_back_kernel,
        out_shape=tuple([panel(POOL)] * hops),
        in_specs=[smem_spec()] + [any_spec()] * len(arrived),
        out_specs=tuple([any_spec()] * hops),
        scratch_shapes=[
            pltpu.VMEM((hops * POOL, NBF, NBF), jnp.bfloat16),
            pltpu.SemaphoreType.DMA((hops * POOL,)),
            pltpu.SemaphoreType.DMA,
        ],
        cost_estimate=pl.CostEstimate(flops=1000, bytes_accessed=4 << 20, transcendentals=0),
        name="relay_back",
    )(places, *arrived)


def domain_kernel(extra_count, starts, places, marks, *refs):
    inbound, *extras = refs[: 1 + extra_count]
    basis, basis_t, base_in, w_in, w_hid1, w_hid1_t, w_hid2, w_hid2_t, w_last, weights = refs[
        1 + extra_count : 11 + extra_count
    ]
    reply, *extra_replies = refs[11 + extra_count : 12 + 2 * extra_count]
    (
        seen,
        stage,
        acc,
        dense,
        basis_v,
        basis_tv,
        rho,
        hid1,
        hid2,
        blocks,
        meta,
        w_row,
        w_out,
        in_sem,
        basis_sem,
        out_sem,
        meta_sem,
    ) = refs[12 + 2 * extra_count :]
    sources = inbound.shape[0]
    direct = ranks_of(inbound)
    points, order = basis.shape
    width = order // NBF
    pairs = width * width
    load_t = pltpu.make_async_copy(basis_t, basis_tv, basis_sem.at[0])
    load_n = pltpu.make_async_copy(basis, basis_v, basis_sem.at[1])
    live = starts[1 + extra_count]

    @pl.loop(0, starts[1])
    def _(k):
        entry = places[k] // LINE
        rows = block_rows(places[k] - entry * LINE)
        pltpu.make_async_copy(inbound.at[entry, rows], stage.at[k], in_sem.at[k]).start()

    for e, ref in enumerate(extras):

        @pl.loop(starts[1 + e], starts[2 + e])
        def _(k):
            rows = block_rows(places[k] - (sources + e) * LINE)
            pltpu.make_async_copy(ref.at[rows], stage.at[k], in_sem.at[k]).start()

    load_t.start()
    load_n.start()

    @pl.loop(0, pairs)
    def _(c):
        seen[c] = 0

    w_row[...] = jnp.broadcast_to(w_in[0:1, :], w_row.shape).T
    w_out[...] = jnp.broadcast_to(w_last[...], w_out.shape).T

    @pl.loop(0, live)
    def _(k):
        c = marks[k]
        pltpu.make_async_copy(inbound.at[0, block_rows(0)], stage.at[k], in_sem.at[k]).wait()
        value = stage[k].astype(jnp.float32)
        before = seen[c]
        seen[c] = 1

        @pl.when(before == 0)
        def _():
            acc[c] = value

        @pl.when(before != 0)
        def _():
            acc[c] = acc[c] + value

    @pl.loop(0, width)
    def _(a):
        rows = block_rows(a)
        for b in range(width):
            there = seen[a * width + b] != 0
            value = jnp.where(there, acc[a * width + b], 0.0)
            dense[rows, b * NBF : (b + 1) * NBF] = value.astype(jnp.bfloat16)

    load_t.wait()
    tile = 512

    @pl.loop(0, points // tile)
    def _(n):
        cols = pl.ds(pl.multiple_of(n * tile, tile), tile)
        part = basis_tv[:, cols]
        projected = jnp.dot(dense[...], part, preferred_element_type=jnp.float32)
        rho[:, cols] = jnp.sum(projected * part.astype(jnp.float32), axis=0, keepdims=True)

    h1 = jnp.tanh(base_in[...] + w_row[:, 0:1] * rho[...])
    hid1[...] = h1
    h2 = jnp.tanh(jnp.dot(w_hid1_t[...], h1, precision=HI, preferred_element_type=jnp.float32))
    hid2[...] = h2
    h3 = jnp.tanh(jnp.dot(w_hid2_t[...], h2, precision=HI, preferred_element_type=jnp.float32))
    logits = jnp.sum(w_out[:, 0:1] * h3, axis=0, keepdims=True)
    decay = jnp.exp(-jnp.abs(logits))
    energy_at = -(jnp.maximum(logits, 0.0) + jnp.log1p(decay))
    slope = -jnp.where(logits >= 0, 1.0, decay) / (1.0 + decay)
    g3 = (w_out[:, 0:1] * slope) * (1.0 - h3 * h3)
    h2 = hid2[...]
    g2 = jnp.dot(w_hid2[...], g3, precision=HI, preferred_element_type=jnp.float32) * (1.0 - h2 * h2)
    h1 = hid1[...]
    g1 = jnp.dot(w_hid1[...], g2, precision=HI, preferred_element_type=jnp.float32) * (1.0 - h1 * h1)
    deriv = jnp.sum(w_row[:, 0:1] * g1, axis=0, keepdims=True)
    rho[...] = weights[...] * deriv
    total = jnp.sum(weights[...] * energy_at, axis=1, keepdims=True)
    top = total.astype(jnp.bfloat16).astype(jnp.float32)
    rest = total - top
    middle = rest.astype(jnp.bfloat16).astype(jnp.float32)
    low = rest - middle
    lane = lax.broadcasted_iota(jnp.int32, (META, NBF), 1)
    line = jnp.where(lane == 0, top, jnp.where(lane == 1, middle, jnp.where(lane == 2, low, 0.0)))
    meta[...] = line.astype(jnp.bfloat16)

    @pl.loop(0, sources)
    def _(source):
        pltpu.make_async_copy(meta, reply.at[source, pl.ds(direct * NBF, META)], meta_sem).start()

    load_n.wait()

    @pl.loop(0, points // NBF)
    def _(n):
        rows = block_rows(n)
        line = jnp.broadcast_to(rho[:, rows], (NBF, NBF))
        column = line.T
        for b in range(width):
            cols = slice(b * NBF, (b + 1) * NBF)
            basis_v[rows, cols] = (column * basis_v[rows, cols].astype(jnp.float32)).astype(jnp.bfloat16)

    @pl.loop(0, width // 2)
    def _(n):
        cols = pl.ds(pl.multiple_of(n * 2 * NBF, 2 * NBF), 2 * NBF)
        result = jnp.dot(basis_tv[...], basis_v[:, cols], preferred_element_type=jnp.float32).astype(jnp.bfloat16)
        for a in range(width):
            for half in range(2):
                blocks[a * width + 2 * n + half] = result[a * NBF : (a + 1) * NBF, half * NBF : (half + 1) * NBF]

    def give(ref, rows, k):
        pltpu.make_async_copy(blocks.at[marks[k]], ref.at[rows], out_sem).start()

    for e, ref in enumerate(extra_replies):

        @pl.loop(starts[1 + e], starts[2 + e])
        def _(k):
            give(ref, block_rows(places[k] - (sources + e) * LINE), k)

    @pl.loop(0, starts[1])
    def _(k):
        entry = places[k] // LINE
        give(reply.at[entry], block_rows(places[k] - entry * LINE), k)

    @pl.loop(0, live)
    def _(k):
        pltpu.make_async_copy(blocks.at[0], reply.at[0, block_rows(0)], out_sem).wait()

    whole = reply.at[:, meta_rows(reply), :]
    pltpu.make_async_copy(whole, whole, meta_sem).wait()


def domain_build(lists, inbound, extras, basis, *fixed):
    sources = inbound.shape[0]
    direct = ranks_of(inbound)
    points, order = basis.shape
    hid = fixed[1].shape[0]
    pairs = (order // NBF) ** 2
    slots = lists[1].shape[0]
    arrays = [inbound] + list(extras)
    replies = [jax.ShapeDtypeStruct((sources, direct * NBF + META, NBF), jnp.bfloat16)]
    replies += [jax.ShapeDtypeStruct((ranks_of(ref) * NBF, NBF), jnp.bfloat16) for ref in extras]
    return pl.pallas_call(
        functools.partial(domain_kernel, len(extras)),
        out_shape=tuple(replies),
        in_specs=[smem_spec()] * 3 + [any_spec()] * (len(arrays) + 2) + [vmem_spec()] * 8,
        out_specs=(any_spec(),) * len(arrays),
        scratch_shapes=[
            pltpu.SMEM((pairs,), jnp.int32),
            pltpu.VMEM((slots, NBF, NBF), jnp.bfloat16),
            pltpu.VMEM((pairs, NBF, NBF), jnp.float32),
            pltpu.VMEM((order, order), jnp.bfloat16),
            pltpu.VMEM((points, order), jnp.bfloat16),
            pltpu.VMEM((order, points), jnp.bfloat16),
            pltpu.VMEM((1, points), jnp.float32),
            pltpu.VMEM((hid, points), jnp.float32),
            pltpu.VMEM((hid, points), jnp.float32),
            pltpu.VMEM((pairs, NBF, NBF), jnp.bfloat16),
            pltpu.VMEM((META, NBF), jnp.bfloat16),
            pltpu.VMEM((NBF, hid), jnp.float32),
            pltpu.VMEM((NBF, hid), jnp.float32),
            pltpu.SemaphoreType.DMA((slots,)),
            pltpu.SemaphoreType.DMA((2,)),
            pltpu.SemaphoreType.DMA,
            pltpu.SemaphoreType.DMA,
        ],
        compiler_params=pltpu.CompilerParams(vmem_limit_bytes=60 << 20),
        name="domain_build",
    )(*lists, *arrays, basis, *fixed)


def collect_kernel(scale, places, returned, *refs):
    extras = refs[:-9]
    fock, energy, listed, parts, result, meta, in_sem, out_sem, meta_sem = refs[-9:]
    owned, copies = parts.shape[:2]
    sources = returned.shape[0]
    meta_in = pltpu.make_async_copy(returned.at[:, meta_rows(returned), :], meta, meta_sem)
    meta_in.start()

    @pl.loop(0, owned)
    def _(p):
        for t in range(copies):
            entry = places[0, t * owned + p] // LINE
            rows = block_rows(places[0, t * owned + p] - entry * LINE)

            @pl.when(entry < sources)
            def _():
                pltpu.make_async_copy(returned.at[entry, rows], parts.at[p, t], in_sem.at[p]).start()

            if extras:

                @pl.when(entry >= sources)
                def _():
                    for k, ref in enumerate(extras):

                        @pl.when(entry == sources + k)
                        def _():
                            pltpu.make_async_copy(ref.at[rows], parts.at[p, t], in_sem.at[p]).start()

    meta_in.wait()
    lane = lax.broadcasted_iota(jnp.int32, meta.shape, 2)
    row = lax.broadcasted_iota(jnp.int32, meta.shape, 1)
    sent = jnp.where((lane < 3) & (row == 0), meta[...].astype(jnp.float32), 0.0)
    per_source = jnp.sum(jnp.sum(sent, axis=0), axis=0, keepdims=True)
    energy[...] = jnp.sum(per_source, axis=1, keepdims=True) * scale
    last = (sources + len(extras)) * LINE
    listed[owned] = 0

    @pl.loop(0, owned)
    def _(p):
        hits = [places[0, t * owned + p] >= last for t in range(copies)]

        @pl.when(functools.reduce(jnp.logical_or, hits))
        def _():
            k = listed[owned]
            listed[k] = p
            listed[owned] = k + 1

        total = jnp.zeros((NBF, NBF), jnp.float32)
        for t in range(copies):
            here = places[0, t * owned + p] < last

            @pl.when(here)
            def _():
                pltpu.make_async_copy(parts.at[p, t], parts.at[p, t], in_sem.at[p]).wait()

            total = total + jnp.where(here, parts[p, t].astype(jnp.float32), 0.0)
        result[p] = total
        pltpu.make_async_copy(result.at[p], fock.at[p], out_sem).start()

    pltpu.make_async_copy(result, fock, out_sem).wait()


def collect_blocks(places, returned, extras, scale, owned, copies):
    sources = returned.shape[0]
    return pl.pallas_call(
        functools.partial(collect_kernel, scale),
        out_shape=(
            jax.ShapeDtypeStruct((owned, NBF, NBF), jnp.float32),
            jax.ShapeDtypeStruct((1, 1), jnp.float32),
            jax.ShapeDtypeStruct((owned + 1,), jnp.int32),
        ),
        in_specs=[smem_spec()] + [any_spec()] * (1 + len(extras)),
        out_specs=(any_spec(), vmem_spec(), smem_spec()),
        scratch_shapes=[
            pltpu.VMEM((owned, copies, NBF, NBF), jnp.bfloat16),
            pltpu.VMEM((owned, NBF, NBF), jnp.float32),
            pltpu.VMEM((sources, META, NBF), jnp.bfloat16),
            pltpu.SemaphoreType.DMA((owned,)),
            pltpu.SemaphoreType.DMA,
            pltpu.SemaphoreType.DMA,
        ],
        cost_estimate=pl.CostEstimate(flops=1000, bytes_accessed=8 << 20, transcendentals=0),
        name="collect_blocks",
    )(places, returned, *extras)


def add_kernel(first, places, listed, partial, *refs):
    extras = refs[:-6]
    fock, parts, result, in_sem, fock_sem, out_sem = refs[-6:]
    owned, copies = parts.shape[:2]
    number = listed[owned]

    @pl.loop(0, number)
    def _(k):
        p = listed[k]
        pltpu.make_async_copy(partial.at[p], result.at[k], fock_sem.at[k]).start()
        for t in range(copies):
            entry = places[0, t * owned + p] // LINE
            rows = block_rows(places[0, t * owned + p] - entry * LINE)
            for e, ref in enumerate(extras):

                @pl.when(entry == first + e)
                def _():
                    pltpu.make_async_copy(ref.at[rows], parts.at[k, t], in_sem.at[k]).start()

    @pl.loop(0, number)
    def _(k):
        p = listed[k]
        pltpu.make_async_copy(partial.at[p], result.at[k], fock_sem.at[k]).wait()
        total = result[k]
        for t in range(copies):
            here = places[0, t * owned + p] >= first * LINE

            @pl.when(here)
            def _():
                pltpu.make_async_copy(parts.at[k, t], parts.at[k, t], in_sem.at[k]).wait()

            total = total + jnp.where(here, parts[k, t].astype(jnp.float32), 0.0)
        result[k] = total
        pltpu.make_async_copy(result.at[k], fock.at[p], out_sem).start()

    @pl.loop(0, number)
    def _(k):
        pltpu.make_async_copy(result.at[0], fock.at[0], out_sem).wait()


def add_blocks(places, listed, partial, extras, first, copies):
    owned = partial.shape[0]
    return pl.pallas_call(
        functools.partial(add_kernel, first),
        out_shape=jax.ShapeDtypeStruct(partial.shape, partial.dtype),
        in_specs=[smem_spec()] * 2 + [any_spec()] * (1 + len(extras)),
        out_specs=any_spec(),
        input_output_aliases={2: 0},
        scratch_shapes=[
            pltpu.VMEM((owned, copies, NBF, NBF), jnp.bfloat16),
            pltpu.VMEM((owned, NBF, NBF), jnp.float32),
            pltpu.SemaphoreType.DMA((owned,)),
            pltpu.SemaphoreType.DMA((owned,)),
            pltpu.SemaphoreType.DMA,
        ],
        name="add_blocks",
    )(places, listed, partial, *extras)


def exchange(array):
    return lax.all_to_all(array, AXES, split_axis=0, concat_axis=0, tiled=True)


def swap(arrays, axis, first):
    size = lax.axis_size(axis)
    return [
        lax.ppermute(array, axis, [(i, i ^ (first + k)) for i in range(size)]) if first + k else array
        for k, array in enumerate(arrays)
    ]


def body(density, dest, code, basis, descriptors, weights, w_in, w_hid1, w_hid2, w_out):
    rows_x, rows_z = lax.axis_size("gx"), lax.axis_size("gy")
    domains = rows_x * rows_z
    owned = density.shape[0]
    copies = dest.shape[1]
    capacity = max(2, 2 * copies * owned // domains)
    points = basis.shape[0]
    scale = 1.0 / (math.sqrt(points) * domains)
    basis_t = basis.T
    base_in = jnp.dot(w_in[1:].T, descriptors, precision=HI)
    fixed = (
        basis, basis_t, base_in, w_in, w_hid1, w_hid1.T, w_hid2, w_hid2.T, w_out[None, :], weights[None, :]
    )

    def plain():
        heads, places = plan_blocks(dest, code, domains)
        lists = scan(exchange(heads), [], capacity)
        inbound = exchange(direct_blocks(places, density, domains, capacity, copies))
        (replies,) = domain_build(lists, inbound, [], *fixed)
        fock, energy, _ = collect_blocks(places, exchange(replies), [], scale, owned, copies)
        return fock, energy[0, 0]

    if capacity < 8 or copies * owned != NBF:
        return plain()
    direct = capacity // 2
    ranks = (rows_z - 1) * (capacity - direct)
    groups = (rows_x, rows_z)
    *panels, places = split_blocks(density, dest, code, direct, groups)
    lines_in = swap(panels[rows_x:], "gy", 1)
    near_in = swap(panels[:rows_x], "gx", 0)
    outgoing = direct_blocks(places, density, domains, direct, copies)
    inbound = exchange(outgoing)
    *relayed, relay_places = relay(lines_in, rows_x, ranks, direct)
    relayed_in = swap(relayed, "gx", 0)
    *lists, raised = merge(near_in + relayed_in, direct, groups)

    def split():
        replies, *others = domain_build(lists, inbound, near_in + relayed_in, *fixed)
        relayed_back = swap(others[rows_x:], "gx", 0)
        near_back = swap(others[:rows_x], "gx", 0)
        returned = exchange(replies)
        lines_back = swap(relay_back(relay_places, relayed_back), "gy", 1)
        fock, energy, listed = collect_blocks(places, returned, near_back, scale, owned, copies)
        return add_blocks(places, listed, fock, lines_back, domains + rows_x, copies), energy[0, 0]

    return lax.cond(raised[0] > 0, plain, split)


def solution(mesh):
    placed = (
        P(AXES, None, None),
        P(AXES, None),
        P(AXES, None),
        P(AXES, None),
        P(None, AXES),
        P(AXES),
        P(),
        P(),
        P(),
        P(),
    )
    return jax.shard_map(
        body,
        mesh=mesh,
        in_specs=placed,
        out_specs=(P(AXES, None, None), P()),
        check_vma=False,
    )
```

```python
import functools
import math

import jax
import jax.numpy as jnp
from jax import lax
from jax.experimental import pallas as pl
from jax.experimental.pallas import tpu as pltpu
from jax.sharding import PartitionSpec as P


NBF = 128
META = 8
LINE = 32
POOL = 16
AXES = ("gx", "gy")
HI = lax.Precision.HIGHEST


def any_spec():
    return pl.BlockSpec(memory_space=pl.ANY)


def smem_spec():
    return pl.BlockSpec(memory_space=pltpu.SMEM)


def vmem_spec():
    return pl.BlockSpec(memory_space=pltpu.VMEM)


def block_rows(rank):
    return pl.ds(pl.multiple_of(rank * NBF, NBF), NBF)


def panel(ranks):
    return jax.ShapeDtypeStruct((ranks * NBF + META, NBF), jnp.bfloat16)


def ranks_of(array):
    return array.shape[-2] // NBF


def meta_rows(array):
    return pl.ds(ranks_of(array) * NBF, META)


def lane_row(shape):
    lane = lax.broadcasted_iota(jnp.int32, shape, len(shape) - 1)
    row = lax.broadcasted_iota(jnp.int32, shape, len(shape) - 2)
    return lane, row


def plan_kernel(dest, code, heads, places, count, codes, codes16, sem):
    copies, owned = dest.shape
    domains = heads.shape[0]

    @pl.loop(0, domains)
    def _(d):
        count[d] = 0

    codes[...] = jnp.full(codes.shape, -1.0, jnp.float32)
    lane, row = lane_row((META, NBF))

    @pl.loop(0, owned)
    def _(p):
        for t in range(copies):
            d = dest[t, p]
            rank = count[d]
            count[d] = rank + 1
            places[0, t * owned + p] = d * LINE + rank
            value = code[t, p].astype(jnp.float32)
            codes[d] = jnp.where((lane == rank) & (row == 0), value, codes[d])

    codes16[...] = codes[...].astype(jnp.bfloat16)
    copy = pltpu.make_async_copy(codes16, heads, sem)
    copy.start()
    copy.wait()


def plan_blocks(dest, code, domains):
    owned, copies = dest.shape
    return pl.pallas_call(
        plan_kernel,
        out_shape=(
            jax.ShapeDtypeStruct((domains, META, NBF), jnp.bfloat16),
            jax.ShapeDtypeStruct((1, copies * owned), jnp.int32),
        ),
        in_specs=[smem_spec(), smem_spec()],
        out_specs=(any_spec(), smem_spec()),
        scratch_shapes=[
            pltpu.SMEM((domains,), jnp.int32),
            pltpu.VMEM((domains, META, NBF), jnp.float32),
            pltpu.VMEM((domains, META, NBF), jnp.bfloat16),
            pltpu.SemaphoreType.DMA,
        ],
        name="plan_blocks",
    )(dest.T, code.T)


def spread(line):
    return jnp.broadcast_to(line, (NBF, NBF)).T


def split_kernel(direct, groups, dest, code, density, *refs):
    copies, owned = dest.shape
    rows_x, rows_z = groups
    domains = rows_x * rows_z
    shift = rows_z.bit_length() - 1
    *panels, lists = refs[:-6]
    wide, stage, blocks, _, codes16, sems = refs[-6:]
    load = pltpu.make_async_copy(density, blocks, sems.at[0])
    load.start()
    me_x, me_z = lax.axis_index("gx"), lax.axis_index("gy")
    lane8, row8 = lane_row((META, NBF))

    def flat(ref):
        wide[...] = jnp.zeros(wide.shape, jnp.int32)
        wide[0:copies, 0:owned] = ref[...]
        rows = wide[...]
        line = rows[0:1, :]
        for t in range(1, copies):
            moved = pltpu.roll(rows, t * owned, 1)
            line = jnp.where(lane8[0:1] < t * owned, line, moved[t : t + 1, :])
        return line

    d = flat(dest)
    value = flat(code).astype(jnp.float32)
    lane = lax.broadcasted_iota(jnp.int32, (NBF, NBF), 1)
    row = lax.broadcasted_iota(jnp.int32, (NBF, NBF), 0)
    lane_f = lane.astype(jnp.float32)
    before = row < lane

    def earlier(key):
        same = (spread(key) == key) & before
        return jnp.sum(jnp.where(same, 1.0, 0.0), axis=0, keepdims=True)

    target = lax.shift_right_logical(d, shift)
    near = (target ^ me_x).astype(jnp.float32)
    far_i = (d & (rows_z - 1)) ^ me_z
    far = far_i.astype(jnp.float32)
    target = target.astype(jnp.float32)
    rank = earlier(d.astype(jnp.float32))
    late = rank >= direct
    home = far_i == 0
    spill = jnp.where(late, jnp.where(home, 0.0, 1.0), 0.0)
    close = jnp.where(late, jnp.where(home, 1.0, 0.0), 0.0)
    taken = earlier(far * spill)
    over = jnp.max(jnp.where(taken >= POOL, spill, 0.0), axis=1, keepdims=True)
    slot = jnp.where(home, rank - direct, jnp.minimum(taken, POOL - 1.0))
    kept = jnp.where(taken >= POOL, 0.0, spill)
    extra = kept + close
    entry = jnp.where(home, near, rows_x - 1.0 + far)
    place = jnp.where(late, (domains + entry) * LINE + slot, d.astype(jnp.float32) * LINE + rank)
    order = jnp.sum(jnp.where(before, spread(extra), 0.0), axis=0, keepdims=True)
    pick = jnp.where(spread(order) == lane_f, spread(extra), 0.0)
    listed = jnp.sum(pick * row.astype(jnp.float32), axis=0, keepdims=True)
    listed_entry = jnp.sum(pick * spread(entry), axis=0, keepdims=True)
    listed_slot = jnp.sum(pick * spread(slot), axis=0, keepdims=True)
    number = jnp.sum(extra, axis=1, keepdims=True)
    out = jnp.zeros((META, NBF), jnp.float32)
    for k, line in enumerate((place, listed, listed_entry, listed_slot, number)):
        out = jnp.where(row8 == k, jnp.broadcast_to(line, (META, NBF)), out)
    stage[...] = out.astype(jnp.int32)
    back = pltpu.make_async_copy(stage, lists, sems.at[1])
    back.start()
    rows16 = lax.broadcasted_iota(jnp.int32, (16, NBF), 0).astype(jnp.float32)

    def table(mark, amount, cell):
        left = jnp.where(rows16 == entry, (amount + 1.0) * mark, 0.0).astype(jnp.bfloat16)
        right = jnp.where(spread(cell) == lane_f, 1.0, 0.0).astype(jnp.bfloat16)
        return jnp.dot(left, right, preferred_element_type=jnp.float32) - 1.0

    early = jnp.where(late, 0.0, 1.0)
    own = jnp.where(home, early, 0.0)
    away = jnp.where(home, 0.0, early)
    tables = (
        table(extra, value, slot),
        table(own + kept, jnp.where(home, value, target), jnp.where(late, slot, rank)),
        table(away, value, target * direct + rank),
    )
    for e in range(len(panels)):
        cells = jnp.where(row8 == 3, jnp.broadcast_to(over, (META, NBF)), -1.0)
        for k, cell in enumerate(tables):
            cells = jnp.where(row8 == k, jnp.broadcast_to(cell[e : e + 1, :], (META, NBF)), cells)
        codes16[e] = cells.astype(jnp.bfloat16)
    metas = [
        pltpu.make_async_copy(codes16.at[k], ref.at[meta_rows(ref), :], sems.at[3 + k]) for k, ref in enumerate(panels)
    ]
    for copy in metas:
        copy.start()
    load.wait()
    back.wait()

    @pl.loop(0, lists[4, 0])
    def _(k):
        p = lax.rem(lists[1, k], owned)
        e = lists[2, k]
        rows = block_rows(lists[3, k])
        for j, ref in enumerate(panels):

            @pl.when(e == j)
            def _():
                pltpu.make_async_copy(blocks.at[p], ref.at[rows], sems.at[2]).start()

    for copy in metas:
        copy.wait()

    @pl.loop(0, lists[4, 0])
    def _(k):
        pltpu.make_async_copy(blocks.at[0], panels[0].at[block_rows(0)], sems.at[2]).wait()


def split_blocks(density, dest, code, direct, groups):
    owned, _ = dest.shape
    panels = [panel(direct)] * groups[0] + [panel(POOL)] * (groups[1] - 1)
    return pl.pallas_call(
        functools.partial(split_kernel, direct, groups),
        out_shape=(*panels, jax.ShapeDtypeStruct((META, NBF), jnp.int32)),
        in_specs=[vmem_spec(), vmem_spec(), any_spec()],
        out_specs=(any_spec(),) * len(panels) + (smem_spec(),),
        scratch_shapes=[
            pltpu.VMEM((META, NBF), jnp.int32),
            pltpu.VMEM((META, NBF), jnp.int32),
            pltpu.VMEM((owned, NBF, NBF), jnp.bfloat16),
            pltpu.VMEM((len(panels), META, NBF), jnp.int32),
            pltpu.VMEM((len(panels), META, NBF), jnp.bfloat16),
            pltpu.SemaphoreType.DMA((3 + len(panels),)),
        ],
        name="split_blocks",
    )(dest.T, code.T, density)


def direct_kernel(copies, places, density, out, blocks, live, load_sem, out_sem):
    owned = blocks.shape[0]
    domains = out.shape[0]
    load = pltpu.make_async_copy(density, blocks, load_sem)
    load.start()
    load.wait()
    live[0] = 0

    @pl.loop(0, owned)
    def _(p):
        for t in range(copies):
            entry = places[0, t * owned + p] // LINE
            rows = block_rows(places[0, t * owned + p] - entry * LINE)

            @pl.when(entry < domains)
            def _():
                live[0] = live[0] + 1
                pltpu.make_async_copy(blocks.at[p], out.at[entry, rows], out_sem).start()

    @pl.loop(0, live[0])
    def _(k):
        pltpu.make_async_copy(blocks.at[0], out.at[0, block_rows(0)], out_sem).wait()


def direct_blocks(places, density, domains, direct, copies):
    return pl.pallas_call(
        functools.partial(direct_kernel, copies),
        out_shape=jax.ShapeDtypeStruct((domains, direct * NBF, NBF), jnp.bfloat16),
        in_specs=[smem_spec(), any_spec()],
        out_specs=any_spec(),
        scratch_shapes=[
            pltpu.VMEM(density.shape, jnp.bfloat16),
            pltpu.SMEM((1,), jnp.int32),
            pltpu.SemaphoreType.DMA,
            pltpu.SemaphoreType.DMA,
        ],
        cost_estimate=pl.CostEstimate(flops=1000, bytes_accessed=8 << 20, transcendentals=0),
        name="direct_blocks",
    )(places, density)


def scan_kernel(direct, heads, *refs):
    extras = refs[:-9]
    starts, places, marks, lines, codes_v, codes, live, line_sem, code_sem = refs[-9:]
    sources = heads.shape[0]
    loads = [pltpu.make_async_copy(heads, lines.at[pl.ds(0, sources)], line_sem.at[0])]
    for k, ref in enumerate(extras):
        loads.append(pltpu.make_async_copy(ref.at[meta_rows(ref), :], lines.at[sources + k], line_sem.at[1 + k]))
    for load in loads:
        load.start()
    for load in loads:
        load.wait()
    head = lax.broadcasted_iota(jnp.int32, lines.shape, 1) == 0
    codes_v[...] = jnp.sum(jnp.where(head, lines[...].astype(jnp.float32), 0.0), axis=1).astype(jnp.int32)
    load = pltpu.make_async_copy(codes_v, codes, code_sem)
    load.start()
    load.wait()
    live[0] = 0

    def note(entry, rank):
        c = codes[entry, rank]

        @pl.when(c >= 0)
        def _():
            k = live[0]
            places[k] = entry * LINE + rank
            marks[k] = c
            live[0] = k + 1

    starts[0] = 0

    @pl.loop(0, sources)
    def _(source):
        for rank in range(direct):
            note(source, rank)

    starts[1] = live[0]
    for k, ref in enumerate(extras):

        @pl.loop(0, ranks_of(ref))
        def _(rank):
            note(sources + k, rank)

        starts[2 + k] = live[0]


def scan(heads, extras, direct):
    sources = heads.shape[0]
    entries = sources + len(extras)
    slots = sources * direct + sum(ranks_of(ref) for ref in extras)
    return pl.pallas_call(
        functools.partial(scan_kernel, direct),
        out_shape=(
            jax.ShapeDtypeStruct((2 + len(extras),), jnp.int32),
            jax.ShapeDtypeStruct((slots,), jnp.int32),
            jax.ShapeDtypeStruct((slots,), jnp.int32),
        ),
        in_specs=[any_spec()] * (1 + len(extras)),
        out_specs=(smem_spec(),) * 3,
        scratch_shapes=[
            pltpu.VMEM((entries, META, NBF), jnp.bfloat16),
            pltpu.VMEM((entries, NBF), jnp.int32),
            pltpu.SMEM((entries, NBF), jnp.int32),
            pltpu.SMEM((1,), jnp.int32),
            pltpu.SemaphoreType.DMA((1 + len(extras),)),
            pltpu.SemaphoreType.DMA,
        ],
        cost_estimate=pl.CostEstimate(flops=1000, bytes_accessed=8 << 20, transcendentals=0),
        name="scan",
    )(heads, *extras)


def merge_kernel(direct, groups, *refs):
    rows_x, rows_z = groups
    panels = refs[:-9]
    starts, places, marks, raised, lines, ints, info, live, sems = refs[-9:]
    loads = [pltpu.make_async_copy(ref.at[meta_rows(ref), :], lines.at[k], sems.at[k]) for k, ref in enumerate(panels)]
    for load in loads:
        load.start()
    for load in loads:
        load.wait()
    ints[...] = lines[...].astype(jnp.float32).astype(jnp.int32)
    load = pltpu.make_async_copy(ints, info, sems.at[0])
    load.start()
    load.wait()
    me_x, me_z = lax.axis_index("gx"), lax.axis_index("gy")
    live[0] = 0
    raised[0] = 0
    starts[0] = 0

    def note(entry, rank, c):
        @pl.when(c >= 0)
        def _():
            k = live[0]
            places[k] = entry * LINE + rank
            marks[k] = c
            live[0] = k + 1

    @pl.loop(0, rows_x)
    def _(k):
        first = (k ^ me_x) * rows_z
        raised[0] = raised[0] | info[k, 3, 0] | info[rows_x + k, 3, 0]
        for rank in range(direct):
            note(first + me_z, rank, info[k, 1, rank])
            for h in range(rows_z - 1):
                note(first + (me_z ^ (h + 1)), rank, info[rows_x + k, 1, h * direct + rank])

    starts[1] = live[0]
    domains = rows_x * rows_z
    for k, ref in enumerate(panels):

        @pl.loop(0, ranks_of(ref))
        def _(rank):
            note(domains + k, rank, info[k, 0, rank])

        starts[2 + k] = live[0]


def merge(panels, direct, groups):
    slots = groups[0] * groups[1] * direct + sum(ranks_of(ref) for ref in panels)
    return pl.pallas_call(
        functools.partial(merge_kernel, direct, groups),
        out_shape=(
            jax.ShapeDtypeStruct((2 + len(panels),), jnp.int32),
            jax.ShapeDtypeStruct((slots,), jnp.int32),
            jax.ShapeDtypeStruct((slots,), jnp.int32),
            jax.ShapeDtypeStruct((1,), jnp.int32),
        ),
        in_specs=[any_spec()] * len(panels),
        out_specs=(smem_spec(),) * 4,
        scratch_shapes=[
            pltpu.VMEM((len(panels), META, NBF), jnp.bfloat16),
            pltpu.VMEM((len(panels), META, NBF), jnp.int32),
            pltpu.SMEM((len(panels), META, NBF), jnp.int32),
            pltpu.SMEM((1,), jnp.int32),
            pltpu.SemaphoreType.DMA((len(panels),)),
        ],
        cost_estimate=pl.CostEstimate(flops=1000, bytes_accessed=8 << 20, transcendentals=0),
        compiler_params=pltpu.CompilerParams(vmem_limit_bytes=60 << 20),
        name="merge",
    )(*panels)


def relay_kernel(direct, *refs):
    info, count, table, stage, lines, ints, cells, codes16, in_sem, sems = refs[-10:]
    hops = lines.shape[0]
    arrived = refs[:hops]
    outs = refs[hops:-11]
    places = refs[-11]
    ranks = ranks_of(outs[0])
    me = lax.axis_index("gx")
    loads = [
        pltpu.make_async_copy(ref.at[meta_rows(ref), :], lines.at[h], sems.at[h]) for h, ref in enumerate(arrived)
    ]
    for load in loads:
        load.start()
    last = sems.at[hops + len(outs)]
    cells[...] = jnp.full(cells.shape, -1, jnp.int32)
    fill = pltpu.make_async_copy(cells, table, last)
    fill.start()
    for k in range(len(outs)):
        count[k] = 0
    for load in loads:
        load.wait()
    ints[...] = lines[...].astype(jnp.float32).astype(jnp.int32)
    load = pltpu.make_async_copy(ints, info, sems.at[0])
    load.start()
    load.wait()
    fill.wait()

    def fetch(h, q):
        return pltpu.make_async_copy(arrived[h].at[block_rows(q)], stage.at[h * POOL + q], in_sem.at[h * POOL + q])

    for h in range(hops):

        @pl.loop(0, POOL)
        def _(q):
            places[h, q] = -1
            c = info[h, 0, q]

            @pl.when(c >= 0)
            def _():
                fetch(h, q).start()
                near = info[h, 1, q] ^ me
                slot = jnp.minimum(count[near], ranks - 1)
                count[near] = slot + 1
                places[h, q] = near * LINE + slot
                table[near, 0, slot] = c

    raised = functools.reduce(jnp.bitwise_or, [info[h, 3, 0] for h in range(hops)])

    @pl.loop(0, len(outs))
    def _(k):
        table[k, 3, 0] = raised
        for h in range(hops):
            for rank in range(direct):
                table[k, 1, h * direct + rank] = info[h, 2, (k ^ me) * direct + rank]

    back = pltpu.make_async_copy(table, cells, last)
    back.start()
    back.wait()
    codes16[...] = cells[...].astype(jnp.float32).astype(jnp.bfloat16)
    metas = [
        pltpu.make_async_copy(codes16.at[k], ref.at[meta_rows(ref), :], sems.at[hops + k])
        for k, ref in enumerate(outs)
    ]
    for copy in metas:
        copy.start()
    for h in range(hops):

        @pl.loop(0, POOL)
        def _(q):
            place = places[h, q]

            @pl.when(place >= 0)
            def _():
                fetch(h, q).wait()
                near = place // LINE
                rows = block_rows(place - near * LINE)
                for k, ref in enumerate(outs):

                    @pl.when(near == k)
                    def _():
                        pltpu.make_async_copy(stage.at[h * POOL + q], ref.at[rows], last).start()

    for copy in metas:
        copy.wait()
    for h in range(hops):

        @pl.loop(0, POOL)
        def _(q):
            @pl.when(places[h, q] >= 0)
            def _():
                pltpu.make_async_copy(stage.at[0], outs[0].at[block_rows(0)], last).wait()


def relay(arrived, near_count, ranks, direct):
    hops = len(arrived)
    return pl.pallas_call(
        functools.partial(relay_kernel, direct),
        out_shape=tuple([panel(ranks)] * near_count + [jax.ShapeDtypeStruct((hops, POOL), jnp.int32)]),
        in_specs=[any_spec()] * hops,
        out_specs=tuple([any_spec()] * near_count + [smem_spec()]),
        scratch_shapes=[
            pltpu.SMEM((hops, META, NBF), jnp.int32),
            pltpu.SMEM((near_count,), jnp.int32),
            pltpu.SMEM((near_count, META, NBF), jnp.int32),
            pltpu.VMEM((hops * POOL, NBF, NBF), jnp.bfloat16),
            pltpu.VMEM((hops, META, NBF), jnp.bfloat16),
            pltpu.VMEM((hops, META, NBF), jnp.int32),
            pltpu.VMEM((near_count, META, NBF), jnp.int32),
            pltpu.VMEM((near_count, META, NBF), jnp.bfloat16),
            pltpu.SemaphoreType.DMA((hops * POOL,)),
            pltpu.SemaphoreType.DMA((hops + near_count + 1,)),
        ],
        cost_estimate=pl.CostEstimate(flops=1000, bytes_accessed=4 << 20, transcendentals=0),
        compiler_params=pltpu.CompilerParams(vmem_limit_bytes=60 << 20),
        name="relay",
    )(*arrived)


def relay_back_kernel(places, *refs):
    stage, in_sem, out_sem = refs[-3:]
    hops = places.shape[0]
    arrived, outs = refs[: -3 - hops], refs[-3 - hops : -3]

    def fetch(ref, rows, h, q):
        return pltpu.make_async_copy(ref.at[rows], stage.at[h * POOL + q], in_sem.at[h * POOL + q])

    def give(h, q):
        return pltpu.make_async_copy(stage.at[h * POOL + q], outs[h].at[block_rows(q)], out_sem)

    for h in range(hops):

        @pl.loop(0, POOL)
        def _(q):
            place = places[h, q]

            @pl.when(place >= 0)
            def _():
                near = place // LINE
                rows = block_rows(place - near * LINE)
                for k, ref in enumerate(arrived):

                    @pl.when(near == k)
                    def _():
                        fetch(ref, rows, h, q).start()

    for h in range(hops):

        @pl.loop(0, POOL)
        def _(q):
            @pl.when(places[h, q] >= 0)
            def _():
                fetch(arrived[0], block_rows(0), h, q).wait()
                give(h, q).start()

    for h in range(hops):

        @pl.loop(0, POOL)
        def _(q):
            @pl.when(places[h, q] >= 0)
            def _():
                give(h, q).wait()


def relay_back(places, arrived):
    hops = places.shape[0]
    return pl.pallas_call(
        relay_back_kernel,
        out_shape=tuple([panel(POOL)] * hops),
        in_specs=[smem_spec()] + [any_spec()] * len(arrived),
        out_specs=tuple([any_spec()] * hops),
        scratch_shapes=[
            pltpu.VMEM((hops * POOL, NBF, NBF), jnp.bfloat16),
            pltpu.SemaphoreType.DMA((hops * POOL,)),
            pltpu.SemaphoreType.DMA,
        ],
        cost_estimate=pl.CostEstimate(flops=1000, bytes_accessed=4 << 20, transcendentals=0),
        compiler_params=pltpu.CompilerParams(vmem_limit_bytes=60 << 20),
        name="relay_back",
    )(places, *arrived)


def domain_kernel(extra_count, starts, places, marks, *refs):
    inbound, *extras = refs[: 1 + extra_count]
    basis, basis_t, base_in, w_in, w_hid1, w_hid1_t, w_hid2, w_hid2_t, w_last, weights = refs[
        1 + extra_count : 11 + extra_count
    ]
    reply, *extra_replies = refs[11 + extra_count : 12 + 2 * extra_count]
    (
        seen,
        stage,
        acc,
        dense,
        basis_v,
        basis_tv,
        rho,
        hid1,
        hid2,
        blocks,
        meta,
        w_row,
        w_out,
        in_sem,
        basis_sem,
        out_sem,
        meta_sem,
    ) = refs[12 + 2 * extra_count :]
    sources = inbound.shape[0]
    direct = ranks_of(inbound)
    points, order = basis.shape
    width = order // NBF
    pairs = width * width
    load_t = pltpu.make_async_copy(basis_t, basis_tv, basis_sem.at[0])
    load_n = pltpu.make_async_copy(basis, basis_v, basis_sem.at[1])
    live = starts[1 + extra_count]

    @pl.loop(0, starts[1])
    def _(k):
        entry = places[k] // LINE
        rows = block_rows(places[k] - entry * LINE)
        pltpu.make_async_copy(inbound.at[entry, rows], stage.at[k], in_sem.at[k]).start()

    for e, ref in enumerate(extras):

        @pl.loop(starts[1 + e], starts[2 + e])
        def _(k):
            rows = block_rows(places[k] - (sources + e) * LINE)
            pltpu.make_async_copy(ref.at[rows], stage.at[k], in_sem.at[k]).start()

    load_t.start()

    @pl.loop(0, pairs)
    def _(c):
        seen[c] = 0

    w_row[...] = jnp.broadcast_to(w_in[0:1, :], w_row.shape).T
    w_out[...] = jnp.broadcast_to(w_last[...], w_out.shape).T

    @pl.loop(0, live)
    def _(k):
        c = marks[k]
        pltpu.make_async_copy(inbound.at[0, block_rows(0)], stage.at[k], in_sem.at[k]).wait()
        value = stage[k].astype(jnp.float32)
        before = seen[c]
        seen[c] = 1

        @pl.when(before == 0)
        def _():
            acc[c] = value

        @pl.when(before != 0)
        def _():
            acc[c] = acc[c] + value

    load_n.start()

    @pl.loop(0, width)
    def _(a):
        rows = block_rows(a)
        for b in range(width):
            there = seen[a * width + b] != 0
            value = jnp.where(there, acc[a * width + b], 0.0)
            dense[rows, b * NBF : (b + 1) * NBF] = value.astype(jnp.bfloat16)

    load_t.wait()
    tile = 512

    @pl.loop(0, points // tile)
    def _(n):
        cols = pl.ds(pl.multiple_of(n * tile, tile), tile)
        part = basis_tv[:, cols]
        projected = jnp.dot(dense[...], part, preferred_element_type=jnp.float32)
        rho[:, cols] = jnp.sum(projected * part.astype(jnp.float32), axis=0, keepdims=True)

    h1 = jnp.tanh(base_in[...] + w_row[:, 0:1] * rho[...])
    hid1[...] = h1
    h2 = jnp.tanh(jnp.dot(w_hid1_t[...], h1, precision=HI, preferred_element_type=jnp.float32))
    hid2[...] = h2
    h3 = jnp.tanh(jnp.dot(w_hid2_t[...], h2, precision=HI, preferred_element_type=jnp.float32))
    logits = jnp.sum(w_out[:, 0:1] * h3, axis=0, keepdims=True)
    decay = jnp.exp(-jnp.abs(logits))
    energy_at = -(jnp.maximum(logits, 0.0) + jnp.log1p(decay))
    slope = -jnp.where(logits >= 0, 1.0, decay) / (1.0 + decay)
    g3 = (w_out[:, 0:1] * slope) * (1.0 - h3 * h3)
    h2 = hid2[...]
    g2 = jnp.dot(w_hid2[...], g3, precision=HI, preferred_element_type=jnp.float32) * (1.0 - h2 * h2)
    h1 = hid1[...]
    g1 = jnp.dot(w_hid1[...], g2, precision=HI, preferred_element_type=jnp.float32) * (1.0 - h1 * h1)
    deriv = jnp.sum(w_row[:, 0:1] * g1, axis=0, keepdims=True)
    rho[...] = weights[...] * deriv
    total = jnp.sum(weights[...] * energy_at, axis=1, keepdims=True)
    top = total.astype(jnp.bfloat16).astype(jnp.float32)
    rest = total - top
    middle = rest.astype(jnp.bfloat16).astype(jnp.float32)
    low = rest - middle
    lane = lax.broadcasted_iota(jnp.int32, (META, NBF), 1)
    line = jnp.where(lane == 0, top, jnp.where(lane == 1, middle, jnp.where(lane == 2, low, 0.0)))
    meta[...] = line.astype(jnp.bfloat16)

    @pl.loop(0, sources)
    def _(source):
        pltpu.make_async_copy(meta, reply.at[source, pl.ds(direct * NBF, META)], meta_sem).start()

    load_n.wait()

    @pl.loop(0, points // NBF)
    def _(n):
        rows = block_rows(n)
        line = jnp.broadcast_to(rho[:, rows], (NBF, NBF))
        column = line.T
        for b in range(width):
            cols = slice(b * NBF, (b + 1) * NBF)
            basis_v[rows, cols] = (column * basis_v[rows, cols].astype(jnp.float32)).astype(jnp.bfloat16)

    @pl.loop(0, width // 2)
    def _(n):
        cols = pl.ds(pl.multiple_of(n * 2 * NBF, 2 * NBF), 2 * NBF)
        result = jnp.dot(basis_tv[...], basis_v[:, cols], preferred_element_type=jnp.float32).astype(jnp.bfloat16)
        for a in range(width):
            for half in range(2):
                blocks[a * width + 2 * n + half] = result[a * NBF : (a + 1) * NBF, half * NBF : (half + 1) * NBF]

    def give(ref, rows, k):
        pltpu.make_async_copy(blocks.at[marks[k]], ref.at[rows], out_sem).start()

    for e, ref in enumerate(extra_replies):

        @pl.loop(starts[1 + e], starts[2 + e])
        def _(k):
            give(ref, block_rows(places[k] - (sources + e) * LINE), k)

    @pl.loop(0, starts[1])
    def _(k):
        entry = places[k] // LINE
        give(reply.at[entry], block_rows(places[k] - entry * LINE), k)

    @pl.loop(0, live)
    def _(k):
        pltpu.make_async_copy(blocks.at[0], reply.at[0, block_rows(0)], out_sem).wait()

    whole = reply.at[:, meta_rows(reply), :]
    pltpu.make_async_copy(whole, whole, meta_sem).wait()


def domain_build(lists, inbound, extras, basis, *fixed):
    sources = inbound.shape[0]
    direct = ranks_of(inbound)
    points, order = basis.shape
    hid = fixed[1].shape[0]
    pairs = (order // NBF) ** 2
    slots = lists[1].shape[0]
    arrays = [inbound] + list(extras)
    replies = [jax.ShapeDtypeStruct((sources, direct * NBF + META, NBF), jnp.bfloat16)]
    replies += [jax.ShapeDtypeStruct((ranks_of(ref) * NBF, NBF), jnp.bfloat16) for ref in extras]
    return pl.pallas_call(
        functools.partial(domain_kernel, len(extras)),
        out_shape=tuple(replies),
        in_specs=[smem_spec()] * 3 + [any_spec()] * (len(arrays) + 2) + [vmem_spec()] * 8,
        out_specs=(any_spec(),) * len(arrays),
        scratch_shapes=[
            pltpu.SMEM((pairs,), jnp.int32),
            pltpu.VMEM((slots, NBF, NBF), jnp.bfloat16),
            pltpu.VMEM((pairs, NBF, NBF), jnp.float32),
            pltpu.VMEM((order, order), jnp.bfloat16),
            pltpu.VMEM((points, order), jnp.bfloat16),
            pltpu.VMEM((order, points), jnp.bfloat16),
            pltpu.VMEM((1, points), jnp.float32),
            pltpu.VMEM((hid, points), jnp.float32),
            pltpu.VMEM((hid, points), jnp.float32),
            pltpu.VMEM((pairs, NBF, NBF), jnp.bfloat16),
            pltpu.VMEM((META, NBF), jnp.bfloat16),
            pltpu.VMEM((NBF, hid), jnp.float32),
            pltpu.VMEM((NBF, hid), jnp.float32),
            pltpu.SemaphoreType.DMA((slots,)),
            pltpu.SemaphoreType.DMA((2,)),
            pltpu.SemaphoreType.DMA,
            pltpu.SemaphoreType.DMA,
        ],
        compiler_params=pltpu.CompilerParams(vmem_limit_bytes=60 << 20),
        name="domain_build",
    )(*lists, *arrays, basis, *fixed)


def collect_kernel(scale, places, returned, *refs):
    extras = refs[:-10]
    fock, energy, listed, parts, result, meta, total_e, in_sem, out_sem, meta_sem = refs[-10:]
    owned, copies = parts.shape[:2]
    sources = returned.shape[0]
    meta_in = pltpu.make_async_copy(returned.at[:, meta_rows(returned), :], meta, meta_sem)
    meta_in.start()

    @pl.loop(0, owned)
    def _(p):
        for t in range(copies):
            entry = places[0, t * owned + p] // LINE
            rows = block_rows(places[0, t * owned + p] - entry * LINE)

            @pl.when(entry < sources)
            def _():
                pltpu.make_async_copy(returned.at[entry, rows], parts.at[p, t], in_sem.at[p]).start()

            if extras:

                @pl.when(entry >= sources)
                def _():
                    for k, ref in enumerate(extras):

                        @pl.when(entry == sources + k)
                        def _():
                            pltpu.make_async_copy(ref.at[rows], parts.at[p, t], in_sem.at[p]).start()

    meta_in.wait()
    lane = lax.broadcasted_iota(jnp.int32, meta.shape, 2)
    row = lax.broadcasted_iota(jnp.int32, meta.shape, 1)
    sent = jnp.where((lane < 3) & (row == 0), meta[...].astype(jnp.float32), 0.0)
    per_source = jnp.sum(jnp.sum(sent, axis=0), axis=0, keepdims=True)
    total_e[...] = jnp.sum(per_source, axis=1, keepdims=True) * scale
    send_e = pltpu.make_async_copy(total_e, energy, meta_sem)
    send_e.start()
    last = (sources + len(extras)) * LINE
    listed[owned] = 0

    @pl.loop(0, owned)
    def _(p):
        hits = [places[0, t * owned + p] >= last for t in range(copies)]

        @pl.when(functools.reduce(jnp.logical_or, hits))
        def _():
            k = listed[owned]
            listed[k] = p
            listed[owned] = k + 1

        total = jnp.zeros((NBF, NBF), jnp.float32)
        for t in range(copies):
            here = places[0, t * owned + p] < last

            @pl.when(here)
            def _():
                pltpu.make_async_copy(parts.at[p, t], parts.at[p, t], in_sem.at[p]).wait()

            total = total + jnp.where(here, parts[p, t].astype(jnp.float32), 0.0)
        result[p] = total
        pltpu.make_async_copy(result.at[p], fock.at[p], out_sem).start()

    pltpu.make_async_copy(result, fock, out_sem).wait()
    send_e.wait()


def collect_blocks(places, returned, extras, scale, owned, copies):
    sources = returned.shape[0]
    return pl.pallas_call(
        functools.partial(collect_kernel, scale),
        out_shape=(
            jax.ShapeDtypeStruct((owned, NBF, NBF), jnp.float32),
            jax.ShapeDtypeStruct((1, 1), jnp.float32),
            jax.ShapeDtypeStruct((owned + 1,), jnp.int32),
        ),
        in_specs=[smem_spec()] + [any_spec()] * (1 + len(extras)),
        out_specs=(any_spec(), any_spec(), smem_spec()),
        scratch_shapes=[
            pltpu.VMEM((owned, copies, NBF, NBF), jnp.bfloat16),
            pltpu.VMEM((owned, NBF, NBF), jnp.float32),
            pltpu.VMEM((sources, META, NBF), jnp.bfloat16),
            pltpu.VMEM((1, 1), jnp.float32),
            pltpu.SemaphoreType.DMA((owned,)),
            pltpu.SemaphoreType.DMA,
            pltpu.SemaphoreType.DMA,
        ],
        cost_estimate=pl.CostEstimate(flops=1000, bytes_accessed=8 << 20, transcendentals=0),
        compiler_params=pltpu.CompilerParams(vmem_limit_bytes=60 << 20),
        name="collect_blocks",
    )(places, returned, *extras)


def add_kernel(first, places, listed, partial, *refs):
    extras = refs[:-6]
    fock, parts, result, in_sem, fock_sem, out_sem = refs[-6:]
    owned, copies = parts.shape[:2]
    number = listed[owned]

    @pl.loop(0, number)
    def _(k):
        p = listed[k]
        pltpu.make_async_copy(partial.at[p], result.at[k], fock_sem.at[k]).start()
        for t in range(copies):
            entry = places[0, t * owned + p] // LINE
            rows = block_rows(places[0, t * owned + p] - entry * LINE)
            for e, ref in enumerate(extras):

                @pl.when(entry == first + e)
                def _():
                    pltpu.make_async_copy(ref.at[rows], parts.at[k, t], in_sem.at[k]).start()

    @pl.loop(0, number)
    def _(k):
        p = listed[k]
        pltpu.make_async_copy(partial.at[p], result.at[k], fock_sem.at[k]).wait()
        total = result[k]
        for t in range(copies):
            here = places[0, t * owned + p] >= first * LINE

            @pl.when(here)
            def _():
                pltpu.make_async_copy(parts.at[k, t], parts.at[k, t], in_sem.at[k]).wait()

            total = total + jnp.where(here, parts[k, t].astype(jnp.float32), 0.0)
        result[k] = total
        pltpu.make_async_copy(result.at[k], fock.at[p], out_sem).start()

    @pl.loop(0, number)
    def _(k):
        pltpu.make_async_copy(result.at[0], fock.at[0], out_sem).wait()


def add_blocks(places, listed, partial, extras, first, copies):
    owned = partial.shape[0]
    return pl.pallas_call(
        functools.partial(add_kernel, first),
        out_shape=jax.ShapeDtypeStruct(partial.shape, partial.dtype),
        in_specs=[smem_spec()] * 2 + [any_spec()] * (1 + len(extras)),
        out_specs=any_spec(),
        input_output_aliases={2: 0},
        scratch_shapes=[
            pltpu.VMEM((owned, copies, NBF, NBF), jnp.bfloat16),
            pltpu.VMEM((owned, NBF, NBF), jnp.float32),
            pltpu.SemaphoreType.DMA((owned,)),
            pltpu.SemaphoreType.DMA((owned,)),
            pltpu.SemaphoreType.DMA,
        ],
        compiler_params=pltpu.CompilerParams(vmem_limit_bytes=60 << 20),
        name="add_blocks",
    )(places, listed, partial, *extras)


def exchange(array):
    return lax.all_to_all(array, AXES, split_axis=0, concat_axis=0, tiled=True)


def swap(arrays, axis, first):
    size = lax.axis_size(axis)
    return [
        lax.ppermute(array, axis, [(i, i ^ (first + k)) for i in range(size)]) if first + k else array
        for k, array in enumerate(arrays)
    ]


def body(density, dest, code, basis, descriptors, weights, w_in, w_hid1, w_hid2, w_out):
    rows_x, rows_z = lax.axis_size("gx"), lax.axis_size("gy")
    domains = rows_x * rows_z
    owned = density.shape[0]
    copies = dest.shape[1]
    capacity = max(2, 2 * copies * owned // domains)
    points = basis.shape[0]
    scale = 1.0 / (math.sqrt(points) * domains)
    basis_t = basis.T
    base_in = jnp.dot(w_in[1:].T, descriptors, precision=HI)
    fixed = (
        basis, basis_t, base_in, w_in, w_hid1, w_hid1.T, w_hid2, w_hid2.T, w_out[None, :], weights[None, :]
    )

    def plain():
        heads, places = plan_blocks(dest, code, domains)
        lists = scan(exchange(heads), [], capacity)
        inbound = exchange(direct_blocks(places, density, domains, capacity, copies))
        (replies,) = domain_build(lists, inbound, [], *fixed)
        fock, energy, _ = collect_blocks(places, exchange(replies), [], scale, owned, copies)
        return fock, energy[0, 0]

    if capacity < 8 or copies * owned != NBF:
        return plain()
    direct = capacity // 2
    ranks = (rows_z - 1) * (capacity - direct)
    groups = (rows_x, rows_z)
    *panels, places = split_blocks(density, dest, code, direct, groups)
    lines_in = []
    for far in reversed(range(1, rows_z)):
        lines_in = swap([panels[rows_x + far - 1]], "gy", far) + lines_in
    near_in = swap(panels[:rows_x], "gx", 0)
    outgoing = direct_blocks(places, density, domains, direct, copies)
    inbound = exchange(outgoing)
    *relayed, relay_places = relay(lines_in, rows_x, ranks, direct)
    relayed_in = swap(relayed, "gx", 0)
    *lists, raised = merge(near_in + relayed_in, direct, groups)

    def split():
        replies, *others = domain_build(lists, inbound, near_in + relayed_in, *fixed)
        relayed_back = swap(others[rows_x:], "gx", 0)
        near_back = swap(others[:rows_x], "gx", 0)
        returned = exchange(replies)
        lines_back = swap(relay_back(relay_places, relayed_back), "gy", 1)
        fock, energy, listed = collect_blocks(places, returned, near_back, scale, owned, copies)
        return add_blocks(places, listed, fock, lines_back, domains + rows_x, copies), energy[0, 0]

    return lax.cond(raised[0] > 0, plain, split)


def solution(mesh):
    placed = (
        P(AXES, None, None),
        P(AXES, None),
        P(AXES, None),
        P(AXES, None),
        P(None, AXES),
        P(AXES),
        P(),
        P(),
        P(),
        P(),
    )
    return jax.shard_map(
        body,
        mesh=mesh,
        in_specs=placed,
        out_specs=(P(AXES, None, None), P()),
        check_vma=False,
    )
```
